32 devices in a mesh: tp: 4 (over y, core), dp: 4 (over z), sp: 2 (over x).
Axes of the slice: x: 2, y: 2, z: 4, core: 2. Of those that a mesh axis runs over, the one named last changes fastest.
Arguments:
- inputs: bfloat16 [4, 2, 1024, 768], P('dp', None, 'sp'), may hold values from -6 to 6
- lengths: int32 [4], P('dp'), may hold values from 128 to 1024, as said below
- gains: float32 [1, 2, 768], replicated, may hold values from 0.1 to 1.9
- w_qkv: bfloat16 [1, 3, 768, 768], P(None, None, None, 'tp'), may hold values from -0.21875 to 0.21875
- w_out: bfloat16 [1, 768, 768], P(None, 'tp'), may hold values from -1.75 to 1.75
- w_up: bfloat16 [1, 768, 3072], P(None, None, 'tp'), may hold values from -0.21875 to 0.21875
- w_down: bfloat16 [1, 3072, 768], P(None, 'tp'), may hold values from -0.109375 to 0.109375
- cotangent: bfloat16 [4, 2, 1024, 768], P('dp', None, 'sp'), may hold values from -6 to 6
Outputs:
- hidden_out: bfloat16 [4, 2, 1024, 768], P('dp', None, 'sp')
- input_grad: float32 [4, 2, 1024, 768], P('dp', None, 'sp')
- grad_qkv: float32 [1, 3, 768, 768], P(None, None, ('dp', 'sp'), 'tp')
- grad_out: float32 [1, 768, 768], P(None, 'tp', ('dp', 'sp'))
- grad_up: float32 [1, 768, 3072], P(None, ('dp', 'sp'), 'tp')
- grad_down: float32 [1, 3072, 768], P(None, 'tp', ('dp', 'sp'))
- grad_gains: float32 [1, 2, 768], P(None, None, ('dp', 'sp'))
The draws below stay inside these ranges and needn't reach their ends.
Inputs may be any that keep to these rules, and one draw needn't show every extreme that they name: `lengths`: each length is a multiple of 16; in every draw one row has length 1024 and another has 128.
All inputs are finite; a program needn't handle non-finite values.
Results may differ from the reference program's by a relative error of at most 0.012.
The reference program's roundings to bfloat16 on the way count: a program that leaves them out, or rounds other values in their place, can miss the bound.
Values may be sent and summed in bfloat16 or wider, within the bound.
A program may use at most 128 MiB of HBM per device.

```python
import jax
import jax.numpy as jnp
from jax import lax

D = 768
HEADS = 12
HEAD_DIM = 64
FF = 3072
BLOCK = 16
LAYERS = 1
SEQ = 1024
ROWS = 4


def draw_lengths(key, part):
    first_key, second_key = jax.random.split(key)
    least = SEQ // (8 * BLOCK)
    most = SEQ // BLOCK
    blocks = jax.random.randint(first_key, (ROWS,), least, most + 1)
    chosen = jax.random.randint(second_key, (), 0, ROWS)
    places = jnp.arange(ROWS)
    blocks = jnp.where(places == chosen, most, blocks)
    blocks = jnp.where(places == (chosen + 1) % ROWS, least, blocks)
    return (blocks * BLOCK).astype(jnp.int32)


def level_of(key, extent, shards, low, largest):
    factor_of = 1.0
    for axis_at, blocks in shards:
        heights = jax.random.uniform(jax.random.fold_in(jax.random.fold_in(key, 6), axis_at), (blocks,), jnp.float32, low / len(shards), largest / len(shards))
        factor_of = factor_of * jnp.repeat(jnp.exp(heights), extent[axis_at] // blocks).reshape((-1,) + (1,) * (len(extent) - 1 - axis_at))
    return factor_of


def normal_values(own_key, dims, deviation, bound, shards=(), held_as=jnp.bfloat16):
    drawn = deviation * jax.random.normal(own_key, dims, jnp.float32)
    if shards:
        drawn = drawn * level_of(own_key, dims, shards, -0.22, 0.18)
    return jnp.clip(drawn, -bound, bound).astype(held_as)


def setup_inputs(seed: int = 0) -> dict:
    streams_of = jax.random.split(jax.random.key(seed), 9)
    return {
        "inputs": normal_values(streams_of[0], (ROWS, 2, SEQ, D), 1.0, 6.0, ((0, 4), (2, 2))),
        "lengths": draw_lengths(jax.random.fold_in(streams_of[8], 71), 0),
        "gains": jnp.clip(1.0 + 0.18 * jax.random.normal(streams_of[2], (LAYERS, 2, D), jnp.float32), 0.1, 1.9),
        "w_qkv": normal_values(streams_of[3], (LAYERS, 3, D, HEADS * HEAD_DIM), D ** -0.5, 0.21875, ((3, 4),)),
        "w_out": normal_values(streams_of[4], (LAYERS, HEADS * HEAD_DIM, D), (D // 64) ** -0.5, 1.75, ((1, 4),)),
        "w_up": normal_values(streams_of[5], (LAYERS, D, FF), D ** -0.5, 0.21875, ((2, 4),)),
        "w_down": normal_values(streams_of[6], (LAYERS, FF, D), FF ** -0.5, 0.109375, ((1, 4),)),
        "cotangent": normal_values(streams_of[7], (ROWS, 2, SEQ, D), 1.0, 6.0, ((0, 4), (2, 2))),
    }


@jax.custom_vjp
def low(v):
    return lax.optimization_barrier(v.astype(jnp.bfloat16)).astype(jnp.float32)

@jax.custom_vjp
def low_back(v):
    return v

def low_keep(v):
    return (low(v), None)

def low_pass(kept, grad):
    return (grad,)

def back_keep(v):
    return (v, None)

def back_low(kept, grad):
    return (low(grad),)
low.defvjp(low_keep, low_pass)
low_back.defvjp(back_keep, back_low)
EPSILON = 1e-05
highest = lax.Precision.HIGHEST

def normalize(value, gain):
    centre = value - lax.optimization_barrier(jnp.mean(value, axis=-1, keepdims=True))
    spread = lax.optimization_barrier(jnp.mean(centre * centre, axis=-1, keepdims=True))
    return centre * lax.rsqrt(spread + EPSILON) * gain

def rotate(value, cosine, sine):
    half_dim = value.shape[-1] // 2
    first = value[..., :half_dim]
    second = value[..., half_dim:]
    return jnp.concatenate([first * cosine - second * sine, second * cosine + first * sine], axis=-1)

def visible(length):
    index = jnp.arange(2 * SEQ)
    clean = index >= SEQ
    place = index % SEQ
    block = place // BLOCK
    query_clean = clean[:, None]
    key_clean = clean[None, :]
    query_block = block[:, None]
    key_block = block[None, :]
    noisy_pair = jnp.logical_not(query_clean) & jnp.logical_not(key_clean) & (key_block == query_block)
    earlier_clean = jnp.logical_not(query_clean) & key_clean & (key_block < query_block)
    causal_clean = query_clean & key_clean & (key_block <= query_block)
    inside = place[None, :] < length
    return (noisy_pair | earlier_clean | causal_clean) & inside

def attend_head(parts):
    query, keys, values, length = parts
    scores = low_back(jnp.einsum('qd,kd->qk', query, keys, precision=highest))
    logits = jnp.where(visible(length), scores * HEAD_DIM ** (-0.5), -1e+30)
    weights = jax.nn.softmax(logits, axis=-1)
    return low_back(jnp.einsum('qk,kd->qd', low(weights), values, precision=highest))

def heads_first(value, rows):
    return jnp.moveaxis(value.reshape(rows, 2 * SEQ, HEADS, HEAD_DIM), 2, 1).reshape(rows * HEADS, 2 * SEQ, HEAD_DIM)

def forward(hidden, gains, w_qkv, w_out, w_up, w_down, lengths):
    half_dim = HEAD_DIM // 2
    freq = 10000.0 ** (-jnp.arange(half_dim).astype(jnp.float32) * 2.0 / HEAD_DIM)
    angle = jnp.arange(SEQ).astype(jnp.float32)[:, None] * freq[None, :]
    cosine = jnp.cos(angle)[:, None, :]
    sine = jnp.sin(angle)[:, None, :]
    rows = hidden.shape[0]
    shape = (rows, 2, SEQ, HEADS, HEAD_DIM)
    head_lengths = jnp.repeat(lengths, HEADS)
    checked = jax.checkpoint(attend_head)
    for layer in range(LAYERS):
        normed = low(normalize(hidden, gains[layer, 0]))
        projected = low_back(jnp.einsum('rcsd,tde->trcse', normed, w_qkv[layer], precision=highest))
        query = low(rotate(projected[0].reshape(shape), cosine, sine))
        keys = low(rotate(projected[1].reshape(shape), cosine, sine))
        values = low(projected[2].reshape(shape))
        mixed = lax.map(checked, (heads_first(query, rows), heads_first(keys, rows), heads_first(values, rows), head_lengths))
        mixed = jnp.moveaxis(mixed.reshape(rows, HEADS, 2 * SEQ, HEAD_DIM), 1, 2).reshape(rows, 2, SEQ, HEADS * HEAD_DIM)
        hidden = hidden + low_back(jnp.einsum('rcse,ed->rcsd', low(mixed), w_out[layer], precision=highest))
        normed = low(normalize(hidden, gains[layer, 1]))
        upward = low_back(jnp.einsum('rcsd,df->rcsf', normed, w_up[layer], precision=highest))
        active = low(jax.nn.gelu(upward, approximate=True))
        hidden = hidden + low_back(jnp.einsum('rcsf,fd->rcsd', active, w_down[layer], precision=highest))
    return hidden

def reference(inputs, lengths, gains, w_qkv, w_out, w_up, w_down, cotangent):

    def wrapped(hidden, gain_set, qkv_set, out_set, up_set, down_set):
        return forward(hidden, gain_set, qkv_set, out_set, up_set, down_set, lengths)
    result, pullback = jax.vjp(wrapped, inputs.astype(jnp.float32), gains.astype(jnp.float32), w_qkv.astype(jnp.float32), w_out.astype(jnp.float32), w_up.astype(jnp.float32), w_down.astype(jnp.float32))
    grads = pullback(cotangent.astype(jnp.float32))
    return (result.astype(jnp.bfloat16), grads[0], grads[2], grads[3], grads[4], grads[5], grads[1])
```

```python
from functools import partial
from types import SimpleNamespace

import jax
import jax.numpy as jnp
import numpy as np
from jax import lax
from jax.experimental import pallas as pl
from jax.experimental.pallas import tpu as pltpu
from jax.sharding import PartitionSpec as P

HEAD_DIM = 64
BLOCK = 16


EPSILON = 1e-05


def normalize(value, gain):
    centre = value - jnp.mean(value, axis=-1, keepdims=True)
    inverse = lax.rsqrt(jnp.mean(centre * centre, axis=-1, keepdims=True) + EPSILON)
    scaled = centre * inverse
    return (scaled * gain, scaled, inverse)


def norm_back(grad, scaled, inverse, gain):
    inner = grad * gain
    gain_grad = jnp.sum(grad * scaled, axis=(0, 1, 2))
    centred = inner - jnp.mean(inner, axis=-1, keepdims=True)
    result = inverse * (centred - scaled * jnp.mean(inner * scaled, axis=-1, keepdims=True))
    return (result, gain_grad)


def rotate(value, cosine, sine):
    half_dim = value.shape[-1] // 2
    first = value[..., :half_dim]
    second = value[..., half_dim:]
    return jnp.concatenate(
        [first * cosine - second * sine, second * cosine + first * sine], axis=-1
    )


def tables(offset, count):
    half_dim = HEAD_DIM // 2
    freq = 10000.0 ** (-jnp.arange(half_dim).astype(jnp.float32) * 2.0 / HEAD_DIM)
    angle = (offset + jnp.arange(count)).astype(jnp.float32)[:, None] * freq[None, :]
    return (jnp.cos(angle)[:, None, :], jnp.sin(angle)[:, None, :])


def visible(lengths, offset, seg, seq):
    places = offset + jnp.arange(seg)
    query_block = jnp.concatenate([places, places]) // BLOCK
    query_clean = jnp.arange(2 * seg) >= seg
    key_place = jnp.concatenate([places, jnp.arange(seq)])
    key_block = key_place // BLOCK
    key_clean = jnp.arange(seg + seq) >= seg
    query_noisy = jnp.logical_not(query_clean)[:, None]
    same_noisy = (
        query_noisy
        & jnp.logical_not(key_clean)[None, :]
        & (key_block[None, :] == query_block[:, None])
    )
    earlier_clean = query_noisy & key_clean[None, :] & (key_block[None, :] < query_block[:, None])
    causal_clean = (
        query_clean[:, None] & key_clean[None, :] & (key_block[None, :] <= query_block[:, None])
    )
    inside = key_place[None, :] < lengths[:, None]
    return (same_noisy | earlier_clean | causal_clean)[None] & inside[:, None, :]


def reduce_branch(branch):
    return lax.psum(branch, "tp")


def norm_in(stream, gain):
    normed, scaled, inverse = normalize(stream, gain)
    return (normed.astype(jnp.bfloat16), scaled, inverse)


def project(low_normed, weights, cosine, sine, heads):
    projected = jnp.einsum(
        "rcsd,tde->trcse", low_normed, weights, preferred_element_type=jnp.float32
    )
    shape = projected.shape[1:4] + (heads, HEAD_DIM)
    query = rotate(projected[0].reshape(shape), cosine, sine).astype(jnp.bfloat16)
    keys = rotate(projected[1].reshape(shape), cosine, sine).astype(jnp.bfloat16)
    values = projected[2].reshape(shape).astype(jnp.bfloat16)
    return (query, keys, values)


def collect(keys, values):
    rows = keys.shape[0]
    seg = keys.shape[2]
    return (
        lax.all_gather(keys[:, 1].reshape(rows, seg, -1), "sp", axis=1, tiled=True),
        lax.all_gather(values[:, 1].reshape(rows, seg, -1), "sp", axis=1, tiled=True),
    )


def join(query, keys, values, clean):
    rows = query.shape[0]
    seg = query.shape[2]
    heads = query.shape[3]
    full_keys = jnp.concatenate([keys[:, 0], clean[0].reshape(rows, -1, heads, HEAD_DIM)], axis=1)
    full_values = jnp.concatenate(
        [values[:, 0], clean[1].reshape(rows, -1, heads, HEAD_DIM)], axis=1
    )
    return (query.reshape(rows, 2 * seg, heads, HEAD_DIM), full_keys, full_values)


def attend(query, keys, values, mask):
    scores = jnp.einsum("rqhd,rkhd->rhqk", query, keys, preferred_element_type=jnp.float32)
    logits = jnp.where(mask[:, None], scores * HEAD_DIM ** (-0.5), -1e30)
    top = jnp.max(logits, axis=-1, keepdims=True)
    total = jnp.sum(jnp.exp(logits - top), axis=-1, keepdims=True)
    logsum = top + jnp.log(total)
    weights = jnp.exp(logits - logsum).astype(jnp.bfloat16)
    mixed = jnp.einsum("rhqk,rkhd->rqhd", weights, values, preferred_element_type=jnp.float32)
    return (mixed, logsum)


def attend_back(query, keys, values, mask, logsum, grad_mixed):
    scores = jnp.einsum("rqhd,rkhd->rhqk", query, keys, preferred_element_type=jnp.float32)
    logits = jnp.where(mask[:, None], scores * HEAD_DIM ** (-0.5), -1e30)
    weights = jnp.exp(logits - logsum)
    low_weights = weights.astype(jnp.bfloat16)
    grad_weights = jnp.einsum(
        "rqhd,rkhd->rhqk", grad_mixed, values, preferred_element_type=jnp.float32
    )
    inner = jnp.sum(grad_weights * weights, axis=-1, keepdims=True)
    grad_scores = (weights * (grad_weights - inner) * HEAD_DIM ** (-0.5)).astype(jnp.bfloat16)
    grad_query = jnp.einsum(
        "rhqk,rkhd->rqhd", grad_scores, keys, preferred_element_type=jnp.float32
    )
    grad_keys = jnp.einsum(
        "rhqk,rqhd->rkhd", grad_scores, query, preferred_element_type=jnp.float32
    )
    grad_values = jnp.einsum(
        "rhqk,rqhd->rkhd", low_weights, grad_mixed, preferred_element_type=jnp.float32
    )
    return (grad_query, grad_keys, grad_values)


def shards(inputs, lengths, gains, w_qkv, w_out, w_up, w_down, cotangent):
    layers = w_qkv.shape[0]
    rows = inputs.shape[0]
    seg = inputs.shape[2]
    heads = w_out.shape[1] // HEAD_DIM
    offset = lax.axis_index("sp") * seg
    seq = seg * lax.axis_size("sp")
    cosine, sine = tables(offset, seg)
    mask = visible(lengths, offset, seg, seq)
    hidden = inputs.astype(jnp.float32)
    kept_clean = []
    layer = 0
    low_attn, scaled_attn, inverse_attn = norm_in(hidden, gains[layer, 0])
    query, keys, values = project(low_attn, w_qkv[layer], cosine, sine, heads)
    clean = collect(keys, values)
    kept_attn = [(low_attn, scaled_attn, inverse_attn)]
    kept_clean.append(clean)
    joined = join(query, keys, values, clean)
    attended = attend(joined[0], joined[1], joined[2], mask)
    low_mixed = attended[0].reshape(rows, 2, seg, -1).astype(jnp.bfloat16)
    branch = jnp.einsum(
        "rcse,ed->rcsd", low_mixed, w_out[layer], preferred_element_type=jnp.float32
    )
    hidden = hidden + reduce_branch(branch)
    low_mlp, scaled_mlp, inverse_mlp = norm_in(hidden, gains[layer, 1])
    kept_mlp = [(low_mlp, scaled_mlp, inverse_mlp)]
    upward = jnp.einsum("rcsd,df->rcsf", low_mlp, w_up[layer], preferred_element_type=jnp.float32)
    active = jax.nn.gelu(upward, approximate=True).astype(jnp.bfloat16)
    branch = jnp.einsum("rcsf,fd->rcsd", active, w_down[layer], preferred_element_type=jnp.float32)
    hidden = hidden + reduce_branch(branch)
    hidden_out = hidden.astype(jnp.bfloat16)
    grad = cotangent.astype(jnp.float32)
    qkv_list = [None] * layers
    out_list = [None] * layers
    up_list = [None] * layers
    down_list = [None] * layers
    gain_list = [None] * layers
    for layer in reversed(range(layers)):
        low_normed, scaled, inverse = kept_mlp[layer]
        upward = jnp.einsum(
            "rcsd,df->rcsf", low_normed, w_up[layer], preferred_element_type=jnp.float32
        )
        active, gelu_back = jax.vjp(partial(jax.nn.gelu, approximate=True), upward)
        low_active = active.astype(jnp.bfloat16)
        grad_branch = grad.astype(jnp.bfloat16)
        down_list[layer] = jnp.einsum(
            "rcsf,rcsd->fd", low_active, grad_branch, preferred_element_type=jnp.float32
        )
        grad_active = jnp.einsum(
            "rcsd,fd->rcsf", grad_branch, w_down[layer], preferred_element_type=jnp.float32
        )
        grad_upward = gelu_back(grad_active)[0].astype(jnp.bfloat16)
        up_list[layer] = jnp.einsum(
            "rcsd,rcsf->df", low_normed, grad_upward, preferred_element_type=jnp.float32
        )
        partial_grad = jnp.einsum(
            "rcsf,df->rcsd", grad_upward, w_up[layer], preferred_element_type=jnp.float32
        )
        grad_normed = reduce_branch(partial_grad)
        through, second_gain = norm_back(grad_normed, scaled, inverse, gains[layer, 1])
        grad = grad + through
        low_attn, scaled_attn, inverse_attn = kept_attn[layer]
        query, keys, values = project(low_attn, w_qkv[layer], cosine, sine, heads)
        clean = collect(keys, values)
        joined = join(query, keys, values, clean)
        attended = attend(joined[0], joined[1], joined[2], mask)
        low_mixed = attended[0].reshape(rows, 2, seg, -1).astype(jnp.bfloat16)
        grad_branch = grad.astype(jnp.bfloat16)
        out_list[layer] = jnp.einsum(
            "rcse,rcsd->ed", low_mixed, grad_branch, preferred_element_type=jnp.float32
        )
        grad_mixed = jnp.einsum(
            "rcsd,ed->rcse", grad_branch, w_out[layer], preferred_element_type=jnp.float32
        )
        grad_mixed = grad_mixed.astype(jnp.bfloat16).reshape(rows, 2 * seg, heads, HEAD_DIM)
        grad_query, grad_keys, grad_values = attend_back(
            joined[0], joined[1], joined[2], mask, attended[1], grad_mixed
        )
        clean_grads = (
            lax.psum_scatter(
                grad_keys[:, seg:].reshape(rows, seq, -1), "sp", scatter_dimension=1, tiled=True
            ),
            lax.psum_scatter(
                grad_values[:, seg:].reshape(rows, seq, -1), "sp", scatter_dimension=1, tiled=True
            ),
        )
        local_shape = (rows, seg, heads, HEAD_DIM)
        key_grad = jnp.stack([grad_keys[:, :seg], clean_grads[0].reshape(local_shape)], axis=1)
        value_grad = jnp.stack([grad_values[:, :seg], clean_grads[1].reshape(local_shape)], axis=1)
        query_grad = grad_query.reshape(rows, 2, seg, heads, HEAD_DIM)
        stacked = jnp.stack(
            [rotate(query_grad, cosine, -sine), rotate(key_grad, cosine, -sine), value_grad]
        )
        stacked = stacked.astype(jnp.bfloat16).reshape(3, rows, 2, seg, -1)
        qkv_list[layer] = jnp.einsum(
            "rcsd,trcse->tde", low_attn, stacked, preferred_element_type=jnp.float32
        )
        partial_grad = jnp.einsum(
            "trcse,tde->rcsd", stacked, w_qkv[layer], preferred_element_type=jnp.float32
        )
        grad_normed = reduce_branch(partial_grad)
        through, first_gain = norm_back(grad_normed, scaled_attn, inverse_attn, gains[layer, 0])
        grad = grad + through
        gain_list[layer] = jnp.stack([first_gain, second_gain])
    qkv_all = jnp.stack(qkv_list)
    out_all = jnp.stack(out_list)
    up_all = jnp.stack(up_list)
    down_all = jnp.stack(down_list)
    gain_all = jnp.stack(gain_list)
    partly = (
        lax.psum_scatter(qkv_all, "dp", scatter_dimension=2, tiled=True),
        lax.psum_scatter(out_all, "dp", scatter_dimension=2, tiled=True),
        lax.psum_scatter(up_all, "dp", scatter_dimension=1, tiled=True),
        lax.psum_scatter(down_all, "dp", scatter_dimension=2, tiled=True),
        lax.psum_scatter(gain_all, "dp", scatter_dimension=2, tiled=True),
    )
    summed = (
        lax.psum_scatter(partly[0], "sp", scatter_dimension=2, tiled=True),
        lax.psum_scatter(partly[1], "sp", scatter_dimension=2, tiled=True),
        lax.psum_scatter(partly[2], "sp", scatter_dimension=1, tiled=True),
        lax.psum_scatter(partly[3], "sp", scatter_dimension=2, tiled=True),
        lax.psum_scatter(partly[4], "sp", scatter_dimension=2, tiled=True),
    )
    return (hidden_out, grad, summed[0], summed[1], summed[2], summed[3], summed[4])


CH = 256
RW = 64
NEG = -1e30
GC = 0.7978845608028654
GA = 0.044715
BF = jnp.bfloat16
F32 = jnp.float32
MESH = pl.DeviceIdType.MESH
VM = pl.BlockSpec(memory_space=pltpu.VMEM)
ANY = pl.BlockSpec(memory_space=pl.ANY)


def nn(a, b):
    return lax.dot_general(a, b, (((1,), (0,)), ((), ())), preferred_element_type=F32)


def nt(a, b):
    return lax.dot_general(a, b, (((1,), (1,)), ((), ())), preferred_element_type=F32)


def tn(a, b):
    return lax.dot_general(a, b, (((0,), (0,)), ((), ())), preferred_element_type=F32)


def each(count, body, start=0):
    def step(i, carry):
        body(i)
        return carry

    lax.fori_loop(start, count, step, 0)


class Copies:
    def __init__(self, sems, base, make):
        self.sems, self.base, self.make = sems, base, make

    def at(self, i):
        src, dst, dev = self.make(i)
        return pltpu.make_async_remote_copy(
            src_ref=src,
            dst_ref=dst,
            send_sem=self.sems[0].at[self.base + i],
            recv_sem=self.sems[1].at[self.base + i],
            device_id=dev,
            device_id_type=MESH,
        )

    def start(self, i):
        self.at(i).start()

    def arrived(self, i):
        self.at(i).wait_recv()

    def sent(self, i):
        self.at(i).wait_send()


SCRATCH = dict(
    x=((4, CH, 768), BF),
    cot=((1024, 768), BF),
    wqkv=((3, 768, 192), BF),
    wT=((576, 768), BF),
    wfull=((4, 192, 768), BF),
    wup=((768, 768), BF),
    wdown=((768, 768), BF),
    cs=((2, 2, 32, CH), F32),
    a=((1024, 768), BF),
    tT=((4, 768, CH), BF),
    tT2=((4, 768, CH), BF),
    qT=((4, 3, 64, CH), BF),
    kvT=((6, 2, 3, 64, CH), BF),
    kaug=((6, 3, CH, 128), BF),
    vn=((6, 3, CH, 64), BF),
    maskb=((4, 64, CH), BF),
    oacc=((4, 3, 64, CH), F32),
    stat=((12, 8, CH), F32),
    on=((4, CH, 192), BF),
    oT=((4, 192, CH), BF),
    orecv=((4, 3, RW, 192), BF),
    h1=((4, RW, 768), F32),
    b=((1024, 768), BF),
    m=((1024, 768), BF),
    gu=((1024, 768), BF),
    gy=((1024, 768), BF),
    g1=((4, RW, 768), F32),
    goT=((4, 3, 64, CH), BF),
    dkv=((6, 2, 3, 64, CH), F32),
    dkvs=((2, 2, 3, 64, CH), BF),
    dkvr=((2, 2, 3, 64, CH), BF),
    dq=((4, 3, 64, CH), F32),
    gT=((4, 9, 64, CH), BF),
    st2=((4, CH, 768), BF),
    st3=((4, CH, 768), BF),
    st4=((4, CH, 768), BF),
    ra2=((4, 128, 768), BF),
    ra3=((4, 128, 768), BF),
    ra4=((4, 128, 768), BF),
    rb2=((4, RW, 768), BF),
    rb3=((4, RW, 768), BF),
    rb4=((4, RW, 768), BF),
    pU=((4, 192, 768), BF),
    pW=((4, 192, 768), BF),
    pO=((4, 192, 192), BF),
    pQ=((4, 192, 576), BF),
    xU=((4, 96, 768), BF),
    xW=((4, 96, 768), BF),
    xO=((4, 96, 192), BF),
    xQ=((4, 96, 576), BF),
    zU=((3, 96, 768), BF),
    zW=((3, 96, 768), BF),
    zO=((3, 96, 192), BF),
    zQ=((3, 96, 576), BF),
    gsum=((4, 8, 768), F32),
    gx=((2, 8, 768), F32),
    gz=((3, 8, 768), F32),
)

TILES = (
    ((0, 0), (2, 1)),
    ((1, 0), (3, 1), (2, 3)),
    ((2, 2),),
    ((3, 2), (2, 3)),
)


def step_kernel(*refs):
    (x_h, len_r, gains, wqkv_h, wout_h, wup_h, wdown_h, cot_h, cs_h) = refs[:9]
    (hid, ig, outQ, outO, outU, outW, outG) = refs[9:16]
    s = SimpleNamespace(**dict(zip(SCRATCH, refs[16 : 16 + len(SCRATCH)])))
    lsem, ssem, rsem = refs[16 + len(SCRATCH) :]
    sems = (ssem, rsem)
    t = lax.axis_index("tp")
    z = lax.axis_index("dp")
    x = lax.axis_index("sp")
    c = lax.rem(t, 2)
    y = lax.div(t, 2)
    slot = 2 * c + y
    pslot = 2 * c + 1 - y
    partner = t + 1 - 2 * c
    ypeer = t + 2 - 4 * y
    diag = 3 - t
    tpdev = (None, partner, ypeer, diag)
    tpslot = (slot, 2 * (1 - c) + y, pslot, 2 * (1 - c) + 1 - y)

    barrier = pltpu.get_barrier_semaphore()
    for dev in (
        {"tp": partner},
        {"tp": ypeer},
        {"tp": diag},
        {"sp": 1 - x},
        {"dp": lax.rem(z + 1, 4)},
        {"dp": lax.rem(z + 2, 4)},
        {"dp": lax.rem(z + 3, 4)},
    ):
        pl.semaphore_signal(barrier, inc=1, device_id=dev, device_id_type=MESH)

    def own(ref, ch):
        return ref.at[pl.ds(ch * CH + slot * RW, RW), :]

    def half(ref, ch):
        return ref.at[pl.ds(ch * CH + c * 128, 128), :]

    def load(i, src, dst):
        return pltpu.make_async_copy(src, dst, lsem.at[i])

    loads = [load(i, x_h.at[i], s.x.at[i]) for i in range(4)]
    loads.append(load(4, wqkv_h, s.wqkv))
    loads.append(load(5, cs_h.at[pl.ds(2 * x, 2)], s.cs))
    loads.append(load(6, wout_h, s.wfull.at[slot]))
    loads.append(load(7, wup_h, s.wup))
    loads.append(load(8, wdown_h, s.wdown))
    loads.append(load(9, cot_h, s.cot))
    for i in (4, 2, 5, 3, 6, 0, 1, 7, 8, 9):
        loads[i].start()

    base = [0]

    def family(count, make):
        made = Copies(sems, base[0], make)
        made.count = count
        base[0] += count
        return made

    def spread(ref):
        return (
            family(4, lambda i: (own(ref, i), own(ref, i), {"tp": ypeer})),
            family(4, lambda i: (half(ref, i), half(ref, i), {"tp": partner})),
        )

    def gather(stage, ra, rb):
        return (
            family(
                4,
                lambda i: (
                    stage.at[i, pl.ds((1 - c) * 128, 128), :],
                    ra.at[i],
                    {"tp": partner},
                ),
            ),
            family(
                4, lambda i: (stage.at[i, pl.ds(pslot * RW, RW), :], rb.at[i], {"tp": ypeer})
            ),
        )

    def wmake(i):
        if i == 0:
            return (s.wfull.at[slot], s.wfull.at[slot], {"tp": ypeer})
        pair = pl.ds(2 * c, 2)
        return (s.wfull.at[pair], s.wfull.at[pair], {"tp": partner})

    wcopy = family(2, wmake)
    kvcopy = family(2, lambda i: (s.kvT.at[2 + i], s.kvT.at[4 + i], {"sp": 1 - x}))
    dkcopy = family(2, lambda i: (s.dkvs.at[i], s.dkvr.at[i], {"sp": 1 - x}))
    ocopy = [
        family(
            4,
            lambda i, r=r: (
                s.on.at[i, pl.ds(tpslot[r] * RW, RW), :],
                s.orecv.at[i, r - 1],
                {"tp": tpdev[r]},
            ),
        )
        for r in (1, 2, 3)
    ]
    ag1 = spread(s.b)
    ag2 = spread(hid)
    ag3 = spread(s.gy)
    ag4 = spread(ig)
    rs2 = gather(s.st2, s.ra2, s.rb2)
    rs3 = gather(s.st3, s.ra3, s.rb3)
    rs4 = gather(s.st4, s.ra4, s.rb4)
    all_waits = [wcopy, *ocopy, *ag1, *ag2, *ag3, *ag4, *rs2, *rs3, *rs4]

    class Piece:
        def __init__(self, stage, xr, zr):
            self.stage, self.xr, self.zr = stage, xr, zr
            self.xc = family(
                4,
                lambda i: (
                    self.stage.at[i, pl.ds(96 * (1 - x), 96), :],
                    self.xr.at[i],
                    {"sp": 1 - x},
                ),
            )
            self.zc = family(
                3,
                lambda i: (
                    self.stage.at[lax.rem(z + 1 + i, 4), pl.ds(96 * x, 96), :],
                    self.zr.at[i],
                    {"dp": lax.rem(z + 1 + i, 4)},
                ),
            )
            all_waits.extend([self.xc, self.zc])

        def compute(self, value):
            def one(i):
                zz = lax.rem(z + 1 + i, 4)
                self.stage[zz] = value(zz).astype(BF)
                self.xc.start(zz)

            each(4, one)

        def zstep(self):
            def one(i):
                zz = lax.rem(z + 1 + i, 4)
                self.xc.arrived(zz)
                rows = pl.ds(96 * x, 96)
                total = self.stage[zz, rows, :].astype(F32) + self.xr[zz].astype(F32)
                self.stage[zz, rows, :] = total.astype(BF)
                self.zc.start(i)

            each(3, one)

        def finish(self):
            self.xc.arrived(z)
            total = self.stage[z, pl.ds(96 * x, 96), :].astype(F32) + self.xr[z].astype(F32)
            for i in range(3):
                self.zc.arrived(i)
                total = total + self.zr[i].astype(F32)
            return total

    pieceU = Piece(s.pU, s.xU, s.zU)
    pieceW = Piece(s.pW, s.xW, s.zW)
    pieceO = Piece(s.pO, s.xO, s.zO)
    pieceQ = Piece(s.pQ, s.xQ, s.zQ)

    gtp = [
        family(1, lambda i, r=r: (s.gsum.at[t], s.gsum.at[t], {"tp": tpdev[r]}))
        for r in (1, 2, 3)
    ]
    gxc = family(1, lambda i: (s.gx.at[0], s.gx.at[1], {"sp": 1 - x}))
    gzc = family(
        3, lambda i: (s.gx.at[0], s.gz.at[i], {"dp": lax.rem(z + 1 + i, 4)})
    )
    all_waits.extend([*gtp, gxc, gzc])

    row = lax.broadcasted_iota(jnp.int32, (64, CH), 0)
    col = lax.broadcasted_iota(jnp.int32, (64, CH), 1)
    blk = lax.shift_right_logical(col, 4)
    ones = jnp.where(row == 16, 1.0, 0.0).astype(F32)
    for v, shown in enumerate((row == blk, row < blk, row <= blk, row < 64)):
        hidden = jnp.where(row < 16, jnp.where(shown, 0.0, NEG), ones)
        s.maskb[v] = hidden.astype(BF)
    length = len_r[0]
    hot = jnp.where(row == blk, 1.0, 0.0).astype(F32)

    def key_tail(start):
        outside = (row == 16) & (col + start >= length)
        return jnp.where(outside, NEG, hot)

    def keep_keys(kt, h, kT, vT, tail):
        s.kaug[kt, h] = jnp.transpose(jnp.concatenate([kT, tail], axis=0)).astype(BF)
        s.vn[kt, h] = jnp.transpose(vT).astype(BF)

    for ref in (s.dkv, s.dq):
        ref[...] = jnp.zeros_like(ref)
    s.gsum[...] = jnp.zeros_like(s.gsum)

    loads[4].wait()
    for i in range(3):
        s.wT[i * 192 : (i + 1) * 192, :] = jnp.transpose(s.wqkv[i])
    pl.semaphore_wait(barrier, 7)
    loads[6].wait()
    wcopy.start(0)
    loads[5].wait()

    gain1 = gains[0:1, :]
    gain2 = gains[1:2, :]

    def centred(v):
        centre = v - jnp.mean(v, axis=-1, keepdims=True)
        inverse = lax.rsqrt(jnp.mean(centre * centre, axis=-1, keepdims=True) + EPSILON)
        return centre * inverse, inverse

    def project_chunk(ch, j, clean):
        def rows(r):
            v = s.x[ch, pl.ds(r * RW, RW), :].astype(F32)
            s.a[pl.ds(ch * CH + r * RW, RW), :] = (centred(v)[0] * gain1).astype(BF)

        each(4, rows)
        proj = nt(s.wT[...], s.a[pl.ds(ch * CH, CH), :])
        cos = s.cs[j, 0]
        sin = s.cs[j, 1]
        tail = key_tail(x * (2 * CH) + j * CH)
        for h in range(3):
            turned = []
            for i in range(2):
                first = proj[i * 192 + h * 64 : i * 192 + h * 64 + 32]
                second = proj[i * 192 + h * 64 + 32 : i * 192 + h * 64 + 64]
                turned.append(
                    jnp.concatenate(
                        [first * cos - second * sin, second * cos + first * sin], axis=0
                    )
                )
            vT = proj[384 + h * 64 : 384 + h * 64 + 64]
            s.qT[ch, h] = (turned[0] * 0.125).astype(BF)
            s.kvT[ch, 0, h] = turned[1].astype(BF)
            s.kvT[ch, 1, h] = vT.astype(BF)
            keep_keys(ch, h, turned[1], vT, tail)

    def clean_chunk(j):
        for i in range(2):
            @pl.when(j == i)
            def _():
                loads[2 + i].wait()

        project_chunk(2 + j, j, True)

        @pl.when(x == 0)
        def _():
            kvcopy.start(j)

    each(2, clean_chunk)

    def noisy_chunk(j):
        for i in range(2):
            @pl.when(j == i)
            def _():
                loads[i].wait()

        project_chunk(j, j, False)

    each(2, noisy_chunk)

    def scores(ch, h, kt, v):
        query = jnp.concatenate([s.qT[ch, h], s.maskb[v]], axis=0)
        return nn(s.kaug[kt, h], query)

    for ch in range(4):
        def own_keys(h, ch=ch):
            parts = [scores(ch, h, kt, v) for kt, v in TILES[ch]]
            top = jnp.max(parts[0], axis=0, keepdims=True)
            for p in parts[1:]:
                top = jnp.maximum(top, jnp.max(p, axis=0, keepdims=True))
            total = jnp.zeros_like(top)
            mixed = jnp.zeros((64, CH), F32)
            for p, (kt, v) in zip(parts, TILES[ch]):
                e = jnp.exp(p - top)
                total = total + jnp.sum(e, axis=0, keepdims=True)
                mixed = mixed + nn(s.kvT[kt, 1, h], e.astype(BF))
            s.oacc[ch, h] = mixed
            s.stat[ch * 3 + h, 0:1, :] = top
            s.stat[ch * 3 + h, 1:2, :] = total

        each(3, own_keys)

    wcopy.arrived(0)
    wcopy.start(1)

    def old_keys(i):
        j = lax.div(i, 12)
        ch = lax.div(lax.rem(i, 12), 3)
        h = lax.rem(i, 3)
        p = scores(ch, h, 4 + j, 3)
        before = s.stat[ch * 3 + h, 0:1, :]
        top = jnp.maximum(before, jnp.max(p, axis=0, keepdims=True))
        e = jnp.exp(p - top)
        scale = jnp.exp(before - top)
        s.stat[ch * 3 + h, 0:1, :] = top
        s.stat[ch * 3 + h, 1:2, :] = s.stat[ch * 3 + h, 1:2, :] * scale + jnp.sum(
            e, axis=0, keepdims=True
        )
        s.oacc[ch, h] = s.oacc[ch, h] * scale + nn(s.kvT[4 + j, 1, h], e.astype(BF))

    @pl.when(x == 1)
    def _():
        def tile(j):
            kvcopy.arrived(j)
            tail = key_tail(j * CH)

            def head(h):
                keep_keys(
                    4 + j, h, s.kvT[4 + j, 0, h].astype(F32), s.kvT[4 + j, 1, h].astype(F32), tail
                )

            each(3, head)
            each(12 * j + 12, old_keys, 12 * j)

        each(2, tile)

    def close(ch):
        for h in range(3):
            at = ch * 3 + h
            total = s.stat[at, 1:2, :]
            out = s.oacc[ch, h] / total
            s.oacc[ch, h] = out
            s.stat[at, 2:3, :] = s.stat[at, 0:1, :] + jnp.log(total)
            s.oT[ch, h * 64 : h * 64 + 64, :] = out.astype(BF)
        whole = jnp.concatenate([s.oacc[ch, h] for h in range(3)], axis=0)
        s.on[ch] = jnp.transpose(whole).astype(BF)
        for copy in ocopy:
            copy.start(ch)

    each(4, close)
    wcopy.arrived(1)

    def out_rows(ch):
        total = s.x[ch, pl.ds(slot * RW, RW), :].astype(F32)
        total = total + nn(s.on[ch, pl.ds(slot * RW, RW), :], s.wfull[slot])
        for r in (1, 2, 3):
            ocopy[r - 1].arrived(ch)
            total = total + nn(s.orecv[ch, r - 1], s.wfull[tpslot[r]])
        s.h1[ch] = total
        own(s.b, ch)[...] = (centred(total)[0] * gain2).astype(BF)
        ag1[0].start(ch)

    each(4, out_rows)
    for i in (7, 8, 9):
        loads[i].wait()

    def add_pair(rs, stage, ra, ch):
        rs[0].arrived(ch)
        rows = pl.ds(pslot * RW, RW)
        total = stage[ch, rows, :].astype(F32) + ra[ch, pl.ds((1 - y) * RW, RW), :].astype(F32)
        stage[ch, rows, :] = total.astype(BF)
        rs[1].start(ch)

    def add_last(rs, stage, ra, rb, ch):
        rs[1].arrived(ch)
        rows = pl.ds(slot * RW, RW)
        total = stage[ch, rows, :].astype(F32) + ra[ch, pl.ds(y * RW, RW), :].astype(F32)
        return total + rb[ch].astype(F32)

    def relay(ag, ch):
        ag[0].arrived(ch)
        ag[1].start(ch)

    def norm_back(grad, stream, gain, at):
        scaled, inverse = centred(stream)
        inner = grad * gain
        s.gsum[t, at : at + 1, :] += jnp.sum(grad * scaled, axis=0, keepdims=True)
        inner_mean = jnp.mean(inner, axis=-1, keepdims=True)
        mixed_mean = jnp.mean(inner * scaled, axis=-1, keepdims=True)
        return inverse * (inner - inner_mean - scaled * mixed_mean)

    def second_back(ch):
        grad = add_last(rs3, s.st3, s.ra3, s.rb3, ch)
        through = norm_back(grad, s.h1[ch], gain2, 1)
        cot = s.cot[pl.ds(ch * CH + slot * RW, RW), :].astype(F32)
        g1 = cot + through
        s.g1[ch] = g1
        own(s.gy, ch)[...] = g1.astype(BF)
        ag3[0].start(ch)

    def feed(ch):
        rows = pl.ds(ch * CH, CH)
        ag1[1].arrived(ch)
        low_b = s.b[rows, :]
        low_g = s.cot[rows, :]
        for n in range(3):
            cols = slice(n * CH, (n + 1) * CH)
            u = nn(low_b, s.wup[:, cols])
            gm = nt(low_g, s.wdown[cols, :])
            square = u * u
            hp = 0.5 + 0.5 * jnp.tanh(u * (GC + GC * GA * square))
            act = u * hp
            slope = hp + (act - act * hp) * (2.0 * GC + 6.0 * GC * GA * square)
            s.m[rows, cols] = act.astype(BF)
            s.gu[rows, cols] = (slope * gm).astype(BF)

        @pl.when(ch < 3)
        def _():
            relay(ag1, ch + 1)

        s.st3[ch] = nt(s.gu[rows, :], s.wup[...]).astype(BF)
        rs3[0].start(ch)

        @pl.when(ch >= 1)
        def _():
            add_pair(rs3, s.st3, s.ra3, ch - 1)

        @pl.when(ch >= 2)
        def _():
            second_back(ch - 2)

    relay(ag1, 0)
    each(4, feed)
    add_pair(rs3, s.st3, s.ra3, 3)
    second_back(2)
    relay(ag3, 0)

    def transposed(dst, src):
        def one(ch):
            dst[ch] = jnp.transpose(src[pl.ds(ch * CH, CH), :])

        each(4, one)

    def rows_by(lhs, rhs):
        def value(zz):
            total = nn(lhs[0, pl.ds(192 * zz, 192), :], rhs[0:CH, :])
            for ch in range(1, 4):
                total = total + nn(lhs[ch, pl.ds(192 * zz, 192), :], rhs[ch * CH : ch * CH + CH, :])
            return total

        return value

    transposed(s.tT, s.b)
    pieceU.compute(rows_by(s.tT, s.gu))
    second_back(3)
    relay(ag3, 1)
    relay(ag3, 2)

    def down(ch):
        s.st2[ch] = nn(s.m[pl.ds(ch * CH, CH), :], s.wdown[...]).astype(BF)
        rs2[0].start(ch)

    each(4, down)
    relay(ag3, 3)
    each(4, lambda ch: add_pair(rs2, s.st2, s.ra2, ch))
    transposed(s.tT, s.cot)
    pieceW.compute(rows_by(s.tT, s.m))

    def grad_mixed(ch):
        ag3[1].arrived(ch)
        goT = nt(s.wfull[slot], s.gy[pl.ds(ch * CH, CH), :])
        for h in range(3):
            low = goT[h * 64 : h * 64 + 64].astype(BF)
            s.goT[ch, h] = low
            s.stat[ch * 3 + h, 3:4, :] = jnp.sum(
                low.astype(F32) * s.oacc[ch, h], axis=0, keepdims=True
            )

    each(4, grad_mixed)

    def back_tile(ch, h, kt, v):
        at = ch * 3 + h
        query = s.qT[ch, h]
        grad = s.goT[ch, h]
        weights = jnp.exp(scores(ch, h, kt, v) - s.stat[at, 2:3, :])
        gp = nn(s.vn[kt, h], grad)
        gs = (weights * (gp - s.stat[at, 3:4, :])).astype(BF)
        s.dkv[kt, 1, h] += nt(grad, weights.astype(BF))
        s.dkv[kt, 0, h] += nt(query, gs)
        s.dq[ch, h] += nn(s.kvT[kt, 0, h], gs)

    @pl.when(x == 1)
    def _():
        def tile(j):
            def one(i):
                back_tile(lax.div(i, 3), lax.rem(i, 3), 4 + j, 3)

            each(12, one)
            s.dkvs[j] = s.dkv[4 + j].astype(BF)
            dkcopy.start(j)

        each(2, tile)

    pieceU.zstep()

    def hidden_rows(ch):
        total = s.h1[ch] + add_last(rs2, s.st2, s.ra2, s.rb2, ch)
        own(hid, ch)[...] = total.astype(BF)
        ag2[0].start(ch)

    each(4, hidden_rows)

    for ch in range(4):
        def own_back(h, ch=ch):
            for kt, v in TILES[ch]:
                back_tile(ch, h, kt, v)

        each(3, own_back)

    pieceW.zstep()
    each(4, lambda ch: relay(ag2, ch))
    transposed(s.tT, s.gy)

    def out_piece(zz):
        total = nt(s.tT[0, pl.ds(192 * zz, 192), :], s.oT[0])
        for ch in range(1, 4):
            total = total + nt(s.tT[ch, pl.ds(192 * zz, 192), :], s.oT[ch])
        return total

    pieceO.compute(out_piece)

    def turn_back(u, cos, sin):
        first = u[:32]
        second = u[32:]
        return jnp.concatenate([first * cos + second * sin, second * cos - first * sin], axis=0)

    def grad_rows(ch):
        j = lax.rem(ch, 2)
        cos = s.cs[j, 0]
        sin = s.cs[j, 1]
        for h in range(3):
            s.gT[ch, h] = turn_back(s.dq[ch, h] * 0.125, cos, sin).astype(BF)
            s.gT[ch, 3 + h] = turn_back(s.dkv[ch, 0, h], cos, sin).astype(BF)
            s.gT[ch, 6 + h] = s.dkv[ch, 1, h].astype(BF)
        s.st4[ch] = tn(s.gT[ch].reshape(576, CH), s.wT[...]).astype(BF)
        rs4[0].start(ch)

    each(2, grad_rows)
    each(2, lambda ch: add_pair(rs4, s.st4, s.ra4, ch))

    @pl.when(x == 0)
    def _():
        def add_old(j):
            dkcopy.arrived(j)
            s.dkv[2 + j] += s.dkvr[j].astype(F32)

        each(2, add_old)

    each(4, grad_rows, 2)
    transposed(s.tT2, s.a)
    each(4, lambda ch: add_pair(rs4, s.st4, s.ra4, ch), 2)

    def qkv_piece(zz):
        total = nt(s.tT2[0, pl.ds(192 * zz, 192), :], s.gT[0].reshape(576, CH))
        for ch in range(1, 4):
            total = total + nt(
                s.tT2[ch, pl.ds(192 * zz, 192), :], s.gT[ch].reshape(576, CH)
            )
        return total

    pieceQ.compute(qkv_piece)

    def input_rows(ch):
        grad = add_last(rs4, s.st4, s.ra4, s.rb4, ch)
        stream = s.x[ch, pl.ds(slot * RW, RW), :].astype(F32)
        total = s.g1[ch] + norm_back(grad, stream, gain1, 0)
        own(ig, ch)[...] = total.astype(BF)
        ag4[0].start(ch)

    each(4, input_rows)

    for copy in gtp:
        copy.start(0)
    pieceO.zstep()
    pieceQ.zstep()
    each(4, lambda ch: relay(ag4, ch))
    for copy in gtp:
        copy.arrived(0)
    s.gx[0] = s.gsum[0] + s.gsum[1] + s.gsum[2] + s.gsum[3]
    gxc.start(0)
    outU[...] = pieceU.finish()
    outW[...] = jnp.transpose(pieceW.finish())
    gxc.arrived(0)
    gxc.sent(0)
    s.gx[0] = s.gx[0] + s.gx[1]
    for i in range(3):
        gzc.start(i)
    outO[...] = jnp.transpose(pieceO.finish())
    outQ[...] = pieceQ.finish()
    total = s.gx[0]
    for i in range(3):
        gzc.arrived(i)
        total = total + s.gz[i]
    for k in range(8):
        @pl.when(z * 2 + x == k)
        def _(k=k):
            outG[...] = total[0:2, 96 * k : 96 * k + 96]

    for ag in (ag2, ag4):
        each(4, lambda ch, ag=ag: ag[1].arrived(ch))
    for fam in all_waits:
        if fam is gxc:
            continue
        for i in range(fam.count):
            fam.sent(i)

    @pl.when(x == 0)
    def _():
        for i in range(2):
            kvcopy.sent(i)

    @pl.when(x == 1)
    def _():
        for i in range(2):
            dkcopy.sent(i)


def rope_table(seq):
    half_dim = HEAD_DIM // 2
    freq = 10000.0 ** (-np.arange(half_dim) * 2.0 / HEAD_DIM)
    angle = freq[:, None] * np.arange(seq)[None, :]
    both = np.stack([np.cos(angle), np.sin(angle)])
    return np.moveaxis(both.reshape(2, half_dim, seq // CH, CH), 2, 0).astype(np.float32)


def fast(inputs, lengths, gains, w_qkv, w_out, w_up, w_down, cotangent):
    seg = inputs.shape[2]
    shape = jax.ShapeDtypeStruct
    hid, ig, gq, go, gu, gd, gg = pl.pallas_call(
        step_kernel,
        out_shape=(
            shape((1024, 768), BF),
            shape((1024, 768), BF),
            shape((96, 576), F32),
            shape((192, 96), F32),
            shape((96, 768), F32),
            shape((768, 96), F32),
            shape((2, 96), F32),
        ),
        in_specs=[ANY, pl.BlockSpec(memory_space=pltpu.SMEM), VM, ANY, ANY, ANY, ANY, ANY, ANY],
        out_specs=[VM] * 7,
        scratch_shapes=[pltpu.VMEM(dims, kind) for dims, kind in SCRATCH.values()]
        + [
            pltpu.SemaphoreType.DMA((10,)),
            pltpu.SemaphoreType.DMA((140,)),
            pltpu.SemaphoreType.DMA((140,)),
        ],
        compiler_params=pltpu.CompilerParams(
            collective_id=0, has_side_effects=True, vmem_limit_bytes=64 * 1024 * 1024 - 65536
        ),
        name="step",
    )(
        inputs.reshape(4, CH, 768),
        lengths,
        gains[0],
        w_qkv[0],
        w_out[0],
        w_up[0],
        w_down[0],
        cotangent.reshape(1024, 768),
        jnp.asarray(rope_table(seg * lax.axis_size("sp"))),
    )
    return (
        hid.reshape(inputs.shape),
        ig.reshape(inputs.shape).astype(F32),
        jnp.moveaxis(gq.reshape(1, 96, 3, 192), 2, 1),
        go[None],
        gu[None],
        gd[None],
        gg[None],
    )


def pick(*args):
    inputs, w_out = args[0], args[4]
    plain = (1, 2, 512, 768)
    sizes = (lax.axis_size("tp"), lax.axis_size("dp"), lax.axis_size("sp"))
    if inputs.shape == plain and w_out.shape[1:] == (192, 768) and sizes == (4, 4, 2):
        return fast(*args)
    return shards(*args)


def solution(mesh):
    in_specs = (
        P("dp", None, "sp", None),
        P("dp"),
        P(),
        P(None, None, None, "tp"),
        P(None, "tp", None),
        P(None, None, "tp"),
        P(None, "tp", None),
        P("dp", None, "sp", None),
    )
    out_specs = (
        P("dp", None, "sp", None),
        P("dp", None, "sp", None),
        P(None, None, ("dp", "sp"), "tp"),
        P(None, "tp", ("dp", "sp")),
        P(None, ("dp", "sp"), "tp"),
        P(None, "tp", ("dp", "sp")),
        P(None, None, ("dp", "sp")),
    )
    return jax.shard_map(pick, mesh=mesh, in_specs=in_specs, out_specs=out_specs, check_vma=False)
```

```python
from functools import partial
from types import SimpleNamespace

import jax
import jax.numpy as jnp
import numpy as np
from jax import lax
from jax.experimental import pallas as pl
from jax.experimental.pallas import tpu as pltpu
from jax.sharding import PartitionSpec as P

HEAD_DIM = 64
BLOCK = 16


EPSILON = 1e-05


def normalize(value, gain):
    centre = value - jnp.mean(value, axis=-1, keepdims=True)
    inverse = lax.rsqrt(jnp.mean(centre * centre, axis=-1, keepdims=True) + EPSILON)
    scaled = centre * inverse
    return (scaled * gain, scaled, inverse)


def norm_back(grad, scaled, inverse, gain):
    inner = grad * gain
    gain_grad = jnp.sum(grad * scaled, axis=(0, 1, 2))
    centred = inner - jnp.mean(inner, axis=-1, keepdims=True)
    result = inverse * (centred - scaled * jnp.mean(inner * scaled, axis=-1, keepdims=True))
    return (result, gain_grad)


def rotate(value, cosine, sine):
    half_dim = value.shape[-1] // 2
    first = value[..., :half_dim]
    second = value[..., half_dim:]
    return jnp.concatenate(
        [first * cosine - second * sine, second * cosine + first * sine], axis=-1
    )


def tables(offset, count):
    half_dim = HEAD_DIM // 2
    freq = 10000.0 ** (-jnp.arange(half_dim).astype(jnp.float32) * 2.0 / HEAD_DIM)
    angle = (offset + jnp.arange(count)).astype(jnp.float32)[:, None] * freq[None, :]
    return (jnp.cos(angle)[:, None, :], jnp.sin(angle)[:, None, :])


def visible(lengths, offset, seg, seq):
    places = offset + jnp.arange(seg)
    query_block = jnp.concatenate([places, places]) // BLOCK
    query_clean = jnp.arange(2 * seg) >= seg
    key_place = jnp.concatenate([places, jnp.arange(seq)])
    key_block = key_place // BLOCK
    key_clean = jnp.arange(seg + seq) >= seg
    query_noisy = jnp.logical_not(query_clean)[:, None]
    same_noisy = (
        query_noisy
        & jnp.logical_not(key_clean)[None, :]
        & (key_block[None, :] == query_block[:, None])
    )
    earlier_clean = query_noisy & key_clean[None, :] & (key_block[None, :] < query_block[:, None])
    causal_clean = (
        query_clean[:, None] & key_clean[None, :] & (key_block[None, :] <= query_block[:, None])
    )
    inside = key_place[None, :] < lengths[:, None]
    return (same_noisy | earlier_clean | causal_clean)[None] & inside[:, None, :]


def reduce_branch(branch):
    return lax.psum(branch, "tp")


def norm_in(stream, gain):
    normed, scaled, inverse = normalize(stream, gain)
    return (normed.astype(jnp.bfloat16), scaled, inverse)


def project(low_normed, weights, cosine, sine, heads):
    projected = jnp.einsum(
        "rcsd,tde->trcse", low_normed, weights, preferred_element_type=jnp.float32
    )
    shape = projected.shape[1:4] + (heads, HEAD_DIM)
    query = rotate(projected[0].reshape(shape), cosine, sine).astype(jnp.bfloat16)
    keys = rotate(projected[1].reshape(shape), cosine, sine).astype(jnp.bfloat16)
    values = projected[2].reshape(shape).astype(jnp.bfloat16)
    return (query, keys, values)


def collect(keys, values):
    rows = keys.shape[0]
    seg = keys.shape[2]
    return (
        lax.all_gather(keys[:, 1].reshape(rows, seg, -1), "sp", axis=1, tiled=True),
        lax.all_gather(values[:, 1].reshape(rows, seg, -1), "sp", axis=1, tiled=True),
    )


def join(query, keys, values, clean):
    rows = query.shape[0]
    seg = query.shape[2]
    heads = query.shape[3]
    full_keys = jnp.concatenate([keys[:, 0], clean[0].reshape(rows, -1, heads, HEAD_DIM)], axis=1)
    full_values = jnp.concatenate(
        [values[:, 0], clean[1].reshape(rows, -1, heads, HEAD_DIM)], axis=1
    )
    return (query.reshape(rows, 2 * seg, heads, HEAD_DIM), full_keys, full_values)


def attend(query, keys, values, mask):
    scores = jnp.einsum("rqhd,rkhd->rhqk", query, keys, preferred_element_type=jnp.float32)
    logits = jnp.where(mask[:, None], scores * HEAD_DIM ** (-0.5), -1e30)
    top = jnp.max(logits, axis=-1, keepdims=True)
    total = jnp.sum(jnp.exp(logits - top), axis=-1, keepdims=True)
    logsum = top + jnp.log(total)
    weights = jnp.exp(logits - logsum).astype(jnp.bfloat16)
    mixed = jnp.einsum("rhqk,rkhd->rqhd", weights, values, preferred_element_type=jnp.float32)
    return (mixed, logsum)


def attend_back(query, keys, values, mask, logsum, grad_mixed):
    scores = jnp.einsum("rqhd,rkhd->rhqk", query, keys, preferred_element_type=jnp.float32)
    logits = jnp.where(mask[:, None], scores * HEAD_DIM ** (-0.5), -1e30)
    weights = jnp.exp(logits - logsum)
    low_weights = weights.astype(jnp.bfloat16)
    grad_weights = jnp.einsum(
        "rqhd,rkhd->rhqk", grad_mixed, values, preferred_element_type=jnp.float32
    )
    inner = jnp.sum(grad_weights * weights, axis=-1, keepdims=True)
    grad_scores = (weights * (grad_weights - inner) * HEAD_DIM ** (-0.5)).astype(jnp.bfloat16)
    grad_query = jnp.einsum(
        "rhqk,rkhd->rqhd", grad_scores, keys, preferred_element_type=jnp.float32
    )
    grad_keys = jnp.einsum(
        "rhqk,rqhd->rkhd", grad_scores, query, preferred_element_type=jnp.float32
    )
    grad_values = jnp.einsum(
        "rhqk,rqhd->rkhd", low_weights, grad_mixed, preferred_element_type=jnp.float32
    )
    return (grad_query, grad_keys, grad_values)


def shards(inputs, lengths, gains, w_qkv, w_out, w_up, w_down, cotangent):
    layers = w_qkv.shape[0]
    rows = inputs.shape[0]
    seg = inputs.shape[2]
    heads = w_out.shape[1] // HEAD_DIM
    offset = lax.axis_index("sp") * seg
    seq = seg * lax.axis_size("sp")
    cosine, sine = tables(offset, seg)
    mask = visible(lengths, offset, seg, seq)
    hidden = inputs.astype(jnp.float32)
    kept_clean = []
    layer = 0
    low_attn, scaled_attn, inverse_attn = norm_in(hidden, gains[layer, 0])
    query, keys, values = project(low_attn, w_qkv[layer], cosine, sine, heads)
    clean = collect(keys, values)
    kept_attn = [(low_attn, scaled_attn, inverse_attn)]
    kept_clean.append(clean)
    joined = join(query, keys, values, clean)
    attended = attend(joined[0], joined[1], joined[2], mask)
    low_mixed = attended[0].reshape(rows, 2, seg, -1).astype(jnp.bfloat16)
    branch = jnp.einsum(
        "rcse,ed->rcsd", low_mixed, w_out[layer], preferred_element_type=jnp.float32
    )
    hidden = hidden + reduce_branch(branch)
    low_mlp, scaled_mlp, inverse_mlp = norm_in(hidden, gains[layer, 1])
    kept_mlp = [(low_mlp, scaled_mlp, inverse_mlp)]
    upward = jnp.einsum("rcsd,df->rcsf", low_mlp, w_up[layer], preferred_element_type=jnp.float32)
    active = jax.nn.gelu(upward, approximate=True).astype(jnp.bfloat16)
    branch = jnp.einsum("rcsf,fd->rcsd", active, w_down[layer], preferred_element_type=jnp.float32)
    hidden = hidden + reduce_branch(branch)
    hidden_out = hidden.astype(jnp.bfloat16)
    grad = cotangent.astype(jnp.float32)
    qkv_list = [None] * layers
    out_list = [None] * layers
    up_list = [None] * layers
    down_list = [None] * layers
    gain_list = [None] * layers
    for layer in reversed(range(layers)):
        low_normed, scaled, inverse = kept_mlp[layer]
        upward = jnp.einsum(
            "rcsd,df->rcsf", low_normed, w_up[layer], preferred_element_type=jnp.float32
        )
        active, gelu_back = jax.vjp(partial(jax.nn.gelu, approximate=True), upward)
        low_active = active.astype(jnp.bfloat16)
        grad_branch = grad.astype(jnp.bfloat16)
        down_list[layer] = jnp.einsum(
            "rcsf,rcsd->fd", low_active, grad_branch, preferred_element_type=jnp.float32
        )
        grad_active = jnp.einsum(
            "rcsd,fd->rcsf", grad_branch, w_down[layer], preferred_element_type=jnp.float32
        )
        grad_upward = gelu_back(grad_active)[0].astype(jnp.bfloat16)
        up_list[layer] = jnp.einsum(
            "rcsd,rcsf->df", low_normed, grad_upward, preferred_element_type=jnp.float32
        )
        partial_grad = jnp.einsum(
            "rcsf,df->rcsd", grad_upward, w_up[layer], preferred_element_type=jnp.float32
        )
        grad_normed = reduce_branch(partial_grad)
        through, second_gain = norm_back(grad_normed, scaled, inverse, gains[layer, 1])
        grad = grad + through
        low_attn, scaled_attn, inverse_attn = kept_attn[layer]
        query, keys, values = project(low_attn, w_qkv[layer], cosine, sine, heads)
        clean = collect(keys, values)
        joined = join(query, keys, values, clean)
        attended = attend(joined[0], joined[1], joined[2], mask)
        low_mixed = attended[0].reshape(rows, 2, seg, -1).astype(jnp.bfloat16)
        grad_branch = grad.astype(jnp.bfloat16)
        out_list[layer] = jnp.einsum(
            "rcse,rcsd->ed", low_mixed, grad_branch, preferred_element_type=jnp.float32
        )
        grad_mixed = jnp.einsum(
            "rcsd,ed->rcse", grad_branch, w_out[layer], preferred_element_type=jnp.float32
        )
        grad_mixed = grad_mixed.astype(jnp.bfloat16).reshape(rows, 2 * seg, heads, HEAD_DIM)
        grad_query, grad_keys, grad_values = attend_back(
            joined[0], joined[1], joined[2], mask, attended[1], grad_mixed
        )
        clean_grads = (
            lax.psum_scatter(
                grad_keys[:, seg:].reshape(rows, seq, -1), "sp", scatter_dimension=1, tiled=True
            ),
            lax.psum_scatter(
                grad_values[:, seg:].reshape(rows, seq, -1), "sp", scatter_dimension=1, tiled=True
            ),
        )
        local_shape = (rows, seg, heads, HEAD_DIM)
        key_grad = jnp.stack([grad_keys[:, :seg], clean_grads[0].reshape(local_shape)], axis=1)
        value_grad = jnp.stack([grad_values[:, :seg], clean_grads[1].reshape(local_shape)], axis=1)
        query_grad = grad_query.reshape(rows, 2, seg, heads, HEAD_DIM)
        stacked = jnp.stack(
            [rotate(query_grad, cosine, -sine), rotate(key_grad, cosine, -sine), value_grad]
        )
        stacked = stacked.astype(jnp.bfloat16).reshape(3, rows, 2, seg, -1)
        qkv_list[layer] = jnp.einsum(
            "rcsd,trcse->tde", low_attn, stacked, preferred_element_type=jnp.float32
        )
        partial_grad = jnp.einsum(
            "trcse,tde->rcsd", stacked, w_qkv[layer], preferred_element_type=jnp.float32
        )
        grad_normed = reduce_branch(partial_grad)
        through, first_gain = norm_back(grad_normed, scaled_attn, inverse_attn, gains[layer, 0])
        grad = grad + through
        gain_list[layer] = jnp.stack([first_gain, second_gain])
    qkv_all = jnp.stack(qkv_list)
    out_all = jnp.stack(out_list)
    up_all = jnp.stack(up_list)
    down_all = jnp.stack(down_list)
    gain_all = jnp.stack(gain_list)
    partly = (
        lax.psum_scatter(qkv_all, "dp", scatter_dimension=2, tiled=True),
        lax.psum_scatter(out_all, "dp", scatter_dimension=2, tiled=True),
        lax.psum_scatter(up_all, "dp", scatter_dimension=1, tiled=True),
        lax.psum_scatter(down_all, "dp", scatter_dimension=2, tiled=True),
        lax.psum_scatter(gain_all, "dp", scatter_dimension=2, tiled=True),
    )
    summed = (
        lax.psum_scatter(partly[0], "sp", scatter_dimension=2, tiled=True),
        lax.psum_scatter(partly[1], "sp", scatter_dimension=2, tiled=True),
        lax.psum_scatter(partly[2], "sp", scatter_dimension=1, tiled=True),
        lax.psum_scatter(partly[3], "sp", scatter_dimension=2, tiled=True),
        lax.psum_scatter(partly[4], "sp", scatter_dimension=2, tiled=True),
    )
    return (hidden_out, grad, summed[0], summed[1], summed[2], summed[3], summed[4])


CH = 256
RW = 64
NEG = -1e30
GC = 0.7978845608028654
GA = 0.044715
BF = jnp.bfloat16
F32 = jnp.float32
MESH = pl.DeviceIdType.MESH
VM = pl.BlockSpec(memory_space=pltpu.VMEM)
ANY = pl.BlockSpec(memory_space=pl.ANY)


def nn(a, b):
    return lax.dot_general(a, b, (((1,), (0,)), ((), ())), preferred_element_type=F32)


def nt(a, b):
    return lax.dot_general(a, b, (((1,), (1,)), ((), ())), preferred_element_type=F32)


def tn(a, b):
    return lax.dot_general(a, b, (((0,), (0,)), ((), ())), preferred_element_type=F32)


def each(count, body, start=0):
    def step(i, carry):
        body(i)
        return carry

    lax.fori_loop(start, count, step, 0)


class Copies:
    def __init__(self, sems, base, make):
        self.sems, self.base, self.make = sems, base, make

    def at(self, i):
        src, dst, dev = self.make(i)
        return pltpu.make_async_remote_copy(
            src_ref=src,
            dst_ref=dst,
            send_sem=self.sems[0].at[self.base + i],
            recv_sem=self.sems[1].at[self.base + i],
            device_id=dev,
            device_id_type=MESH,
        )

    def start(self, i):
        self.at(i).start()

    def arrived(self, i):
        self.at(i).wait_recv()

    def sent(self, i):
        self.at(i).wait_send()


SCRATCH = dict(
    x=((4, CH, 768), BF),
    cot=((1024, 768), BF),
    wT=((576, 768), BF),
    wfull=((4, 192, 768), BF),
    wup=((768, 768), BF),
    wdown=((768, 768), BF),
    cs=((2, 2, 32, CH), F32),
    a=((1024, 768), BF),
    tT=((4, 768, CH), BF),
    tT2=((4, 768, CH), BF),
    qT=((4, 3, 64, CH), BF),
    kvT=((6, 2, 3, 64, CH), BF),
    kaug=((6, 3, CH, 128), BF),
    vn=((6, 3, CH, 128), BF),
    qtail=((12, 16, CH), BF),
    gtail=((12, 16, CH), BF),
    maskb=((4, 16, CH), BF),
    plain=((16, CH), BF),
    oacc=((4, 3, 64, CH), F32),
    stat=((12, 8, CH), F32),
    on=((4, CH, 192), BF),
    oT=((4, 192, CH), BF),
    orecv=((4, 3, RW, 192), BF),
    h1=((4, RW, 768), F32),
    b=((1024, 768), BF),
    m=((1024, 768), BF),
    gu=((1024, 768), BF),
    gy=((1024, 768), BF),
    g1=((4, RW, 768), F32),
    goT=((4, 3, 64, CH), BF),
    dkv=((6, 2, 3, 64, CH), F32),
    dkvs=((2, 2, 3, 64, CH), BF),
    dkvr=((2, 2, 3, 64, CH), BF),
    dq=((4, 3, 64, CH), F32),
    gT=((4, 9, 64, CH), BF),
    st2=((4, CH, 768), BF),
    st3=((4, CH, 768), BF),
    st4=((4, CH, 768), BF),
    ra2=((4, 128, 768), BF),
    ra3=((4, 128, 768), BF),
    ra4=((4, 128, 768), BF),
    rb2=((4, RW, 768), BF),
    rb3=((4, RW, 768), BF),
    rb4=((4, RW, 768), BF),
    pU=((4, 192, 768), BF),
    pW=((4, 192, 768), BF),
    pO=((4, 192, 192), BF),
    pQ=((4, 192, 192), BF),
    pK=((4, 192, 384), BF),
    xU=((4, 96, 768), BF),
    xW=((96, 768), BF),
    xWs=((96, 768), BF),
    xO=((4, 96, 192), BF),
    xQ=((4, 96, 192), BF),
    xK=((4, 96, 384), BF),
    zU=((3, 96, 768), BF),
    zW=((2, 192, 768), BF),
    zW2=((192, 768), BF),
    zO=((3, 96, 192), BF),
    zQ=((3, 96, 192), BF),
    zK=((3, 96, 384), BF),
    hid=((1024, 768), BF),
    ig=((1024, 768), BF),
    gsum=((4, 8, 768), F32),
    gx=((2, 8, 768), F32),
    gz=((3, 8, 768), F32),
)

TILES = (
    ((0, 0), (2, 1)),
    ((1, 0), (3, 1), (2, 3)),
    ((2, 2),),
    ((3, 2), (2, 3)),
)


def step_kernel(*refs):
    (x_h, len_r, gains, wqkv_h, wout_h, wup_h, wdown_h, cot_h, cs_h) = refs[:9]
    (hid_h, ig_h, outQ, outO, outU, outW, outG) = refs[9:16]
    s = SimpleNamespace(**dict(zip(SCRATCH, refs[16 : 16 + len(SCRATCH)])))
    lsem, ssem, rsem = refs[16 + len(SCRATCH) :]
    sems = (ssem, rsem)
    hid, ig = s.hid, s.ig
    t = lax.axis_index("tp")
    z = lax.axis_index("dp")
    x = lax.axis_index("sp")
    c = lax.rem(t, 2)
    y = lax.div(t, 2)
    slot = 2 * c + y
    pslot = 2 * c + 1 - y
    partner = t + 1 - 2 * c
    ypeer = t + 2 - 4 * y
    diag = 3 - t
    tpdev = (None, partner, ypeer, diag)
    tpslot = (slot, 2 * (1 - c) + y, pslot, 2 * (1 - c) + 1 - y)

    barrier = pltpu.get_barrier_semaphore()
    for dev in (
        {"tp": partner},
        {"tp": ypeer},
        {"tp": diag},
        {"sp": 1 - x},
        {"dp": lax.rem(z + 1, 4)},
        {"dp": lax.rem(z + 2, 4)},
        {"dp": lax.rem(z + 3, 4)},
    ):
        pl.semaphore_signal(barrier, inc=1, device_id=dev, device_id_type=MESH)

    def own(ref, ch):
        return ref.at[pl.ds(ch * CH + slot * RW, RW), :]

    def half(ref, ch):
        return ref.at[pl.ds(ch * CH + c * 128, 128), :]

    def load(i, src, dst):
        return pltpu.make_async_copy(src, dst, lsem.at[i])

    loads = [load(i, x_h.at[i], s.x.at[i]) for i in range(4)]
    loads.append(load(4, wqkv_h, s.wT))
    loads.append(load(5, cs_h.at[pl.ds(2 * x, 2)], s.cs))
    loads.append(load(6, wout_h, s.wfull.at[slot]))
    loads.append(load(7, wup_h, s.wup))
    loads.append(load(8, wdown_h, s.wdown))
    loads.append(load(9, cot_h, s.cot))
    for i in (4, 2, 5, 3, 6, 0, 1, 7, 8, 9):
        loads[i].start()

    base = [0]

    def family(count, make):
        made = Copies(sems, base[0], make)
        made.count = count
        base[0] += count
        return made

    def spread(ref):
        return (
            family(4, lambda i: (own(ref, i), own(ref, i), {"tp": ypeer})),
            family(4, lambda i: (half(ref, i), half(ref, i), {"tp": partner})),
        )

    def gather(stage, ra, rb):
        return (
            family(
                4,
                lambda i: (
                    stage.at[i, pl.ds((1 - c) * 128, 128), :],
                    ra.at[i],
                    {"tp": partner},
                ),
            ),
            family(
                4, lambda i: (stage.at[i, pl.ds(pslot * RW, RW), :], rb.at[i], {"tp": ypeer})
            ),
        )

    def wmake(i):
        if i == 0:
            return (s.wfull.at[slot], s.wfull.at[slot], {"tp": ypeer})
        pair = pl.ds(2 * c, 2)
        return (s.wfull.at[pair], s.wfull.at[pair], {"tp": partner})

    wcopy = family(2, wmake)
    kvcopy = family(2, lambda i: (s.kvT.at[2 + i], s.kvT.at[4 + i], {"sp": 1 - x}))
    dkcopy = family(2, lambda i: (s.dkvs.at[i], s.dkvr.at[i], {"sp": 1 - x}))
    ocopy = [
        family(
            4,
            lambda i, r=r: (
                s.on.at[i, pl.ds(tpslot[r] * RW, RW), :],
                s.orecv.at[i, r - 1],
                {"tp": tpdev[r]},
            ),
        )
        for r in (1, 2, 3)
    ]
    ag1 = spread(s.b)
    ag2 = spread(hid)
    ag3 = spread(s.gy)
    ag4 = spread(ig)
    rs2 = gather(s.st2, s.ra2, s.rb2)
    rs3 = gather(s.st3, s.ra3, s.rb3)
    rs4 = gather(s.st4, s.ra4, s.rb4)
    all_waits = [wcopy, *ocopy, *ag1, *ag2, *ag3, *ag4, *rs2, *rs3, *rs4]

    znear = z + 1 - 2 * lax.rem(z, 2)
    zfar = lax.rem(z + 2, 4)
    order = (lax.rem(znear + 2, 4), znear, zfar, z)

    class Piece:
        def __init__(self, stage, xr, zr):
            self.stage, self.xr, self.zr = stage, xr, zr
            rows = pl.ds(96 * x, 96)
            self.xc = family(
                4,
                lambda i: (
                    stage.at[i, pl.ds(96 * (1 - x), 96), :],
                    xr.at[i],
                    {"sp": 1 - x},
                ),
            )
            self.nc = family(
                2, lambda i: (stage.at[order[i], rows, :], zr.at[1 - i], {"dp": znear})
            )
            self.fc = family(1, lambda i: (stage.at[zfar, rows, :], zr.at[2], {"dp": zfar}))
            all_waits.extend([self.xc, self.nc, self.fc])

        def compute(self, value, send=True):
            for zz in order:
                self.stage[zz] = value(zz).astype(BF)
                if send:
                    self.xc.start(zz)

        def send(self):
            for zz in order:
                self.xc.start(zz)

        def both(self, zz):
            self.xc.arrived(zz)
            return self.stage[zz, pl.ds(96 * x, 96), :].astype(F32) + self.xr[zz].astype(F32)

        def z_near(self):
            for i in range(2):
                self.stage[order[i], pl.ds(96 * x, 96), :] = self.both(order[i]).astype(BF)
                self.nc.start(i)

        def z_far(self):
            total = self.both(zfar)
            self.nc.arrived(0)
            total = total + self.zr[1].astype(F32)
            self.stage[zfar, pl.ds(96 * x, 96), :] = total.astype(BF)
            self.fc.start(0)

        def finish(self):
            total = self.both(z)
            self.nc.arrived(1)
            self.fc.arrived(0)
            return total + self.zr[0].astype(F32) + self.zr[2].astype(F32)

    pieceU = Piece(s.pU, s.xU, s.zU)
    pieceK = Piece(s.pK, s.xK, s.zK)

    def near_make(i):
        k = 1 - lax.div(i, 2)
        rows = pl.ds(96 * lax.rem(i, 2), 96)
        return (
            s.pW.at[lax.rem(znear + 2 * k, 4), rows, :],
            s.zW.at[k, rows, :],
            {"dp": znear},
        )

    def far_make(i):
        rows = pl.ds(96 * i, 96)
        return (s.pW.at[zfar, rows, :], s.zW2.at[rows, :], {"dp": zfar})

    wnear = family(4, near_make)
    wfar = family(2, far_make)
    wlast = family(1, lambda i: (s.xWs, s.xW, {"sp": 1 - x}))
    all_waits.extend([wnear, wfar, wlast])

    def send_near(value):
        for i, zz in enumerate(order):
            s.pW[zz] = value(zz).astype(BF)
            if i < 2:
                wnear.start(2 * i)
                wnear.start(2 * i + 1)

    def send_far():
        for i in range(2):
            wnear.arrived(i)
            rows = pl.ds(96 * i, 96)
            total = s.pW[zfar, rows, :].astype(F32) + s.zW[1, rows, :].astype(F32)
            s.pW[zfar, rows, :] = total.astype(BF)
            wfar.start(i)

    def summed(side):
        rows = pl.ds(96 * side, 96)
        total = s.pW[z, rows, :].astype(F32) + s.zW[0, rows, :].astype(F32)
        return total + s.zW2[rows, :].astype(F32)

    def send_last():
        for i in range(2):
            wnear.arrived(2 + i)
            wfar.arrived(i)
        s.xWs[...] = summed(1 - x).astype(BF)
        wlast.start(0)

    pieceO = Piece(s.pO, s.xO, s.zO)
    pieceQ = Piece(s.pQ, s.xQ, s.zQ)

    gtp = [
        family(1, lambda i, r=r: (s.gsum.at[t], s.gsum.at[t], {"tp": tpdev[r]}))
        for r in (1, 2, 3)
    ]
    gxc = family(1, lambda i: (s.gx.at[0], s.gx.at[1], {"sp": 1 - x}))
    gzc = family(
        3, lambda i: (s.gx.at[0], s.gz.at[i], {"dp": lax.rem(z + 1 + i, 4)})
    )
    all_waits.extend([*gtp, gxc, gzc])

    row = lax.broadcasted_iota(jnp.int32, (64, CH), 0)
    col = lax.broadcasted_iota(jnp.int32, (64, CH), 1)
    blk = lax.shift_right_logical(col, 4)
    few = row[:16]
    blk16 = blk[:16]
    for v, shown in enumerate((few == blk16, few < blk16, few <= blk16, few < 16)):
        s.maskb[v] = jnp.where(shown, 0.0, NEG).astype(BF)
    s.plain[...] = jnp.where(few == 0, 1.0, 0.0).astype(BF)
    length = len_r[0]
    hot = jnp.where((row == blk) | ((row > 16) & (row < 20)), 1.0, 0.0).astype(F32)
    unit = jnp.where(row < 3, 1.0, 0.0).astype(F32)

    def minus(value, first):
        high = value.astype(BF).astype(F32)
        middle = (value - high).astype(BF).astype(F32)
        low = value - high - middle
        out = jnp.where(few == first, -high, 0.0)
        out = jnp.where(few == first + 1, -middle, out)
        return jnp.where(few == first + 2, -low, out)

    def query_tail(value):
        return (minus(value, 1) + jnp.where(few == 0, 1.0, 0.0)).astype(BF)

    def key_tail(start):
        outside = (row == 16) & (col + start >= length)
        return jnp.where(outside, NEG, hot)

    def keep_keys(kt, h, kT, vT, tail):
        s.kaug[kt, h] = jnp.transpose(jnp.concatenate([kT, tail], axis=0)).astype(BF)
        s.vn[kt, h] = jnp.transpose(jnp.concatenate([vT, unit], axis=0)).astype(BF)

    for ref in (s.dkv, s.dq):
        ref[...] = jnp.zeros_like(ref)
    s.gsum[...] = jnp.zeros_like(s.gsum)

    loads[4].wait()
    pl.semaphore_wait(barrier, 7)
    loads[6].wait()
    wcopy.start(0)
    loads[5].wait()

    gain1 = gains[0:1, :]
    gain2 = gains[1:2, :]

    def centred(v):
        centre = v - jnp.mean(v, axis=-1, keepdims=True)
        inverse = lax.rsqrt(jnp.mean(centre * centre, axis=-1, keepdims=True) + EPSILON)
        return centre * inverse, inverse

    def project_chunk(ch, j):
        def rows(r):
            v = s.x[ch, pl.ds(r * RW, RW), :].astype(F32)
            s.a[pl.ds(ch * CH + r * RW, RW), :] = (centred(v)[0] * gain1).astype(BF)

        for r in range(4):
            rows(r)
        proj = nt(s.wT[...], s.a[pl.ds(ch * CH, CH), :])
        cos = s.cs[j, 0]
        sin = s.cs[j, 1]
        tail = key_tail(x * (2 * CH) + j * CH)
        for h in range(3):
            turned = []
            for i in range(2):
                first = proj[i * 192 + h * 64 : i * 192 + h * 64 + 32]
                second = proj[i * 192 + h * 64 + 32 : i * 192 + h * 64 + 64]
                turned.append(
                    jnp.concatenate(
                        [first * cos - second * sin, second * cos + first * sin], axis=0
                    )
                )
            vT = proj[384 + h * 64 : 384 + h * 64 + 64]
            s.qT[ch, h] = (turned[0] * 0.125).astype(BF)
            s.kvT[ch, 0, h] = turned[1].astype(BF)
            s.kvT[ch, 1, h] = vT.astype(BF)
            keep_keys(ch, h, turned[1], vT, tail)

    def clean_chunk(j):
        loads[2 + j].wait()
        project_chunk(2 + j, j)

        @pl.when(x == 0)
        def _():
            kvcopy.start(j)

    for j in range(2):
        clean_chunk(j)

    def noisy_chunk(j):
        loads[j].wait()
        project_chunk(j, j)

    for j in range(2):
        noisy_chunk(j)

    def scores(ch, h, kt, v, tail):
        query = jnp.concatenate([s.qT[ch, h], s.maskb[v], tail], axis=0)
        return nn(s.kaug[kt, h, :, 0:96], query)

    HEADS3 = [(ch, h) for ch in range(4) for h in range(3)]

    def mix(heads, tiles, fresh):
        tops = {}
        for ch, h in heads:
            top = None if fresh else s.stat[ch * 3 + h, 0:1, :]
            for kt, v in tiles[ch]:
                p = jnp.max(scores(ch, h, kt, v, s.plain[...]), axis=0, keepdims=True)
                top = p if top is None else jnp.maximum(top, p)
            tops[ch, h] = top
        items = [(ch, h, kt, v) for ch, h in heads for kt, v in tiles[ch]]
        tails = {}

        def product(ch, h, kt, v):
            if (ch, h) not in tails:
                tails[ch, h] = query_tail(tops[ch, h])
            return scores(ch, h, kt, v, tails[ch, h])

        sums, mixed = {}, {}
        ahead = product(*items[0])
        for n, (ch, h, kt, v) in enumerate(items):
            logits = ahead
            if n + 1 < len(items):
                ahead = product(*items[n + 1])
            e = jnp.exp(logits)
            total = jnp.sum(e, axis=0, keepdims=True)
            part = nn(s.kvT[kt, 1, h], e.astype(BF))
            sums[ch, h] = sums[ch, h] + total if (ch, h) in sums else total
            mixed[ch, h] = mixed[ch, h] + part if (ch, h) in mixed else part
            if n + 1 == len(items) or items[n + 1][:2] != (ch, h):
                at = ch * 3 + h
                total, part = sums[ch, h], mixed[ch, h]
                if not fresh:
                    scale = jnp.exp(s.stat[at, 0:1, :] - tops[ch, h])
                    total = total + s.stat[at, 1:2, :] * scale
                    part = part + s.oacc[ch, h] * scale
                s.stat[at, 0:1, :] = tops[ch, h]
                s.stat[at, 1:2, :] = total
                s.oacc[ch, h] = part

    mix(HEADS3, TILES, True)
    wcopy.arrived(0)
    wcopy.start(1)

    def close(ch):
        for h in range(3):
            at = ch * 3 + h
            total = s.stat[at, 1:2, :]
            out = s.oacc[ch, h] / total
            s.oacc[ch, h] = out
            s.qtail[at] = query_tail(s.stat[at, 0:1, :] + jnp.log(total))
            s.oT[ch, h * 64 : h * 64 + 64, :] = out.astype(BF)
        whole = jnp.concatenate([s.oacc[ch, h] for h in range(3)], axis=0)
        s.on[ch] = jnp.transpose(whole).astype(BF)
        for copy in ocopy:
            copy.start(ch)

    @pl.when(x == 1)
    def _():
        for j in range(2):
            kvcopy.arrived(j)
            tail = key_tail(j * CH)
            for h in range(3):
                keep_keys(
                    4 + j, h, s.kvT[4 + j, 0, h].astype(F32), s.kvT[4 + j, 1, h].astype(F32), tail
                )
            tiles = [((4 + j, 3),)] * 4
            if j == 0:
                mix(HEADS3, tiles, False)
        for ch in range(4):
            mix(HEADS3[3 * ch : 3 * ch + 3], tiles, False)
            close(ch)

    @pl.when(x == 0)
    def _():
        for ch in range(4):
            close(ch)

    wcopy.arrived(1)

    def out_rows(ch):
        total = s.x[ch, pl.ds(slot * RW, RW), :].astype(F32)
        total = total + nn(s.on[ch, pl.ds(slot * RW, RW), :], s.wfull[slot])
        for r in (1, 2, 3):
            ocopy[r - 1].arrived(ch)
            total = total + nn(s.orecv[ch, r - 1], s.wfull[tpslot[r]])
        s.h1[ch] = total
        own(s.b, ch)[...] = (centred(total)[0] * gain2).astype(BF)
        ag1[0].start(ch)

    each(4, out_rows)
    for i in (7, 8, 9):
        loads[i].wait()

    def add_pair(rs, stage, ra, ch):
        rs[0].arrived(ch)
        rows = pl.ds(pslot * RW, RW)
        total = stage[ch, rows, :].astype(F32) + ra[ch, pl.ds((1 - y) * RW, RW), :].astype(F32)
        stage[ch, rows, :] = total.astype(BF)
        rs[1].start(ch)

    def add_last(rs, stage, ra, rb, ch):
        rs[1].arrived(ch)
        rows = pl.ds(slot * RW, RW)
        total = stage[ch, rows, :].astype(F32) + ra[ch, pl.ds(y * RW, RW), :].astype(F32)
        return total + rb[ch].astype(F32)

    def relay(ag, ch):
        ag[0].arrived(ch)
        ag[1].start(ch)

    def norm_back(grad, stream, gain, at):
        scaled, inverse = centred(stream)
        inner = grad * gain
        s.gsum[t, at : at + 1, :] += jnp.sum(grad * scaled, axis=0, keepdims=True)
        inner_mean = jnp.mean(inner, axis=-1, keepdims=True)
        mixed_mean = jnp.mean(inner * scaled, axis=-1, keepdims=True)
        return inverse * (inner - inner_mean - scaled * mixed_mean)

    def second_back(ch):
        grad = add_last(rs3, s.st3, s.ra3, s.rb3, ch)
        through = norm_back(grad, s.h1[ch], gain2, 1)
        cot = s.cot[pl.ds(ch * CH + slot * RW, RW), :].astype(F32)
        g1 = cot + through
        s.g1[ch] = g1
        own(s.gy, ch)[...] = g1.astype(BF)
        ag3[0].start(ch)

    def feed(ch):
        rows = pl.ds(ch * CH, CH)

        @pl.when(ch >= 1)
        def _():
            add_pair(rs3, s.st3, s.ra3, ch - 1)

        ag1[1].arrived(ch)
        low_b = s.b[rows, :]
        low_g = s.cot[rows, :]
        for n in range(3):
            cols = slice(n * CH, (n + 1) * CH)
            u = nn(low_b, s.wup[:, cols])
            gm = nt(low_g, s.wdown[cols, :])
            square = u * u
            hp = 0.5 + 0.5 * jnp.tanh(u * (GC + GC * GA * square))
            act = u * hp
            slope = hp + (act - act * hp) * (2.0 * GC + 6.0 * GC * GA * square)
            s.m[rows, cols] = act.astype(BF)
            s.gu[rows, cols] = (slope * gm).astype(BF)

        s.st3[ch] = nt(s.gu[rows, :], s.wup[...]).astype(BF)
        rs3[0].start(ch)

        @pl.when(ch < 3)
        def _():
            relay(ag1, ch + 1)

        s.st2[ch] = nn(s.m[rows, :], s.wdown[...]).astype(BF)
        rs2[0].start(ch)

    relay(ag1, 0)
    each(4, feed)
    add_pair(rs3, s.st3, s.ra3, 3)

    def transposed(dst, src):
        for ch in range(4):
            dst[ch] = jnp.transpose(src[pl.ds(ch * CH, CH), :])

    def rows_by(lhs, rhs):
        def value(zz):
            total = nn(lhs[0, pl.ds(192 * zz, 192), :], rhs[0:CH, :])
            for ch in range(1, 4):
                total = total + nn(lhs[ch, pl.ds(192 * zz, 192), :], rhs[ch * CH : ch * CH + CH, :])
            return total

        return value

    def back_tiles(items):
        def products(ch, h, kt, v):
            at = ch * 3 + h
            grad = jnp.concatenate([s.goT[ch, h], s.gtail[at]], axis=0)
            return scores(ch, h, kt, v, s.qtail[at]), nn(s.vn[kt, h, :, 0:80], grad)

        ahead = products(*items[0])
        for n, (ch, h, kt, v) in enumerate(items):
            logits, gp = ahead
            if n + 1 < len(items):
                ahead = products(*items[n + 1])
            weights = jnp.exp(logits)
            gs = (weights * gp).astype(BF)
            s.dkv[kt, 1, h] += nt(s.goT[ch, h], weights.astype(BF))
            s.dkv[kt, 0, h] += nt(s.qT[ch, h], gs)
            s.dq[ch, h] += nn(s.kvT[kt, 0, h], gs)

    def attention_back(ch):
        ag3[1].arrived(ch)
        goT = nt(s.wfull[slot], s.gy[pl.ds(ch * CH, CH), :])
        for h in range(3):
            low = goT[h * 64 : h * 64 + 64].astype(BF)
            s.goT[ch, h] = low
            inner = jnp.sum(low.astype(F32) * s.oacc[ch, h], axis=0, keepdims=True)
            s.gtail[ch * 3 + h] = minus(inner, 0).astype(BF)

        @pl.when(x == 1)
        def _():
            back_tiles([(ch, h, 4 + j, 3) for j in range(2) for h in range(3)])
            if ch == 3:
                for j in range(2):
                    s.dkvs[j] = s.dkv[4 + j].astype(BF)
                    dkcopy.start(j)

        back_tiles([(ch, h, kt, v) for h in range(3) for kt, v in TILES[ch]])

    second_back(0)
    second_back(1)
    transposed(s.tT, s.b)
    pieceU.compute(rows_by(s.tT, s.gu))
    transposed(s.tT, s.cot)
    send_near(rows_by(s.tT, s.m))
    second_back(2)
    relay(ag3, 0)
    relay(ag3, 1)
    second_back(3)
    for ch in range(4):
        add_pair(rs2, s.st2, s.ra2, ch)
    relay(ag3, 2)
    attention_back(0)
    attention_back(1)
    relay(ag3, 3)
    attention_back(2)
    attention_back(3)

    def turn_back(u, cos, sin):
        first = u[:32]
        second = u[32:]
        return jnp.concatenate([first * cos + second * sin, second * cos - first * sin], axis=0)

    def grad_rows(ch):
        j = ch % 2
        cos = s.cs[j, 0]
        sin = s.cs[j, 1]
        for h in range(3):
            s.gT[ch, h] = turn_back(s.dq[ch, h] * 0.125, cos, sin).astype(BF)
            s.gT[ch, 3 + h] = turn_back(s.dkv[ch, 0, h], cos, sin).astype(BF)
            s.gT[ch, 6 + h] = s.dkv[ch, 1, h].astype(BF)
        s.st4[ch] = tn(s.gT[ch].reshape(576, CH), s.wT[...]).astype(BF)
        rs4[0].start(ch)

    def turn_query(ch):
        for h in range(3):
            s.gT[ch, h] = turn_back(s.dq[ch, h] * 0.125, s.cs[ch % 2, 0], s.cs[ch % 2, 1]).astype(BF)

    def hidden_rows(ch):
        total = s.h1[ch] + add_last(rs2, s.st2, s.ra2, s.rb2, ch)
        own(hid, ch)[...] = total.astype(BF)
        ag2[0].start(ch)

    def input_rows(ch):
        grad = add_last(rs4, s.st4, s.ra4, s.rb4, ch)
        stream = s.x[ch, pl.ds(slot * RW, RW), :].astype(F32)
        total = s.g1[ch] + norm_back(grad, stream, gain1, 0)
        own(ig, ch)[...] = total.astype(BF)
        ag4[0].start(ch)

    def out_piece(zz):
        total = nt(s.tT[0, pl.ds(192 * zz, 192), :], s.oT[0])
        for ch in range(1, 4):
            total = total + nt(s.tT[ch, pl.ds(192 * zz, 192), :], s.oT[ch])
        return total

    def part_piece(lo, hi):
        def value(zz):
            total = None
            for ch in range(4):
                grads = s.gT[ch, lo:hi].reshape((hi - lo) * 64, CH)
                part = nt(s.tT2[ch, pl.ds(192 * zz, 192), :], grads)
                total = part if total is None else total + part
            return total

        return value

    for ch in range(2):
        grad_rows(ch)
    for ch in range(2):
        add_pair(rs4, s.st4, s.ra4, ch)
    pieceU.z_near()
    for ch in range(3):
        hidden_rows(ch)
    send_far()
    hidden_rows(3)
    transposed(s.tT, s.gy)
    pieceO.compute(out_piece, False)
    transposed(s.tT2, s.a)
    for ch in range(2, 4):
        turn_query(ch)
    pieceQ.compute(part_piece(0, 3), False)

    @pl.when(x == 1)
    def _():
        for j in range(2):
            dkcopy.sent(j)

    @pl.when(x == 0)
    def _():
        for j in range(2):
            dkcopy.arrived(j)
            s.dkv[2 + j] += s.dkvr[j].astype(F32)

    pieceO.send()
    pieceQ.send()
    for ch in range(2, 4):
        grad_rows(ch)
    for ch in range(2, 4):
        add_pair(rs4, s.st4, s.ra4, ch)
    pieceK.compute(part_piece(3, 9))
    for ch in range(2):
        input_rows(ch)
    pieceU.z_far()
    for ch in range(2):
        relay(ag2, ch)
    pieceO.z_near()
    pieceQ.z_near()
    for ch in range(2, 4):
        relay(ag2, ch)
    send_last()
    for ch in range(2, 4):
        input_rows(ch)

    for copy in gtp:
        copy.start(0)
    pieceK.z_near()
    for ch in range(2):
        relay(ag4, ch)
    pieceO.z_far()
    pieceQ.z_far()
    for copy in gtp:
        copy.arrived(0)
    s.gx[0] = s.gsum[0] + s.gsum[1] + s.gsum[2] + s.gsum[3]
    gxc.start(0)
    pieceK.z_far()
    outU[...] = pieceU.finish()
    wlast.arrived(0)
    outW[...] = summed(x) + s.xW[...].astype(F32)
    gxc.arrived(0)
    gxc.sent(0)
    s.gx[0] = s.gx[0] + s.gx[1]
    for i in range(3):
        gzc.start(i)
    for ch in range(2, 4):
        relay(ag4, ch)
    outO[...] = jnp.transpose(pieceO.finish())
    outQ[0] = pieceQ.finish()
    both = pieceK.finish()
    outQ[1] = both[:, :192]
    outQ[2] = both[:, 192:]
    total = s.gx[0]
    for i in range(3):
        gzc.arrived(i)
        total = total + s.gz[i]
    for k in range(8):
        @pl.when(z * 2 + x == k)
        def _(k=k):
            outG[...] = total[0:2, 96 * k : 96 * k + 96]

    def keep(i):
        rows = pl.ds(i * CH, CH)
        return (
            pltpu.make_async_copy(hid.at[rows, :], hid_h.at[rows, :], lsem.at[10 + i]),
            pltpu.make_async_copy(ig.at[rows, :], ig_h.at[rows, :], lsem.at[14 + i]),
        )

    def save_hidden(i):
        ag2[1].arrived(i)
        keep(i)[0].start()

    def save_input(i):
        ag4[1].arrived(i)
        keep(i)[1].start()

    each(4, save_hidden)
    each(4, save_input)
    for fam in all_waits:
        if fam is gxc:
            continue
        for i in range(fam.count):
            fam.sent(i)

    @pl.when(x == 0)
    def _():
        for i in range(2):
            kvcopy.sent(i)

    def kept(i):
        for copy in keep(i):
            copy.wait()

    each(4, kept)


def finish_kernel(*refs):
    sources, results = refs[:7], refs[7:14]
    rows, wide, smalls = refs[14], refs[15], refs[16:21]
    isem, osem = refs[21:]

    def part(ref, i):
        return ref.at[pl.ds(i * CH, CH), :]

    def move(src, dst, sem):
        return pltpu.make_async_copy(src, dst, sem)

    ins = [move(part(sources[1], i), rows.at[1, i], isem.at[4 + i]) for i in range(4)]
    ins += [move(part(sources[0], i), rows.at[0, i], isem.at[i]) for i in range(4)]
    ins += [move(sources[2 + k], smalls[k], isem.at[8 + k]) for k in range(5)]
    for copy in ins:
        copy.start()
    outs = []
    for i in range(4):
        ins[i].wait()
        wide[i] = rows[1, i].astype(F32)
        outs.append(move(wide.at[i], part(results[1], i), osem.at[4 + i]))
        outs[-1].start()
    for i in range(4):
        ins[4 + i].wait()
        outs.append(move(rows.at[0, i], part(results[0], i), osem.at[i]))
        outs[-1].start()
    for k in range(5):
        ins[8 + k].wait()
        outs.append(move(smalls[k], results[2 + k], osem.at[8 + k]))
        outs[-1].start()
    for copy in outs:
        copy.wait()


def finish(arrays):
    shapes = [jax.ShapeDtypeStruct(v.shape, v.dtype) for v in arrays]
    shapes[1] = jax.ShapeDtypeStruct(arrays[1].shape, F32)
    return pl.pallas_call(
        finish_kernel,
        out_shape=shapes,
        in_specs=[ANY] * 7,
        out_specs=[ANY] * 7,
        scratch_shapes=[pltpu.VMEM((2, 4, CH, 768), BF), pltpu.VMEM((4, CH, 768), F32)]
        + [pltpu.VMEM(v.shape, v.dtype) for v in arrays[2:]]
        + [pltpu.SemaphoreType.DMA((13,)), pltpu.SemaphoreType.DMA((13,))],
        name="finish",
    )(*arrays)


def rope_table(seq):
    half_dim = HEAD_DIM // 2
    freq = 10000.0 ** (-np.arange(half_dim) * 2.0 / HEAD_DIM)
    angle = freq[:, None] * np.arange(seq)[None, :]
    both = np.stack([np.cos(angle), np.sin(angle)])
    return np.moveaxis(both.reshape(2, half_dim, seq // CH, CH), 2, 0).astype(np.float32)


def fast(inputs, lengths, gains, w_qkv, w_out, w_up, w_down, cotangent):
    seg = inputs.shape[2]
    shape = jax.ShapeDtypeStruct
    found = pl.pallas_call(
        step_kernel,
        out_shape=(
            shape((1024, 768), BF),
            shape((1024, 768), BF),
            shape((3, 96, 192), F32),
            shape((192, 96), F32),
            shape((96, 768), F32),
            shape((96, 768), F32),
            shape((2, 96), F32),
        ),
        in_specs=[ANY, pl.BlockSpec(memory_space=pltpu.SMEM), VM, ANY, ANY, ANY, ANY, ANY, ANY],
        out_specs=[ANY] * 2 + [VM] * 5,
        scratch_shapes=[pltpu.VMEM(dims, kind) for dims, kind in SCRATCH.values()]
        + [
            pltpu.SemaphoreType.DMA((18,)),
            pltpu.SemaphoreType.DMA((140,)),
            pltpu.SemaphoreType.DMA((140,)),
        ],
        compiler_params=pltpu.CompilerParams(
            collective_id=0, has_side_effects=True, vmem_limit_bytes=64 * 1024 * 1024 - 65536
        ),
        name="step",
    )(
        inputs.reshape(4, CH, 768),
        lengths,
        gains[0],
        jnp.swapaxes(w_qkv[0], 1, 2).reshape(576, 768),
        w_out[0],
        w_up[0],
        w_down[0],
        cotangent.reshape(1024, 768),
        jnp.asarray(rope_table(seg * lax.axis_size("sp"))),
    )
    hid, ig, gq, go, gu, gd, gg = finish(found)
    return (
        hid.reshape(inputs.shape),
        ig.reshape(inputs.shape),
        gq[None],
        go[None],
        gu[None],
        jnp.swapaxes(gd, 0, 1)[None],
        gg[None],
    )


def pick(*args):
    inputs, w_out = args[0], args[4]
    plain = (1, 2, 512, 768)
    sizes = (lax.axis_size("tp"), lax.axis_size("dp"), lax.axis_size("sp"))
    if inputs.shape == plain and w_out.shape[1:] == (192, 768) and sizes == (4, 4, 2):
        return fast(*args)
    return shards(*args)


def solution(mesh):
    in_specs = (
        P("dp", None, "sp", None),
        P("dp"),
        P(),
        P(None, None, None, "tp"),
        P(None, "tp", None),
        P(None, None, "tp"),
        P(None, "tp", None),
        P("dp", None, "sp", None),
    )
    out_specs = (
        P("dp", None, "sp", None),
        P("dp", None, "sp", None),
        P(None, None, ("dp", "sp"), "tp"),
        P(None, "tp", ("dp", "sp")),
        P(None, ("dp", "sp"), "tp"),
        P(None, "tp", ("dp", "sp")),
        P(None, None, ("dp", "sp")),
    )
    return jax.shard_map(pick, mesh=mesh, in_specs=in_specs, out_specs=out_specs, check_vma=False)
```

```python
from functools import partial
from types import SimpleNamespace

import jax
import jax.numpy as jnp
import numpy as np
from jax import lax
from jax.experimental import pallas as pl
from jax.experimental.pallas import tpu as pltpu
from jax.sharding import PartitionSpec as P

HEAD_DIM = 64
BLOCK = 16


EPSILON = 1e-05


def normalize(value, gain):
    centre = value - jnp.mean(value, axis=-1, keepdims=True)
    inverse = lax.rsqrt(jnp.mean(centre * centre, axis=-1, keepdims=True) + EPSILON)
    scaled = centre * inverse
    return (scaled * gain, scaled, inverse)


def norm_back(grad, scaled, inverse, gain):
    inner = grad * gain
    gain_grad = jnp.sum(grad * scaled, axis=(0, 1, 2))
    centred = inner - jnp.mean(inner, axis=-1, keepdims=True)
    result = inverse * (centred - scaled * jnp.mean(inner * scaled, axis=-1, keepdims=True))
    return (result, gain_grad)


def rotate(value, cosine, sine):
    half_dim = value.shape[-1] // 2
    first = value[..., :half_dim]
    second = value[..., half_dim:]
    return jnp.concatenate(
        [first * cosine - second * sine, second * cosine + first * sine], axis=-1
    )


def tables(offset, count):
    half_dim = HEAD_DIM // 2
    freq = 10000.0 ** (-jnp.arange(half_dim).astype(jnp.float32) * 2.0 / HEAD_DIM)
    angle = (offset + jnp.arange(count)).astype(jnp.float32)[:, None] * freq[None, :]
    return (jnp.cos(angle)[:, None, :], jnp.sin(angle)[:, None, :])


def visible(lengths, offset, seg, seq):
    places = offset + jnp.arange(seg)
    query_block = jnp.concatenate([places, places]) // BLOCK
    query_clean = jnp.arange(2 * seg) >= seg
    key_place = jnp.concatenate([places, jnp.arange(seq)])
    key_block = key_place // BLOCK
    key_clean = jnp.arange(seg + seq) >= seg
    query_noisy = jnp.logical_not(query_clean)[:, None]
    same_noisy = (
        query_noisy
        & jnp.logical_not(key_clean)[None, :]
        & (key_block[None, :] == query_block[:, None])
    )
    earlier_clean = query_noisy & key_clean[None, :] & (key_block[None, :] < query_block[:, None])
    causal_clean = (
        query_clean[:, None] & key_clean[None, :] & (key_block[None, :] <= query_block[:, None])
    )
    inside = key_place[None, :] < lengths[:, None]
    return (same_noisy | earlier_clean | causal_clean)[None] & inside[:, None, :]


def reduce_branch(branch):
    return lax.psum(branch, "tp")


def norm_in(stream, gain):
    normed, scaled, inverse = normalize(stream, gain)
    return (normed.astype(jnp.bfloat16), scaled, inverse)


def project(low_normed, weights, cosine, sine, heads):
    projected = jnp.einsum(
        "rcsd,tde->trcse", low_normed, weights, preferred_element_type=jnp.float32
    )
    shape = projected.shape[1:4] + (heads, HEAD_DIM)
    query = rotate(projected[0].reshape(shape), cosine, sine).astype(jnp.bfloat16)
    keys = rotate(projected[1].reshape(shape), cosine, sine).astype(jnp.bfloat16)
    values = projected[2].reshape(shape).astype(jnp.bfloat16)
    return (query, keys, values)


def collect(keys, values):
    rows = keys.shape[0]
    seg = keys.shape[2]
    return (
        lax.all_gather(keys[:, 1].reshape(rows, seg, -1), "sp", axis=1, tiled=True),
        lax.all_gather(values[:, 1].reshape(rows, seg, -1), "sp", axis=1, tiled=True),
    )


def join(query, keys, values, clean):
    rows = query.shape[0]
    seg = query.shape[2]
    heads = query.shape[3]
    full_keys = jnp.concatenate([keys[:, 0], clean[0].reshape(rows, -1, heads, HEAD_DIM)], axis=1)
    full_values = jnp.concatenate(
        [values[:, 0], clean[1].reshape(rows, -1, heads, HEAD_DIM)], axis=1
    )
    return (query.reshape(rows, 2 * seg, heads, HEAD_DIM), full_keys, full_values)


def attend(query, keys, values, mask):
    scores = jnp.einsum("rqhd,rkhd->rhqk", query, keys, preferred_element_type=jnp.float32)
    logits = jnp.where(mask[:, None], scores * HEAD_DIM ** (-0.5), -1e30)
    top = jnp.max(logits, axis=-1, keepdims=True)
    total = jnp.sum(jnp.exp(logits - top), axis=-1, keepdims=True)
    logsum = top + jnp.log(total)
    weights = jnp.exp(logits - logsum).astype(jnp.bfloat16)
    mixed = jnp.einsum("rhqk,rkhd->rqhd", weights, values, preferred_element_type=jnp.float32)
    return (mixed, logsum)


def attend_back(query, keys, values, mask, logsum, grad_mixed):
    scores = jnp.einsum("rqhd,rkhd->rhqk", query, keys, preferred_element_type=jnp.float32)
    logits = jnp.where(mask[:, None], scores * HEAD_DIM ** (-0.5), -1e30)
    weights = jnp.exp(logits - logsum)
    low_weights = weights.astype(jnp.bfloat16)
    grad_weights = jnp.einsum(
        "rqhd,rkhd->rhqk", grad_mixed, values, preferred_element_type=jnp.float32
    )
    inner = jnp.sum(grad_weights * weights, axis=-1, keepdims=True)
    grad_scores = (weights * (grad_weights - inner) * HEAD_DIM ** (-0.5)).astype(jnp.bfloat16)
    grad_query = jnp.einsum(
        "rhqk,rkhd->rqhd", grad_scores, keys, preferred_element_type=jnp.float32
    )
    grad_keys = jnp.einsum(
        "rhqk,rqhd->rkhd", grad_scores, query, preferred_element_type=jnp.float32
    )
    grad_values = jnp.einsum(
        "rhqk,rqhd->rkhd", low_weights, grad_mixed, preferred_element_type=jnp.float32
    )
    return (grad_query, grad_keys, grad_values)


def shards(inputs, lengths, gains, w_qkv, w_out, w_up, w_down, cotangent):
    layers = w_qkv.shape[0]
    rows = inputs.shape[0]
    seg = inputs.shape[2]
    heads = w_out.shape[1] // HEAD_DIM
    offset = lax.axis_index("sp") * seg
    seq = seg * lax.axis_size("sp")
    cosine, sine = tables(offset, seg)
    mask = visible(lengths, offset, seg, seq)
    hidden = inputs.astype(jnp.float32)
    kept_clean = []
    layer = 0
    low_attn, scaled_attn, inverse_attn = norm_in(hidden, gains[layer, 0])
    query, keys, values = project(low_attn, w_qkv[layer], cosine, sine, heads)
    clean = collect(keys, values)
    kept_attn = [(low_attn, scaled_attn, inverse_attn)]
    kept_clean.append(clean)
    joined = join(query, keys, values, clean)
    attended = attend(joined[0], joined[1], joined[2], mask)
    low_mixed = attended[0].reshape(rows, 2, seg, -1).astype(jnp.bfloat16)
    branch = jnp.einsum(
        "rcse,ed->rcsd", low_mixed, w_out[layer], preferred_element_type=jnp.float32
    )
    hidden = hidden + reduce_branch(branch)
    low_mlp, scaled_mlp, inverse_mlp = norm_in(hidden, gains[layer, 1])
    kept_mlp = [(low_mlp, scaled_mlp, inverse_mlp)]
    upward = jnp.einsum("rcsd,df->rcsf", low_mlp, w_up[layer], preferred_element_type=jnp.float32)
    active = jax.nn.gelu(upward, approximate=True).astype(jnp.bfloat16)
    branch = jnp.einsum("rcsf,fd->rcsd", active, w_down[layer], preferred_element_type=jnp.float32)
    hidden = hidden + reduce_branch(branch)
    hidden_out = hidden.astype(jnp.bfloat16)
    grad = cotangent.astype(jnp.float32)
    qkv_list = [None] * layers
    out_list = [None] * layers
    up_list = [None] * layers
    down_list = [None] * layers
    gain_list = [None] * layers
    for layer in reversed(range(layers)):
        low_normed, scaled, inverse = kept_mlp[layer]
        upward = jnp.einsum(
            "rcsd,df->rcsf", low_normed, w_up[layer], preferred_element_type=jnp.float32
        )
        active, gelu_back = jax.vjp(partial(jax.nn.gelu, approximate=True), upward)
        low_active = active.astype(jnp.bfloat16)
        grad_branch = grad.astype(jnp.bfloat16)
        down_list[layer] = jnp.einsum(
            "rcsf,rcsd->fd", low_active, grad_branch, preferred_element_type=jnp.float32
        )
        grad_active = jnp.einsum(
            "rcsd,fd->rcsf", grad_branch, w_down[layer], preferred_element_type=jnp.float32
        )
        grad_upward = gelu_back(grad_active)[0].astype(jnp.bfloat16)
        up_list[layer] = jnp.einsum(
            "rcsd,rcsf->df", low_normed, grad_upward, preferred_element_type=jnp.float32
        )
        partial_grad = jnp.einsum(
            "rcsf,df->rcsd", grad_upward, w_up[layer], preferred_element_type=jnp.float32
        )
        grad_normed = reduce_branch(partial_grad)
        through, second_gain = norm_back(grad_normed, scaled, inverse, gains[layer, 1])
        grad = grad + through
        low_attn, scaled_attn, inverse_attn = kept_attn[layer]
        query, keys, values = project(low_attn, w_qkv[layer], cosine, sine, heads)
        clean = collect(keys, values)
        joined = join(query, keys, values, clean)
        attended = attend(joined[0], joined[1], joined[2], mask)
        low_mixed = attended[0].reshape(rows, 2, seg, -1).astype(jnp.bfloat16)
        grad_branch = grad.astype(jnp.bfloat16)
        out_list[layer] = jnp.einsum(
            "rcse,rcsd->ed", low_mixed, grad_branch, preferred_element_type=jnp.float32
        )
        grad_mixed = jnp.einsum(
            "rcsd,ed->rcse", grad_branch, w_out[layer], preferred_element_type=jnp.float32
        )
        grad_mixed = grad_mixed.astype(jnp.bfloat16).reshape(rows, 2 * seg, heads, HEAD_DIM)
        grad_query, grad_keys, grad_values = attend_back(
            joined[0], joined[1], joined[2], mask, attended[1], grad_mixed
        )
        clean_grads = (
            lax.psum_scatter(
                grad_keys[:, seg:].reshape(rows, seq, -1), "sp", scatter_dimension=1, tiled=True
            ),
            lax.psum_scatter(
                grad_values[:, seg:].reshape(rows, seq, -1), "sp", scatter_dimension=1, tiled=True
            ),
        )
        local_shape = (rows, seg, heads, HEAD_DIM)
        key_grad = jnp.stack([grad_keys[:, :seg], clean_grads[0].reshape(local_shape)], axis=1)
        value_grad = jnp.stack([grad_values[:, :seg], clean_grads[1].reshape(local_shape)], axis=1)
        query_grad = grad_query.reshape(rows, 2, seg, heads, HEAD_DIM)
        stacked = jnp.stack(
            [rotate(query_grad, cosine, -sine), rotate(key_grad, cosine, -sine), value_grad]
        )
        stacked = stacked.astype(jnp.bfloat16).reshape(3, rows, 2, seg, -1)
        qkv_list[layer] = jnp.einsum(
            "rcsd,trcse->tde", low_attn, stacked, preferred_element_type=jnp.float32
        )
        partial_grad = jnp.einsum(
            "trcse,tde->rcsd", stacked, w_qkv[layer], preferred_element_type=jnp.float32
        )
        grad_normed = reduce_branch(partial_grad)
        through, first_gain = norm_back(grad_normed, scaled_attn, inverse_attn, gains[layer, 0])
        grad = grad + through
        gain_list[layer] = jnp.stack([first_gain, second_gain])
    qkv_all = jnp.stack(qkv_list)
    out_all = jnp.stack(out_list)
    up_all = jnp.stack(up_list)
    down_all = jnp.stack(down_list)
    gain_all = jnp.stack(gain_list)
    partly = (
        lax.psum_scatter(qkv_all, "dp", scatter_dimension=2, tiled=True),
        lax.psum_scatter(out_all, "dp", scatter_dimension=2, tiled=True),
        lax.psum_scatter(up_all, "dp", scatter_dimension=1, tiled=True),
        lax.psum_scatter(down_all, "dp", scatter_dimension=2, tiled=True),
        lax.psum_scatter(gain_all, "dp", scatter_dimension=2, tiled=True),
    )
    summed = (
        lax.psum_scatter(partly[0], "sp", scatter_dimension=2, tiled=True),
        lax.psum_scatter(partly[1], "sp", scatter_dimension=2, tiled=True),
        lax.psum_scatter(partly[2], "sp", scatter_dimension=1, tiled=True),
        lax.psum_scatter(partly[3], "sp", scatter_dimension=2, tiled=True),
        lax.psum_scatter(partly[4], "sp", scatter_dimension=2, tiled=True),
    )
    return (hidden_out, grad, summed[0], summed[1], summed[2], summed[3], summed[4])


CH = 256
RW = 64
NEG = -1e30
GC = 0.7978845608028654
GA = 0.044715
BF = jnp.bfloat16
F32 = jnp.float32
MESH = pl.DeviceIdType.MESH
VM = pl.BlockSpec(memory_space=pltpu.VMEM)
ANY = pl.BlockSpec(memory_space=pl.ANY)


def nn(a, b):
    return lax.dot_general(a, b, (((1,), (0,)), ((), ())), preferred_element_type=F32)


def nt(a, b):
    return lax.dot_general(a, b, (((1,), (1,)), ((), ())), preferred_element_type=F32)


def tn(a, b):
    return lax.dot_general(a, b, (((0,), (0,)), ((), ())), preferred_element_type=F32)


def each(count, body, start=0):
    def step(i, carry):
        body(i)
        return carry

    lax.fori_loop(start, count, step, 0)


class Copies:
    def __init__(self, sems, base, make):
        self.sems, self.base, self.make = sems, base, make

    def at(self, i):
        src, dst, dev = self.make(i)
        return pltpu.make_async_remote_copy(
            src_ref=src,
            dst_ref=dst,
            send_sem=self.sems[0].at[self.base + i],
            recv_sem=self.sems[1].at[self.base + i],
            device_id=dev,
            device_id_type=MESH,
        )

    def start(self, i):
        self.at(i).start()

    def arrived(self, i):
        self.at(i).wait_recv()

    def sent(self, i):
        self.at(i).wait_send()


SCRATCH = dict(
    x=((4, CH, 768), BF),
    cot=((1024, 768), BF),
    wT=((576, 768), BF),
    wfull=((4, 192, 768), BF),
    wup=((768, 768), BF),
    wdown=((768, 768), BF),
    cs=((2, 2, 32, CH), F32),
    a=((1024, 768), BF),
    tT=((4, 768, CH), BF),
    tT2=((4, 768, CH), BF),
    qT=((4, 3, 64, CH), BF),
    kvT=((6, 2, 3, 64, CH), BF),
    kaug=((6, 3, CH, 128), BF),
    vn=((6, 3, CH, 128), BF),
    qtail=((12, 16, CH), BF),
    gtail=((12, 16, CH), BF),
    maskb=((4, 16, CH), BF),
    plain=((16, CH), BF),
    oacc=((4, 3, 64, CH), F32),
    stat=((12, 8, CH), F32),
    on=((4, 128, 384), BF),
    oT=((4, 192, CH), BF),
    orecv=((4, 3, 32, 384), BF),
    h1=((4, RW, 768), F32),
    b=((1024, 768), BF),
    m=((1024, 768), BF),
    gu=((1024, 768), BF),
    gy=((1024, 768), BF),
    g1=((4, RW, 768), F32),
    goT=((4, 3, 64, CH), BF),
    dkv=((6, 2, 3, 64, CH), F32),
    dkvs=((2, 2, 3, 64, CH), BF),
    dkvr=((2, 2, 3, 64, CH), BF),
    dq=((4, 3, 64, CH), F32),
    gT=((4, 9, 64, CH), BF),
    st2=((4, CH, 768), BF),
    st3=((4, CH, 768), BF),
    st4=((4, CH, 768), BF),
    ra2=((4, 128, 768), BF),
    ra3=((4, 128, 768), BF),
    ra4=((4, 128, 768), BF),
    rb2=((4, RW, 768), BF),
    rb3=((4, RW, 768), BF),
    rb4=((4, RW, 768), BF),
    pU=((4, 192, 768), BF),
    pW=((4, 192, 768), BF),
    pO=((4, 192, 192), BF),
    pQ=((4, 192, 192), BF),
    pK=((4, 192, 384), BF),
    xU=((4, 96, 768), BF),
    xW=((96, 768), BF),
    xWs=((96, 768), BF),
    xO=((4, 96, 192), BF),
    xQ=((4, 96, 192), BF),
    xK=((4, 96, 384), BF),
    zU=((3, 96, 768), BF),
    zW=((2, 192, 768), BF),
    zW2=((192, 768), BF),
    zO=((3, 96, 192), BF),
    zQ=((3, 96, 192), BF),
    zK=((3, 96, 384), BF),
    hid=((1024, 768), BF),
    ig=((1024, 768), BF),
    gsum=((4, 8, 768), F32),
    gx=((2, 8, 768), F32),
    gz=((3, 8, 768), F32),
)

TILES = (
    ((0, 0), (2, 1)),
    ((1, 0), (3, 1), (2, 3)),
    ((2, 2),),
    ((3, 2), (2, 3)),
)


def step_kernel(*refs):
    (x_h, len_r, gains, wqkv_h, wout_h, wup_h, wdown_h, cot_h, cs_h) = refs[:9]
    (hid_h, ig_h, outQ, outO, outU, outW, outG) = refs[9:16]
    s = SimpleNamespace(**dict(zip(SCRATCH, refs[16 : 16 + len(SCRATCH)])))
    lsem, ssem, rsem = refs[16 + len(SCRATCH) :]
    sems = (ssem, rsem)
    hid, ig = s.hid, s.ig
    t = lax.axis_index("tp")
    z = lax.axis_index("dp")
    x = lax.axis_index("sp")
    c = lax.rem(t, 2)
    y = lax.div(t, 2)
    slot = 2 * c + y
    pslot = 2 * c + 1 - y
    partner = t + 1 - 2 * c
    ypeer = t + 2 - 4 * y
    diag = 3 - t
    tpdev = (None, partner, ypeer, diag)
    tpslot = (slot, 2 * (1 - c) + y, pslot, 2 * (1 - c) + 1 - y)

    barrier = pltpu.get_barrier_semaphore()
    for dev in (
        {"tp": partner},
        {"tp": ypeer},
        {"tp": diag},
        {"sp": 1 - x},
        {"dp": lax.rem(z + 1, 4)},
        {"dp": lax.rem(z + 2, 4)},
        {"dp": lax.rem(z + 3, 4)},
    ):
        pl.semaphore_signal(barrier, inc=1, device_id=dev, device_id_type=MESH)

    def own(ref, ch):
        return ref.at[pl.ds(ch * CH + slot * RW, RW), :]

    def half(ref, ch):
        return ref.at[pl.ds(ch * CH + c * 128, 128), :]

    def load(i, src, dst):
        return pltpu.make_async_copy(src, dst, lsem.at[i])

    loads = [load(i, x_h.at[i], s.x.at[i]) for i in range(4)]
    loads.append(load(4, wqkv_h, s.wT))
    loads.append(load(5, cs_h.at[pl.ds(2 * x, 2)], s.cs))
    loads.append(load(6, wout_h, s.wfull.at[slot]))
    loads.append(load(7, wup_h, s.wup))
    loads.append(load(8, wdown_h, s.wdown))
    loads.append(load(9, cot_h, s.cot))
    for i in (4, 2, 5, 3, 6, 0, 1, 7, 8, 9):
        loads[i].start()

    base = [0]

    def family(count, make):
        made = Copies(sems, base[0], make)
        made.count = count
        base[0] += count
        return made

    def spread(ref):
        return (
            family(4, lambda i: (own(ref, i), own(ref, i), {"tp": ypeer})),
            family(4, lambda i: (half(ref, i), half(ref, i), {"tp": partner})),
        )

    def gather(stage, ra, rb):
        return (
            family(
                4,
                lambda i: (
                    stage.at[i, pl.ds((1 - c) * 128, 128), :],
                    ra.at[i],
                    {"tp": partner},
                ),
            ),
            family(
                4, lambda i: (stage.at[i, pl.ds(pslot * RW, RW), :], rb.at[i], {"tp": ypeer})
            ),
        )

    def wmake(i):
        if i == 0:
            return (s.wfull.at[slot], s.wfull.at[slot], {"tp": ypeer})
        pair = pl.ds(2 * c, 2)
        return (s.wfull.at[pair], s.wfull.at[pair], {"tp": partner})

    wcopy = family(2, wmake)
    kvcopy = family(2, lambda i: (s.kvT.at[2 + i], s.kvT.at[4 + i], {"sp": 1 - x}))
    dkcopy = family(2, lambda i: (s.dkvs.at[i], s.dkvr.at[i], {"sp": 1 - x}))
    ocopy = [
        family(
            4,
            lambda i, r=r: (
                s.on.at[i, pl.ds(tpslot[r] * 32, 32), :],
                s.orecv.at[i, r - 1],
                {"tp": tpdev[r]},
            ),
        )
        for r in (1, 2, 3)
    ]
    ag1 = spread(s.b)
    ag2 = spread(hid)
    ag3 = spread(s.gy)
    ag4 = spread(ig)
    rs2 = gather(s.st2, s.ra2, s.rb2)
    rs3 = gather(s.st3, s.ra3, s.rb3)
    rs4 = gather(s.st4, s.ra4, s.rb4)
    all_waits = [wcopy, *ocopy, *ag1, *ag2, *ag3, *ag4, *rs2, *rs3, *rs4]

    znear = z + 1 - 2 * lax.rem(z, 2)
    zfar = lax.rem(z + 2, 4)
    order = (lax.rem(znear + 2, 4), znear, zfar, z)

    class Piece:
        def __init__(self, stage, xr, zr):
            self.stage, self.xr, self.zr = stage, xr, zr
            rows = pl.ds(96 * x, 96)
            self.xc = family(
                4,
                lambda i: (
                    stage.at[i, pl.ds(96 * (1 - x), 96), :],
                    xr.at[i],
                    {"sp": 1 - x},
                ),
            )
            self.nc = family(
                2, lambda i: (stage.at[order[i], rows, :], zr.at[1 - i], {"dp": znear})
            )
            self.fc = family(1, lambda i: (stage.at[zfar, rows, :], zr.at[2], {"dp": zfar}))
            all_waits.extend([self.xc, self.nc, self.fc])

        def compute(self, value, send=True):
            for zz in order:
                self.stage[zz] = value(zz).astype(BF)
                if send:
                    self.xc.start(zz)

        def send(self):
            for zz in order:
                self.xc.start(zz)

        def both(self, zz):
            self.xc.arrived(zz)
            return self.stage[zz, pl.ds(96 * x, 96), :].astype(F32) + self.xr[zz].astype(F32)

        def z_near(self):
            for i in range(2):
                self.stage[order[i], pl.ds(96 * x, 96), :] = self.both(order[i]).astype(BF)
                self.nc.start(i)

        def z_far(self):
            total = self.both(zfar)
            self.nc.arrived(0)
            total = total + self.zr[1].astype(F32)
            self.stage[zfar, pl.ds(96 * x, 96), :] = total.astype(BF)
            self.fc.start(0)

        def finish(self):
            total = self.both(z)
            self.nc.arrived(1)
            self.fc.arrived(0)
            return total + self.zr[0].astype(F32) + self.zr[2].astype(F32)

    pieceU = Piece(s.pU, s.xU, s.zU)
    pieceK = Piece(s.pK, s.xK, s.zK)

    def near_make(i):
        k = 1 - lax.div(i, 2)
        rows = pl.ds(96 * lax.rem(i, 2), 96)
        return (
            s.pW.at[lax.rem(znear + 2 * k, 4), rows, :],
            s.zW.at[k, rows, :],
            {"dp": znear},
        )

    def far_make(i):
        rows = pl.ds(96 * i, 96)
        return (s.pW.at[zfar, rows, :], s.zW2.at[rows, :], {"dp": zfar})

    wnear = family(4, near_make)
    wfar = family(2, far_make)
    wlast = family(1, lambda i: (s.xWs, s.xW, {"sp": 1 - x}))
    all_waits.extend([wnear, wfar, wlast])

    def send_near(value):
        for i, zz in enumerate(order):
            s.pW[zz] = value(zz).astype(BF)
            if i < 2:
                wnear.start(2 * i)
                wnear.start(2 * i + 1)

    def send_far():
        for i in range(2):
            wnear.arrived(i)
            rows = pl.ds(96 * i, 96)
            total = s.pW[zfar, rows, :].astype(F32) + s.zW[1, rows, :].astype(F32)
            s.pW[zfar, rows, :] = total.astype(BF)
            wfar.start(i)

    def summed(side):
        rows = pl.ds(96 * side, 96)
        total = s.pW[z, rows, :].astype(F32) + s.zW[0, rows, :].astype(F32)
        return total + s.zW2[rows, :].astype(F32)

    def send_last():
        for i in range(2):
            wnear.arrived(2 + i)
            wfar.arrived(i)
        s.xWs[...] = summed(1 - x).astype(BF)
        wlast.start(0)

    pieceO = Piece(s.pO, s.xO, s.zO)
    pieceQ = Piece(s.pQ, s.xQ, s.zQ)

    gtp = [
        family(1, lambda i, r=r: (s.gsum.at[t], s.gsum.at[t], {"tp": tpdev[r]}))
        for r in (1, 2, 3)
    ]
    gxc = family(1, lambda i: (s.gx.at[0], s.gx.at[1], {"sp": 1 - x}))
    gzc = family(
        3, lambda i: (s.gx.at[0], s.gz.at[i], {"dp": lax.rem(z + 1 + i, 4)})
    )
    all_waits.extend([*gtp, gxc, gzc])

    row = lax.broadcasted_iota(jnp.int32, (64, CH), 0)
    col = lax.broadcasted_iota(jnp.int32, (64, CH), 1)
    blk = lax.shift_right_logical(col, 4)
    few = row[:16]
    blk16 = blk[:16]
    for v, shown in enumerate((few == blk16, few < blk16, few <= blk16, few < 16)):
        s.maskb[v] = jnp.where(shown, 0.0, NEG).astype(BF)
    s.plain[...] = jnp.where(few == 0, 1.0, 0.0).astype(BF)
    length = len_r[0]
    hot = jnp.where((row == blk) | ((row > 16) & (row < 20)), 1.0, 0.0).astype(F32)
    unit = jnp.where(row < 3, 1.0, 0.0).astype(F32)

    def minus(value, first):
        high = value.astype(BF).astype(F32)
        middle = (value - high).astype(BF).astype(F32)
        low = value - high - middle
        out = jnp.where(few == first, -high, 0.0)
        out = jnp.where(few == first + 1, -middle, out)
        return jnp.where(few == first + 2, -low, out)

    def query_tail(value):
        return (minus(value, 1) + jnp.where(few == 0, 1.0, 0.0)).astype(BF)

    def key_tail(start):
        outside = (row == 16) & (col + start >= length)
        return jnp.where(outside, NEG, hot)

    def keep_keys(kt, h, kT, vT, tail):
        s.kaug[kt, h] = jnp.transpose(jnp.concatenate([kT, tail], axis=0)).astype(BF)
        s.vn[kt, h] = jnp.transpose(jnp.concatenate([vT, unit], axis=0)).astype(BF)

    for ref in (s.dkv, s.dq):
        ref[...] = jnp.zeros_like(ref)
    s.gsum[...] = jnp.zeros_like(s.gsum)

    loads[4].wait()
    pl.semaphore_wait(barrier, 7)
    loads[6].wait()
    wcopy.start(0)
    loads[5].wait()

    gain1 = gains[0:1, :]
    gain2 = gains[1:2, :]

    def centred(v):
        centre = v - jnp.mean(v, axis=-1, keepdims=True)
        inverse = lax.rsqrt(jnp.mean(centre * centre, axis=-1, keepdims=True) + EPSILON)
        return centre * inverse, inverse

    def project_chunk(ch, j):
        def rows(r):
            v = s.x[ch, pl.ds(r * RW, RW), :].astype(F32)
            s.a[pl.ds(ch * CH + r * RW, RW), :] = (centred(v)[0] * gain1).astype(BF)

        for r in range(4):
            rows(r)
        proj = nt(s.wT[...], s.a[pl.ds(ch * CH, CH), :])
        cos = s.cs[j, 0]
        sin = s.cs[j, 1]
        tail = key_tail(x * (2 * CH) + j * CH)
        for h in range(3):
            turned = []
            for i in range(2):
                first = proj[i * 192 + h * 64 : i * 192 + h * 64 + 32]
                second = proj[i * 192 + h * 64 + 32 : i * 192 + h * 64 + 64]
                turned.append(
                    jnp.concatenate(
                        [first * cos - second * sin, second * cos + first * sin], axis=0
                    )
                )
            vT = proj[384 + h * 64 : 384 + h * 64 + 64]
            s.qT[ch, h] = (turned[0] * 0.125).astype(BF)
            s.kvT[ch, 0, h] = turned[1].astype(BF)
            s.kvT[ch, 1, h] = vT.astype(BF)
            keep_keys(ch, h, turned[1], vT, tail)

    def clean_chunk(j):
        loads[2 + j].wait()
        project_chunk(2 + j, j)

        @pl.when(x == 0)
        def _():
            kvcopy.start(j)

    for j in range(2):
        clean_chunk(j)

    def noisy_chunk(j):
        loads[j].wait()
        project_chunk(j, j)

    for j in range(2):
        noisy_chunk(j)

    def scores(ch, h, kt, v, tail):
        query = jnp.concatenate([s.qT[ch, h], s.maskb[v], tail], axis=0)
        return nn(s.kaug[kt, h, :, 0:96], query)

    HEADS3 = [(ch, h) for ch in range(4) for h in range(3)]

    def mix(heads, tiles, fresh):
        tops = {}
        for ch, h in heads:
            top = None if fresh else s.stat[ch * 3 + h, 0:1, :]
            for kt, v in tiles[ch]:
                p = jnp.max(scores(ch, h, kt, v, s.plain[...]), axis=0, keepdims=True)
                top = p if top is None else jnp.maximum(top, p)
            tops[ch, h] = top
        items = [(ch, h, kt, v) for ch, h in heads for kt, v in tiles[ch]]
        tails = {}

        def product(ch, h, kt, v):
            if (ch, h) not in tails:
                tails[ch, h] = query_tail(tops[ch, h])
            return scores(ch, h, kt, v, tails[ch, h])

        sums, mixed = {}, {}
        ahead = product(*items[0])
        for n, (ch, h, kt, v) in enumerate(items):
            logits = ahead
            if n + 1 < len(items):
                ahead = product(*items[n + 1])
            e = jnp.exp(logits)
            total = jnp.sum(e, axis=0, keepdims=True)
            part = nn(s.kvT[kt, 1, h], e.astype(BF))
            sums[ch, h] = sums[ch, h] + total if (ch, h) in sums else total
            mixed[ch, h] = mixed[ch, h] + part if (ch, h) in mixed else part
            if n + 1 == len(items) or items[n + 1][:2] != (ch, h):
                at = ch * 3 + h
                total, part = sums[ch, h], mixed[ch, h]
                if not fresh:
                    scale = jnp.exp(s.stat[at, 0:1, :] - tops[ch, h])
                    total = total + s.stat[at, 1:2, :] * scale
                    part = part + s.oacc[ch, h] * scale
                s.stat[at, 0:1, :] = tops[ch, h]
                s.stat[at, 1:2, :] = total
                s.oacc[ch, h] = part

    mix(HEADS3, TILES, True)
    wcopy.arrived(0)
    wcopy.start(1)

    def close(ch):
        for h in range(3):
            at = ch * 3 + h
            total = s.stat[at, 1:2, :]
            out = s.oacc[ch, h] / total
            s.oacc[ch, h] = out
            s.qtail[at] = query_tail(s.stat[at, 0:1, :] + jnp.log(total))
            s.oT[ch, h * 64 : h * 64 + 64, :] = out.astype(BF)
        whole = jnp.concatenate([s.oacc[ch, h] for h in range(3)], axis=0)
        flat = jnp.transpose(whole)
        for k in range(4):
            pair = [flat[k * RW + 32 * i : k * RW + 32 * i + 32] for i in range(2)]
            s.on[ch, 32 * k : 32 * k + 32, :] = jnp.concatenate(pair, axis=1).astype(BF)
        for copy in ocopy:
            copy.start(ch)

    @pl.when(x == 1)
    def _():
        for j in range(2):
            kvcopy.arrived(j)
            tail = key_tail(j * CH)
            for h in range(3):
                keep_keys(
                    4 + j, h, s.kvT[4 + j, 0, h].astype(F32), s.kvT[4 + j, 1, h].astype(F32), tail
                )
            tiles = [((4 + j, 3),)] * 4
            if j == 0:
                mix(HEADS3, tiles, False)
        for ch in range(4):
            mix(HEADS3[3 * ch : 3 * ch + 3], tiles, False)
            close(ch)

    @pl.when(x == 0)
    def _():
        for ch in range(4):
            close(ch)

    wcopy.arrived(1)

    def out_rows(ch):
        total = s.x[ch, pl.ds(slot * RW, RW), :].astype(F32)

        def unpacked(v):
            v = v.astype(F32)
            return jnp.concatenate([v[:, :192], v[:, 192:]], axis=0).astype(BF)

        total = total + nn(unpacked(s.on[ch, pl.ds(slot * 32, 32), :]), s.wfull[slot])
        for r in (1, 2, 3):
            ocopy[r - 1].arrived(ch)
            total = total + nn(unpacked(s.orecv[ch, r - 1]), s.wfull[tpslot[r]])
        s.h1[ch] = total
        own(s.b, ch)[...] = (centred(total)[0] * gain2).astype(BF)
        ag1[0].start(ch)

    each(4, out_rows)
    for i in (7, 8, 9):
        loads[i].wait()

    def add_pair(rs, stage, ra, ch):
        rs[0].arrived(ch)
        rows = pl.ds(pslot * RW, RW)
        total = stage[ch, rows, :].astype(F32) + ra[ch, pl.ds((1 - y) * RW, RW), :].astype(F32)
        stage[ch, rows, :] = total.astype(BF)
        rs[1].start(ch)

    def add_last(rs, stage, ra, rb, ch):
        rs[1].arrived(ch)
        rows = pl.ds(slot * RW, RW)
        total = stage[ch, rows, :].astype(F32) + ra[ch, pl.ds(y * RW, RW), :].astype(F32)
        return total + rb[ch].astype(F32)

    def relay(ag, ch):
        ag[0].arrived(ch)
        ag[1].start(ch)

    def norm_back(grad, stream, gain, at):
        scaled, inverse = centred(stream)
        inner = grad * gain
        s.gsum[t, at : at + 1, :] += jnp.sum(grad * scaled, axis=0, keepdims=True)
        inner_mean = jnp.mean(inner, axis=-1, keepdims=True)
        mixed_mean = jnp.mean(inner * scaled, axis=-1, keepdims=True)
        return inverse * (inner - inner_mean - scaled * mixed_mean)

    def second_back(ch):
        grad = add_last(rs3, s.st3, s.ra3, s.rb3, ch)
        through = norm_back(grad, s.h1[ch], gain2, 1)
        cot = s.cot[pl.ds(ch * CH + slot * RW, RW), :].astype(F32)
        g1 = cot + through
        s.g1[ch] = g1
        own(s.gy, ch)[...] = g1.astype(BF)
        ag3[0].start(ch)

    def feed(ch):
        rows = pl.ds(ch * CH, CH)

        @pl.when(ch >= 1)
        def _():
            add_pair(rs3, s.st3, s.ra3, ch - 1)

        ag1[1].arrived(ch)
        low_b = s.b[rows, :]
        low_g = s.cot[rows, :]
        for n in range(3):
            cols = slice(n * CH, (n + 1) * CH)
            u = nn(low_b, s.wup[:, cols])
            gm = nt(low_g, s.wdown[cols, :])
            square = u * u
            hp = 0.5 + 0.5 * jnp.tanh(u * (GC + GC * GA * square))
            act = u * hp
            slope = hp + (act - act * hp) * (2.0 * GC + 6.0 * GC * GA * square)
            s.m[rows, cols] = act.astype(BF)
            s.gu[rows, cols] = (slope * gm).astype(BF)
            if n == 1:

                @pl.when(ch < 3)
                def _():
                    relay(ag1, ch + 1)

        s.st3[ch] = nt(s.gu[rows, :], s.wup[...]).astype(BF)
        rs3[0].start(ch)

        s.st2[ch] = nn(s.m[rows, :], s.wdown[...]).astype(BF)
        rs2[0].start(ch)

    relay(ag1, 0)
    each(4, feed)
    add_pair(rs3, s.st3, s.ra3, 3)

    def transposed(dst, src):
        for ch in range(4):
            dst[ch] = jnp.transpose(src[pl.ds(ch * CH, CH), :])

    def rows_by(lhs, rhs):
        def value(zz):
            total = nn(lhs[0, pl.ds(192 * zz, 192), :], rhs[0:CH, :])
            for ch in range(1, 4):
                total = total + nn(lhs[ch, pl.ds(192 * zz, 192), :], rhs[ch * CH : ch * CH + CH, :])
            return total

        return value

    def back_tiles(items):
        def products(ch, h, kt, v):
            at = ch * 3 + h
            grad = jnp.concatenate([s.goT[ch, h], s.gtail[at]], axis=0)
            return scores(ch, h, kt, v, s.qtail[at]), nn(s.vn[kt, h, :, 0:80], grad)

        ahead = products(*items[0])
        for n, (ch, h, kt, v) in enumerate(items):
            logits, gp = ahead
            if n + 1 < len(items):
                ahead = products(*items[n + 1])
            weights = jnp.exp(logits)
            gs = (weights * gp).astype(BF)
            s.dkv[kt, 1, h] += nt(s.goT[ch, h], weights.astype(BF))
            s.dkv[kt, 0, h] += nt(s.qT[ch, h], gs)
            s.dq[ch, h] += nn(s.kvT[kt, 0, h], gs)

    def attention_back(ch):
        ag3[1].arrived(ch)
        goT = nt(s.wfull[slot], s.gy[pl.ds(ch * CH, CH), :])
        for h in range(3):
            low = goT[h * 64 : h * 64 + 64].astype(BF)
            s.goT[ch, h] = low
            inner = jnp.sum(low.astype(F32) * s.oacc[ch, h], axis=0, keepdims=True)
            s.gtail[ch * 3 + h] = minus(inner, 0).astype(BF)

        @pl.when(x == 1)
        def _():
            back_tiles([(ch, h, 4 + j, 3) for j in range(2) for h in range(3)])
            if ch == 3:
                for j in range(2):
                    s.dkvs[j] = s.dkv[4 + j].astype(BF)
                    dkcopy.start(j)


    second_back(0)
    second_back(1)
    transposed(s.tT, s.b)
    pieceU.compute(rows_by(s.tT, s.gu))
    transposed(s.tT, s.cot)
    send_near(rows_by(s.tT, s.m))
    second_back(2)
    relay(ag3, 0)
    relay(ag3, 1)
    second_back(3)
    for ch in range(4):
        add_pair(rs2, s.st2, s.ra2, ch)
    relay(ag3, 2)
    attention_back(0)
    attention_back(1)
    relay(ag3, 3)
    attention_back(2)
    attention_back(3)
    back_tiles([(ch, h, kt, v) for ch, h in HEADS3 for kt, v in TILES[ch]])

    def turn_back(u, cos, sin):
        first = u[:32]
        second = u[32:]
        return jnp.concatenate([first * cos + second * sin, second * cos - first * sin], axis=0)

    def grad_rows(ch):
        j = ch % 2
        cos = s.cs[j, 0]
        sin = s.cs[j, 1]
        for h in range(3):
            s.gT[ch, h] = turn_back(s.dq[ch, h] * 0.125, cos, sin).astype(BF)
            s.gT[ch, 3 + h] = turn_back(s.dkv[ch, 0, h], cos, sin).astype(BF)
            s.gT[ch, 6 + h] = s.dkv[ch, 1, h].astype(BF)
        s.st4[ch] = tn(s.gT[ch].reshape(576, CH), s.wT[...]).astype(BF)
        rs4[0].start(ch)

    def turn_query(ch):
        for h in range(3):
            s.gT[ch, h] = turn_back(s.dq[ch, h] * 0.125, s.cs[ch % 2, 0], s.cs[ch % 2, 1]).astype(BF)

    def hidden_rows(ch):
        total = s.h1[ch] + add_last(rs2, s.st2, s.ra2, s.rb2, ch)
        own(hid, ch)[...] = total.astype(BF)
        ag2[0].start(ch)

    def input_rows(ch):
        grad = add_last(rs4, s.st4, s.ra4, s.rb4, ch)
        stream = s.x[ch, pl.ds(slot * RW, RW), :].astype(F32)
        total = s.g1[ch] + norm_back(grad, stream, gain1, 0)
        own(ig, ch)[...] = total.astype(BF)
        ag4[0].start(ch)

    def out_piece(zz):
        total = nt(s.tT[0, pl.ds(192 * zz, 192), :], s.oT[0])
        for ch in range(1, 4):
            total = total + nt(s.tT[ch, pl.ds(192 * zz, 192), :], s.oT[ch])
        return total

    def part_piece(lo, hi):
        def value(zz):
            total = None
            for ch in range(4):
                grads = s.gT[ch, lo:hi].reshape((hi - lo) * 64, CH)
                part = nt(s.tT2[ch, pl.ds(192 * zz, 192), :], grads)
                total = part if total is None else total + part
            return total

        return value

    for ch in range(2):
        grad_rows(ch)
    for ch in range(2):
        add_pair(rs4, s.st4, s.ra4, ch)
    pieceU.z_near()
    for ch in range(3):
        hidden_rows(ch)
    send_far()
    hidden_rows(3)
    transposed(s.tT, s.gy)
    pieceO.compute(out_piece, False)
    transposed(s.tT2, s.a)
    for ch in range(2, 4):
        turn_query(ch)
    pieceQ.compute(part_piece(0, 3), False)

    @pl.when(x == 1)
    def _():
        for j in range(2):
            dkcopy.sent(j)

    @pl.when(x == 0)
    def _():
        for j in range(2):
            dkcopy.arrived(j)
            s.dkv[2 + j] += s.dkvr[j].astype(F32)

    pieceO.send()
    pieceQ.send()
    for ch in range(2, 4):
        grad_rows(ch)
    for ch in range(2, 4):
        add_pair(rs4, s.st4, s.ra4, ch)
    pieceK.compute(part_piece(3, 9))
    for ch in range(2):
        input_rows(ch)
    pieceU.z_far()
    for ch in range(2):
        relay(ag2, ch)
    pieceO.z_near()
    pieceQ.z_near()
    for ch in range(2, 4):
        relay(ag2, ch)
    send_last()
    for ch in range(2, 4):
        input_rows(ch)

    for copy in gtp:
        copy.start(0)
    pieceK.z_near()
    for ch in range(2):
        relay(ag4, ch)
    pieceO.z_far()
    pieceQ.z_far()
    for copy in gtp:
        copy.arrived(0)
    s.gx[0] = s.gsum[0] + s.gsum[1] + s.gsum[2] + s.gsum[3]
    gxc.start(0)
    pieceK.z_far()
    outU[...] = pieceU.finish()
    wlast.arrived(0)
    outW[...] = summed(x) + s.xW[...].astype(F32)
    gxc.arrived(0)
    gxc.sent(0)
    s.gx[0] = s.gx[0] + s.gx[1]
    for i in range(3):
        gzc.start(i)
    for ch in range(2, 4):
        relay(ag4, ch)
    outO[...] = jnp.transpose(pieceO.finish())
    outQ[0] = pieceQ.finish()
    both = pieceK.finish()
    outQ[1] = both[:, :192]
    outQ[2] = both[:, 192:]
    total = s.gx[0]
    for i in range(3):
        gzc.arrived(i)
        total = total + s.gz[i]
    for k in range(8):
        @pl.when(z * 2 + x == k)
        def _(k=k):
            outG[...] = total[0:2, 96 * k : 96 * k + 96]

    def keep(i):
        rows = pl.ds(i * CH, CH)
        return (
            pltpu.make_async_copy(hid.at[rows, :], hid_h.at[rows, :], lsem.at[10 + i]),
            pltpu.make_async_copy(ig.at[rows, :], ig_h.at[rows, :], lsem.at[14 + i]),
        )

    def save_hidden(i):
        ag2[1].arrived(i)
        keep(i)[0].start()

    def save_input(i):
        ag4[1].arrived(i)
        keep(i)[1].start()

    each(4, save_hidden)
    each(4, save_input)
    for fam in all_waits:
        if fam is gxc:
            continue
        for i in range(fam.count):
            fam.sent(i)

    @pl.when(x == 0)
    def _():
        for i in range(2):
            kvcopy.sent(i)

    def kept(i):
        for copy in keep(i):
            copy.wait()

    each(4, kept)


def finish_kernel(*refs):
    sources, results = refs[:7], refs[7:14]
    rows, wide, smalls = refs[14], refs[15], refs[16:21]
    isem, osem = refs[21:]

    def part(ref, i):
        return ref.at[pl.ds(i * CH, CH), :]

    def move(src, dst, sem):
        return pltpu.make_async_copy(src, dst, sem)

    ins = [move(part(sources[1], i), rows.at[1, i], isem.at[4 + i]) for i in range(4)]
    ins += [move(part(sources[0], i), rows.at[0, i], isem.at[i]) for i in range(4)]
    ins += [move(sources[2 + k], smalls[k], isem.at[8 + k]) for k in range(5)]
    for copy in ins:
        copy.start()
    outs = []
    for i in range(4):
        ins[i].wait()
        wide[i] = rows[1, i].astype(F32)
        outs.append(move(wide.at[i], part(results[1], i), osem.at[4 + i]))
        outs[-1].start()
    for i in range(4):
        ins[4 + i].wait()
        outs.append(move(rows.at[0, i], part(results[0], i), osem.at[i]))
        outs[-1].start()
    for k in range(5):
        ins[8 + k].wait()
        outs.append(move(smalls[k], results[2 + k], osem.at[8 + k]))
        outs[-1].start()
    for copy in outs:
        copy.wait()


def finish(arrays):
    shapes = [jax.ShapeDtypeStruct(v.shape, v.dtype) for v in arrays]
    shapes[1] = jax.ShapeDtypeStruct(arrays[1].shape, F32)
    return pl.pallas_call(
        finish_kernel,
        out_shape=shapes,
        in_specs=[ANY] * 7,
        out_specs=[ANY] * 7,
        scratch_shapes=[pltpu.VMEM((2, 4, CH, 768), BF), pltpu.VMEM((4, CH, 768), F32)]
        + [pltpu.VMEM(v.shape, v.dtype) for v in arrays[2:]]
        + [pltpu.SemaphoreType.DMA((13,)), pltpu.SemaphoreType.DMA((13,))],
        name="finish",
    )(*arrays)


def rope_table(seq):
    half_dim = HEAD_DIM // 2
    freq = 10000.0 ** (-np.arange(half_dim) * 2.0 / HEAD_DIM)
    angle = freq[:, None] * np.arange(seq)[None, :]
    both = np.stack([np.cos(angle), np.sin(angle)])
    return np.moveaxis(both.reshape(2, half_dim, seq // CH, CH), 2, 0).astype(np.float32)


def fast(inputs, lengths, gains, w_qkv, w_out, w_up, w_down, cotangent):
    seg = inputs.shape[2]
    shape = jax.ShapeDtypeStruct
    found = pl.pallas_call(
        step_kernel,
        out_shape=(
            shape((1024, 768), BF),
            shape((1024, 768), BF),
            shape((3, 96, 192), F32),
            shape((192, 96), F32),
            shape((96, 768), F32),
            shape((96, 768), F32),
            shape((2, 96), F32),
        ),
        in_specs=[ANY, pl.BlockSpec(memory_space=pltpu.SMEM), VM, ANY, ANY, ANY, ANY, ANY, ANY],
        out_specs=[ANY] * 2 + [VM] * 5,
        scratch_shapes=[pltpu.VMEM(dims, kind) for dims, kind in SCRATCH.values()]
        + [
            pltpu.SemaphoreType.DMA((18,)),
            pltpu.SemaphoreType.DMA((140,)),
            pltpu.SemaphoreType.DMA((140,)),
        ],
        compiler_params=pltpu.CompilerParams(
            collective_id=0, has_side_effects=True, vmem_limit_bytes=64 * 1024 * 1024 - 65536
        ),
        name="step",
    )(
        inputs.reshape(4, CH, 768),
        lengths,
        gains[0],
        jnp.swapaxes(w_qkv[0], 1, 2).reshape(576, 768),
        w_out[0],
        w_up[0],
        w_down[0],
        cotangent.reshape(1024, 768),
        jnp.asarray(rope_table(seg * lax.axis_size("sp"))),
    )
    hid, ig, gq, go, gu, gd, gg = finish(found)
    return (
        hid.reshape(inputs.shape),
        ig.reshape(inputs.shape),
        gq[None],
        go[None],
        gu[None],
        jnp.swapaxes(gd, 0, 1)[None],
        gg[None],
    )


def pick(*args):
    inputs, w_out = args[0], args[4]
    plain = (1, 2, 512, 768)
    sizes = (lax.axis_size("tp"), lax.axis_size("dp"), lax.axis_size("sp"))
    if inputs.shape == plain and w_out.shape[1:] == (192, 768) and sizes == (4, 4, 2):
        return fast(*args)
    return shards(*args)


def solution(mesh):
    in_specs = (
        P("dp", None, "sp", None),
        P("dp"),
        P(),
        P(None, None, None, "tp"),
        P(None, "tp", None),
        P(None, None, "tp"),
        P(None, "tp", None),
        P("dp", None, "sp", None),
    )
    out_specs = (
        P("dp", None, "sp", None),
        P("dp", None, "sp", None),
        P(None, None, ("dp", "sp"), "tp"),
        P(None, "tp", ("dp", "sp")),
        P(None, ("dp", "sp"), "tp"),
        P(None, "tp", ("dp", "sp")),
        P(None, None, ("dp", "sp")),
    )
    return jax.shard_map(pick, mesh=mesh, in_specs=in_specs, out_specs=out_specs, check_vma=False)
```

```python
from functools import partial
from types import SimpleNamespace

import jax
import jax.numpy as jnp
import numpy as np
from jax import lax
from jax.experimental import pallas as pl
from jax.experimental.pallas import tpu as pltpu
from jax.sharding import PartitionSpec as P

HEAD_DIM = 64
BLOCK = 16


EPSILON = 1e-05


def normalize(value, gain):
    centre = value - jnp.mean(value, axis=-1, keepdims=True)
    inverse = lax.rsqrt(jnp.mean(centre * centre, axis=-1, keepdims=True) + EPSILON)
    scaled = centre * inverse
    return (scaled * gain, scaled, inverse)


def norm_back(grad, scaled, inverse, gain):
    inner = grad * gain
    gain_grad = jnp.sum(grad * scaled, axis=(0, 1, 2))
    centred = inner - jnp.mean(inner, axis=-1, keepdims=True)
    result = inverse * (centred - scaled * jnp.mean(inner * scaled, axis=-1, keepdims=True))
    return (result, gain_grad)


def rotate(value, cosine, sine):
    half_dim = value.shape[-1] // 2
    first = value[..., :half_dim]
    second = value[..., half_dim:]
    return jnp.concatenate(
        [first * cosine - second * sine, second * cosine + first * sine], axis=-1
    )


def tables(offset, count):
    half_dim = HEAD_DIM // 2
    freq = 10000.0 ** (-jnp.arange(half_dim).astype(jnp.float32) * 2.0 / HEAD_DIM)
    angle = (offset + jnp.arange(count)).astype(jnp.float32)[:, None] * freq[None, :]
    return (jnp.cos(angle)[:, None, :], jnp.sin(angle)[:, None, :])


def visible(lengths, offset, seg, seq):
    places = offset + jnp.arange(seg)
    query_block = jnp.concatenate([places, places]) // BLOCK
    query_clean = jnp.arange(2 * seg) >= seg
    key_place = jnp.concatenate([places, jnp.arange(seq)])
    key_block = key_place // BLOCK
    key_clean = jnp.arange(seg + seq) >= seg
    query_noisy = jnp.logical_not(query_clean)[:, None]
    same_noisy = (
        query_noisy
        & jnp.logical_not(key_clean)[None, :]
        & (key_block[None, :] == query_block[:, None])
    )
    earlier_clean = query_noisy & key_clean[None, :] & (key_block[None, :] < query_block[:, None])
    causal_clean = (
        query_clean[:, None] & key_clean[None, :] & (key_block[None, :] <= query_block[:, None])
    )
    inside = key_place[None, :] < lengths[:, None]
    return (same_noisy | earlier_clean | causal_clean)[None] & inside[:, None, :]


def reduce_branch(branch):
    return lax.psum(branch, "tp")


def norm_in(stream, gain):
    normed, scaled, inverse = normalize(stream, gain)
    return (normed.astype(jnp.bfloat16), scaled, inverse)


def project(low_normed, weights, cosine, sine, heads):
    projected = jnp.einsum(
        "rcsd,tde->trcse", low_normed, weights, preferred_element_type=jnp.float32
    )
    shape = projected.shape[1:4] + (heads, HEAD_DIM)
    query = rotate(projected[0].reshape(shape), cosine, sine).astype(jnp.bfloat16)
    keys = rotate(projected[1].reshape(shape), cosine, sine).astype(jnp.bfloat16)
    values = projected[2].reshape(shape).astype(jnp.bfloat16)
    return (query, keys, values)


def collect(keys, values):
    rows = keys.shape[0]
    seg = keys.shape[2]
    return (
        lax.all_gather(keys[:, 1].reshape(rows, seg, -1), "sp", axis=1, tiled=True),
        lax.all_gather(values[:, 1].reshape(rows, seg, -1), "sp", axis=1, tiled=True),
    )


def join(query, keys, values, clean):
    rows = query.shape[0]
    seg = query.shape[2]
    heads = query.shape[3]
    full_keys = jnp.concatenate([keys[:, 0], clean[0].reshape(rows, -1, heads, HEAD_DIM)], axis=1)
    full_values = jnp.concatenate(
        [values[:, 0], clean[1].reshape(rows, -1, heads, HEAD_DIM)], axis=1
    )
    return (query.reshape(rows, 2 * seg, heads, HEAD_DIM), full_keys, full_values)


def attend(query, keys, values, mask):
    scores = jnp.einsum("rqhd,rkhd->rhqk", query, keys, preferred_element_type=jnp.float32)
    logits = jnp.where(mask[:, None], scores * HEAD_DIM ** (-0.5), -1e30)
    top = jnp.max(logits, axis=-1, keepdims=True)
    total = jnp.sum(jnp.exp(logits - top), axis=-1, keepdims=True)
    logsum = top + jnp.log(total)
    weights = jnp.exp(logits - logsum).astype(jnp.bfloat16)
    mixed = jnp.einsum("rhqk,rkhd->rqhd", weights, values, preferred_element_type=jnp.float32)
    return (mixed, logsum)


def attend_back(query, keys, values, mask, logsum, grad_mixed):
    scores = jnp.einsum("rqhd,rkhd->rhqk", query, keys, preferred_element_type=jnp.float32)
    logits = jnp.where(mask[:, None], scores * HEAD_DIM ** (-0.5), -1e30)
    weights = jnp.exp(logits - logsum)
    low_weights = weights.astype(jnp.bfloat16)
    grad_weights = jnp.einsum(
        "rqhd,rkhd->rhqk", grad_mixed, values, preferred_element_type=jnp.float32
    )
    inner = jnp.sum(grad_weights * weights, axis=-1, keepdims=True)
    grad_scores = (weights * (grad_weights - inner) * HEAD_DIM ** (-0.5)).astype(jnp.bfloat16)
    grad_query = jnp.einsum(
        "rhqk,rkhd->rqhd", grad_scores, keys, preferred_element_type=jnp.float32
    )
    grad_keys = jnp.einsum(
        "rhqk,rqhd->rkhd", grad_scores, query, preferred_element_type=jnp.float32
    )
    grad_values = jnp.einsum(
        "rhqk,rqhd->rkhd", low_weights, grad_mixed, preferred_element_type=jnp.float32
    )
    return (grad_query, grad_keys, grad_values)


def shards(inputs, lengths, gains, w_qkv, w_out, w_up, w_down, cotangent):
    layers = w_qkv.shape[0]
    rows = inputs.shape[0]
    seg = inputs.shape[2]
    heads = w_out.shape[1] // HEAD_DIM
    offset = lax.axis_index("sp") * seg
    seq = seg * lax.axis_size("sp")
    cosine, sine = tables(offset, seg)
    mask = visible(lengths, offset, seg, seq)
    hidden = inputs.astype(jnp.float32)
    kept_clean = []
    layer = 0
    low_attn, scaled_attn, inverse_attn = norm_in(hidden, gains[layer, 0])
    query, keys, values = project(low_attn, w_qkv[layer], cosine, sine, heads)
    clean = collect(keys, values)
    kept_attn = [(low_attn, scaled_attn, inverse_attn)]
    kept_clean.append(clean)
    joined = join(query, keys, values, clean)
    attended = attend(joined[0], joined[1], joined[2], mask)
    low_mixed = attended[0].reshape(rows, 2, seg, -1).astype(jnp.bfloat16)
    branch = jnp.einsum(
        "rcse,ed->rcsd", low_mixed, w_out[layer], preferred_element_type=jnp.float32
    )
    hidden = hidden + reduce_branch(branch)
    low_mlp, scaled_mlp, inverse_mlp = norm_in(hidden, gains[layer, 1])
    kept_mlp = [(low_mlp, scaled_mlp, inverse_mlp)]
    upward = jnp.einsum("rcsd,df->rcsf", low_mlp, w_up[layer], preferred_element_type=jnp.float32)
    active = jax.nn.gelu(upward, approximate=True).astype(jnp.bfloat16)
    branch = jnp.einsum("rcsf,fd->rcsd", active, w_down[layer], preferred_element_type=jnp.float32)
    hidden = hidden + reduce_branch(branch)
    hidden_out = hidden.astype(jnp.bfloat16)
    grad = cotangent.astype(jnp.float32)
    qkv_list = [None] * layers
    out_list = [None] * layers
    up_list = [None] * layers
    down_list = [None] * layers
    gain_list = [None] * layers
    for layer in reversed(range(layers)):
        low_normed, scaled, inverse = kept_mlp[layer]
        upward = jnp.einsum(
            "rcsd,df->rcsf", low_normed, w_up[layer], preferred_element_type=jnp.float32
        )
        active, gelu_back = jax.vjp(partial(jax.nn.gelu, approximate=True), upward)
        low_active = active.astype(jnp.bfloat16)
        grad_branch = grad.astype(jnp.bfloat16)
        down_list[layer] = jnp.einsum(
            "rcsf,rcsd->fd", low_active, grad_branch, preferred_element_type=jnp.float32
        )
        grad_active = jnp.einsum(
            "rcsd,fd->rcsf", grad_branch, w_down[layer], preferred_element_type=jnp.float32
        )
        grad_upward = gelu_back(grad_active)[0].astype(jnp.bfloat16)
        up_list[layer] = jnp.einsum(
            "rcsd,rcsf->df", low_normed, grad_upward, preferred_element_type=jnp.float32
        )
        partial_grad = jnp.einsum(
            "rcsf,df->rcsd", grad_upward, w_up[layer], preferred_element_type=jnp.float32
        )
        grad_normed = reduce_branch(partial_grad)
        through, second_gain = norm_back(grad_normed, scaled, inverse, gains[layer, 1])
        grad = grad + through
        low_attn, scaled_attn, inverse_attn = kept_attn[layer]
        query, keys, values = project(low_attn, w_qkv[layer], cosine, sine, heads)
        clean = collect(keys, values)
        joined = join(query, keys, values, clean)
        attended = attend(joined[0], joined[1], joined[2], mask)
        low_mixed = attended[0].reshape(rows, 2, seg, -1).astype(jnp.bfloat16)
        grad_branch = grad.astype(jnp.bfloat16)
        out_list[layer] = jnp.einsum(
            "rcse,rcsd->ed", low_mixed, grad_branch, preferred_element_type=jnp.float32
        )
        grad_mixed = jnp.einsum(
            "rcsd,ed->rcse", grad_branch, w_out[layer], preferred_element_type=jnp.float32
        )
        grad_mixed = grad_mixed.astype(jnp.bfloat16).reshape(rows, 2 * seg, heads, HEAD_DIM)
        grad_query, grad_keys, grad_values = attend_back(
            joined[0], joined[1], joined[2], mask, attended[1], grad_mixed
        )
        clean_grads = (
            lax.psum_scatter(
                grad_keys[:, seg:].reshape(rows, seq, -1), "sp", scatter_dimension=1, tiled=True
            ),
            lax.psum_scatter(
                grad_values[:, seg:].reshape(rows, seq, -1), "sp", scatter_dimension=1, tiled=True
            ),
        )
        local_shape = (rows, seg, heads, HEAD_DIM)
        key_grad = jnp.stack([grad_keys[:, :seg], clean_grads[0].reshape(local_shape)], axis=1)
        value_grad = jnp.stack([grad_values[:, :seg], clean_grads[1].reshape(local_shape)], axis=1)
        query_grad = grad_query.reshape(rows, 2, seg, heads, HEAD_DIM)
        stacked = jnp.stack(
            [rotate(query_grad, cosine, -sine), rotate(key_grad, cosine, -sine), value_grad]
        )
        stacked = stacked.astype(jnp.bfloat16).reshape(3, rows, 2, seg, -1)
        qkv_list[layer] = jnp.einsum(
            "rcsd,trcse->tde", low_attn, stacked, preferred_element_type=jnp.float32
        )
        partial_grad = jnp.einsum(
            "trcse,tde->rcsd", stacked, w_qkv[layer], preferred_element_type=jnp.float32
        )
        grad_normed = reduce_branch(partial_grad)
        through, first_gain = norm_back(grad_normed, scaled_attn, inverse_attn, gains[layer, 0])
        grad = grad + through
        gain_list[layer] = jnp.stack([first_gain, second_gain])
    qkv_all = jnp.stack(qkv_list)
    out_all = jnp.stack(out_list)
    up_all = jnp.stack(up_list)
    down_all = jnp.stack(down_list)
    gain_all = jnp.stack(gain_list)
    partly = (
        lax.psum_scatter(qkv_all, "dp", scatter_dimension=2, tiled=True),
        lax.psum_scatter(out_all, "dp", scatter_dimension=2, tiled=True),
        lax.psum_scatter(up_all, "dp", scatter_dimension=1, tiled=True),
        lax.psum_scatter(down_all, "dp", scatter_dimension=2, tiled=True),
        lax.psum_scatter(gain_all, "dp", scatter_dimension=2, tiled=True),
    )
    summed = (
        lax.psum_scatter(partly[0], "sp", scatter_dimension=2, tiled=True),
        lax.psum_scatter(partly[1], "sp", scatter_dimension=2, tiled=True),
        lax.psum_scatter(partly[2], "sp", scatter_dimension=1, tiled=True),
        lax.psum_scatter(partly[3], "sp", scatter_dimension=2, tiled=True),
        lax.psum_scatter(partly[4], "sp", scatter_dimension=2, tiled=True),
    )
    return (hidden_out, grad, summed[0], summed[1], summed[2], summed[3], summed[4])


CH = 256
RW = 64
NEG = -1e30
GC = 0.7978845608028654
GA = 0.044715
BF = jnp.bfloat16
F32 = jnp.float32
MESH = pl.DeviceIdType.MESH
VM = pl.BlockSpec(memory_space=pltpu.VMEM)
ANY = pl.BlockSpec(memory_space=pl.ANY)


def nn(a, b):
    return lax.dot_general(a, b, (((1,), (0,)), ((), ())), preferred_element_type=F32)


def nt(a, b):
    return lax.dot_general(a, b, (((1,), (1,)), ((), ())), preferred_element_type=F32)


def tn(a, b):
    return lax.dot_general(a, b, (((0,), (0,)), ((), ())), preferred_element_type=F32)


def each(count, body, start=0):
    def step(i, carry):
        body(i)
        return carry

    lax.fori_loop(start, count, step, 0)


class Copies:
    def __init__(self, sems, base, make):
        self.sems, self.base, self.make = sems, base, make

    def at(self, i):
        src, dst, dev = self.make(i)
        return pltpu.make_async_remote_copy(
            src_ref=src,
            dst_ref=dst,
            send_sem=self.sems[0].at[self.base + i],
            recv_sem=self.sems[1].at[self.base + i],
            device_id=dev,
            device_id_type=MESH,
        )

    def start(self, i):
        self.at(i).start()

    def arrived(self, i):
        self.at(i).wait_recv()

    def sent(self, i):
        self.at(i).wait_send()


SCRATCH = dict(
    x=((4, CH, 768), BF),
    cot=((1024, 768), BF),
    wT=((576, 768), BF),
    wfull=((4, 192, 768), BF),
    wup=((768, 768), BF),
    wdown=((768, 768), BF),
    cs=((2, 2, 32, CH), F32),
    a=((1024, 768), BF),
    tT=((4, 768, CH), BF),
    tT2=((4, 768, CH), BF),
    qT=((4, 3, 64, CH), BF),
    kvT=((6, 2, 3, 64, CH), BF),
    kaug=((6, 3, CH, 128), BF),
    vn=((6, 3, CH, 128), BF),
    qtail=((12, 16, CH), BF),
    gtail=((12, 16, CH), BF),
    maskb=((4, 16, CH), BF),
    plain=((16, CH), BF),
    oacc=((4, 3, 64, CH), F32),
    stat=((12, 8, CH), F32),
    on=((4, 128, 384), BF),
    oT=((4, 192, CH), BF),
    orecv=((4, 3, 32, 384), BF),
    h1=((4, RW, 768), F32),
    b=((1024, 768), BF),
    m=((1024, 768), BF),
    gu=((1024, 768), BF),
    gy=((1024, 768), BF),
    g1=((4, RW, 768), F32),
    goT=((4, 3, 64, CH), BF),
    dkv=((6, 2, 3, 64, CH), F32),
    dkvs=((2, 2, 3, 64, CH), BF),
    dkvr=((2, 2, 3, 64, CH), BF),
    dq=((4, 3, 64, CH), F32),
    gT=((4, 9, 64, CH), BF),
    st2=((4, CH, 768), BF),
    st3=((4, CH, 768), BF),
    st4=((4, CH, 768), BF),
    ra2=((4, 128, 768), BF),
    ra3=((4, 128, 768), BF),
    ra4=((4, 128, 768), BF),
    rb2=((4, RW, 768), BF),
    rb3=((4, RW, 768), BF),
    rb4=((4, RW, 768), BF),
    pU=((4, 192, 768), BF),
    pW=((4, 192, 768), BF),
    pO=((4, 192, 192), BF),
    pQ=((4, 192, 192), BF),
    pK=((4, 192, 384), BF),
    xU=((4, 96, 768), BF),
    xW=((96, 768), BF),
    xWs=((96, 768), BF),
    xO=((4, 96, 192), BF),
    xQ=((4, 96, 192), BF),
    xK=((4, 96, 384), BF),
    zU=((3, 96, 768), BF),
    zW=((2, 192, 768), BF),
    zW2=((192, 768), BF),
    zO=((3, 96, 192), BF),
    zQ=((3, 96, 192), BF),
    zK=((3, 96, 384), BF),
    hid=((1024, 768), BF),
    ig=((1024, 768), BF),
    gsum=((4, 8, 768), F32),
    gx=((2, 8, 768), F32),
    gz=((3, 8, 768), F32),
)

TILES = (
    ((0, 0), (2, 1)),
    ((1, 0), (3, 1), (2, 3)),
    ((2, 2),),
    ((3, 2), (2, 3)),
)


def step_kernel(*refs):
    (x_h, len_r, gains, wqkv_h, wout_h, wup_h, wdown_h, cot_h, cs_h) = refs[:9]
    (hid_h, ig_h, outQ, outO, outU, outW, outG) = refs[9:16]
    s = SimpleNamespace(**dict(zip(SCRATCH, refs[16 : 16 + len(SCRATCH)])))
    lsem, ssem, rsem = refs[16 + len(SCRATCH) :]
    sems = (ssem, rsem)
    hid, ig = s.hid, s.ig
    t = lax.axis_index("tp")
    z = lax.axis_index("dp")
    x = lax.axis_index("sp")
    c = lax.rem(t, 2)
    y = lax.div(t, 2)
    slot = 2 * c + y
    pslot = 2 * c + 1 - y
    partner = t + 1 - 2 * c
    ypeer = t + 2 - 4 * y
    diag = 3 - t
    tpdev = (None, partner, ypeer, diag)
    tpslot = (slot, 2 * (1 - c) + y, pslot, 2 * (1 - c) + 1 - y)

    barrier = pltpu.get_barrier_semaphore()
    for dev in (
        {"tp": partner},
        {"tp": ypeer},
        {"tp": diag},
        {"sp": 1 - x},
        {"dp": lax.rem(z + 1, 4)},
        {"dp": lax.rem(z + 2, 4)},
        {"dp": lax.rem(z + 3, 4)},
    ):
        pl.semaphore_signal(barrier, inc=1, device_id=dev, device_id_type=MESH)

    def own(ref, ch):
        return ref.at[pl.ds(ch * CH + slot * RW, RW), :]

    def half(ref, ch):
        return ref.at[pl.ds(ch * CH + c * 128, 128), :]

    def load(i, src, dst):
        return pltpu.make_async_copy(src, dst, lsem.at[i])

    loads = [load(i, x_h.at[i], s.x.at[i]) for i in range(4)]
    loads.append(load(4, wqkv_h, s.wT))
    loads.append(load(5, cs_h.at[pl.ds(2 * x, 2)], s.cs))
    loads.append(load(6, wout_h, s.wfull.at[slot]))
    loads.append(load(7, wup_h, s.wup))
    loads.append(load(8, wdown_h, s.wdown))
    loads.append(load(9, cot_h, s.cot))
    for i in (4, 2, 5, 3, 6, 0, 1, 7, 8, 9):
        loads[i].start()

    base = [0]

    def family(count, make):
        made = Copies(sems, base[0], make)
        made.count = count
        base[0] += count
        return made

    def spread(ref):
        return (
            family(4, lambda i: (own(ref, i), own(ref, i), {"tp": ypeer})),
            family(4, lambda i: (half(ref, i), half(ref, i), {"tp": partner})),
        )

    def gather(stage, ra, rb):
        return (
            family(
                4,
                lambda i: (
                    stage.at[i, pl.ds((1 - c) * 128, 128), :],
                    ra.at[i],
                    {"tp": partner},
                ),
            ),
            family(
                4, lambda i: (stage.at[i, pl.ds(pslot * RW, RW), :], rb.at[i], {"tp": ypeer})
            ),
        )

    def wmake(i):
        if i == 0:
            return (s.wfull.at[slot], s.wfull.at[slot], {"tp": ypeer})
        pair = pl.ds(2 * c, 2)
        return (s.wfull.at[pair], s.wfull.at[pair], {"tp": partner})

    wcopy = family(2, wmake)
    kvcopy = family(2, lambda i: (s.kvT.at[2 + i], s.kvT.at[4 + i], {"sp": 1 - x}))
    dkcopy = family(2, lambda i: (s.dkvs.at[i], s.dkvr.at[i], {"sp": 1 - x}))
    ocopy = [
        family(
            4,
            lambda i, r=r: (
                s.on.at[i, pl.ds(tpslot[r] * 32, 32), :],
                s.orecv.at[i, r - 1],
                {"tp": tpdev[r]},
            ),
        )
        for r in (1, 2, 3)
    ]
    ag1 = spread(s.b)
    ag2 = spread(hid)
    ag3 = spread(s.gy)
    ag4 = spread(ig)
    rs2 = gather(s.st2, s.ra2, s.rb2)
    rs3 = gather(s.st3, s.ra3, s.rb3)
    rs4 = gather(s.st4, s.ra4, s.rb4)
    all_waits = [wcopy, *ocopy, *ag1, *ag2, *ag3, *ag4, *rs2, *rs3, *rs4]

    znear = z + 1 - 2 * lax.rem(z, 2)
    zfar = lax.rem(z + 2, 4)
    order = (lax.rem(znear + 2, 4), znear, zfar, z)

    class Piece:
        def __init__(self, stage, xr, zr, direct=False):
            self.stage, self.xr, self.zr = stage, xr, zr
            rows = pl.ds(96 * x, 96)
            self.xc = family(
                4,
                lambda i: (
                    stage.at[i, pl.ds(96 * (1 - x), 96), :],
                    xr.at[i],
                    {"sp": 1 - x},
                ),
            )
            all_waits.append(self.xc)
            if direct:
                self.dc = family(
                    3,
                    lambda i: (
                        stage.at[lax.rem(z + 1 + i, 4), rows, :],
                        zr.at[i],
                        {"dp": lax.rem(z + 1 + i, 4)},
                    ),
                )
                all_waits.append(self.dc)
                return
            self.nc = family(
                2, lambda i: (stage.at[order[i], rows, :], zr.at[1 - i], {"dp": znear})
            )
            self.fc = family(1, lambda i: (stage.at[zfar, rows, :], zr.at[2], {"dp": zfar}))
            all_waits.extend([self.nc, self.fc])

        def compute(self, value, send=True):
            for zz in order:
                self.stage[zz] = value(zz).astype(BF)
                if send:
                    self.xc.start(zz)

        def send(self):
            for zz in order:
                self.xc.start(zz)

        def both(self, zz):
            self.xc.arrived(zz)
            return self.stage[zz, pl.ds(96 * x, 96), :].astype(F32) + self.xr[zz].astype(F32)

        def z_near(self):
            for i in range(2):
                self.stage[order[i], pl.ds(96 * x, 96), :] = self.both(order[i]).astype(BF)
                self.nc.start(i)

        def z_far(self):
            total = self.both(zfar)
            self.nc.arrived(0)
            total = total + self.zr[1].astype(F32)
            self.stage[zfar, pl.ds(96 * x, 96), :] = total.astype(BF)
            self.fc.start(0)

        def z_direct(self):
            for i in range(3):
                zz = lax.rem(z + 1 + i, 4)
                self.stage[zz, pl.ds(96 * x, 96), :] = self.both(zz).astype(BF)
                self.dc.start(i)

        def finish_direct(self):
            total = self.both(z)
            for i in range(3):
                self.dc.arrived(i)
                total = total + self.zr[i].astype(F32)
            return total

        def finish(self):
            total = self.both(z)
            self.nc.arrived(1)
            self.fc.arrived(0)
            return total + self.zr[0].astype(F32) + self.zr[2].astype(F32)

    pieceU = Piece(s.pU, s.xU, s.zU)
    pieceK = Piece(s.pK, s.xK, s.zK, True)

    def near_make(i):
        k = 1 - lax.div(i, 2)
        rows = pl.ds(96 * lax.rem(i, 2), 96)
        return (
            s.pW.at[lax.rem(znear + 2 * k, 4), rows, :],
            s.zW.at[k, rows, :],
            {"dp": znear},
        )

    def far_make(i):
        rows = pl.ds(96 * i, 96)
        return (s.pW.at[zfar, rows, :], s.zW2.at[rows, :], {"dp": zfar})

    wnear = family(4, near_make)
    wfar = family(2, far_make)
    wlast = family(1, lambda i: (s.xWs, s.xW, {"sp": 1 - x}))
    all_waits.extend([wnear, wfar, wlast])

    def send_near(value):
        for i, zz in enumerate(order):
            s.pW[zz] = value(zz).astype(BF)
            if i < 2:
                wnear.start(2 * i)
                wnear.start(2 * i + 1)

    def send_far():
        for i in range(2):
            wnear.arrived(i)
            rows = pl.ds(96 * i, 96)
            total = s.pW[zfar, rows, :].astype(F32) + s.zW[1, rows, :].astype(F32)
            s.pW[zfar, rows, :] = total.astype(BF)
            wfar.start(i)

    def summed(side):
        rows = pl.ds(96 * side, 96)
        total = s.pW[z, rows, :].astype(F32) + s.zW[0, rows, :].astype(F32)
        return total + s.zW2[rows, :].astype(F32)

    def send_last():
        for i in range(2):
            wnear.arrived(2 + i)
            wfar.arrived(i)
        s.xWs[...] = summed(1 - x).astype(BF)
        wlast.start(0)

    pieceO = Piece(s.pO, s.xO, s.zO)
    pieceQ = Piece(s.pQ, s.xQ, s.zQ)

    gtp = [
        family(1, lambda i, r=r: (s.gsum.at[t], s.gsum.at[t], {"tp": tpdev[r]}))
        for r in (1, 2, 3)
    ]
    gxc = family(1, lambda i: (s.gx.at[0], s.gx.at[1], {"sp": 1 - x}))
    gzc = family(
        3, lambda i: (s.gx.at[0], s.gz.at[i], {"dp": lax.rem(z + 1 + i, 4)})
    )
    all_waits.extend([*gtp, gxc, gzc])

    row = lax.broadcasted_iota(jnp.int32, (64, CH), 0)
    col = lax.broadcasted_iota(jnp.int32, (64, CH), 1)
    blk = lax.shift_right_logical(col, 4)
    few = row[:16]
    blk16 = blk[:16]
    for v, shown in enumerate((few == blk16, few < blk16, few <= blk16, few < 16)):
        s.maskb[v] = jnp.where(shown, 0.0, NEG).astype(BF)
    s.plain[...] = jnp.where(few == 0, 1.0, 0.0).astype(BF)
    length = len_r[0]
    hot = jnp.where((row == blk) | ((row > 16) & (row < 20)), 1.0, 0.0).astype(F32)
    unit = jnp.where(row < 3, 1.0, 0.0).astype(F32)

    def minus(value, first):
        high = value.astype(BF).astype(F32)
        middle = (value - high).astype(BF).astype(F32)
        low = value - high - middle
        out = jnp.where(few == first, -high, 0.0)
        out = jnp.where(few == first + 1, -middle, out)
        return jnp.where(few == first + 2, -low, out)

    def query_tail(value):
        return (minus(value, 1) + jnp.where(few == 0, 1.0, 0.0)).astype(BF)

    def key_tail(start):
        outside = (row == 16) & (col + start >= length)
        return jnp.where(outside, NEG, hot)

    def keep_keys(kt, h, kT, vT, tail):
        s.kaug[kt, h] = jnp.transpose(jnp.concatenate([kT, tail], axis=0)).astype(BF)
        s.vn[kt, h] = jnp.transpose(jnp.concatenate([vT, unit], axis=0)).astype(BF)

    for ref in (s.dkv, s.dq):
        ref[...] = jnp.zeros_like(ref)
    s.gsum[...] = jnp.zeros_like(s.gsum)

    loads[4].wait()
    pl.semaphore_wait(barrier, 7)
    loads[6].wait()
    wcopy.start(0)
    loads[5].wait()

    gain1 = gains[0:1, :]
    gain2 = gains[1:2, :]

    def centred(v):
        centre = v - jnp.mean(v, axis=-1, keepdims=True)
        inverse = lax.rsqrt(jnp.mean(centre * centre, axis=-1, keepdims=True) + EPSILON)
        return centre * inverse, inverse

    def project_chunk(ch, j):
        def rows(r):
            v = s.x[ch, pl.ds(r * RW, RW), :].astype(F32)
            s.a[pl.ds(ch * CH + r * RW, RW), :] = (centred(v)[0] * gain1).astype(BF)

        for r in range(4):
            rows(r)
        proj = nt(s.wT[...], s.a[pl.ds(ch * CH, CH), :])
        cos = s.cs[j, 0]
        sin = s.cs[j, 1]
        tail = key_tail(x * (2 * CH) + j * CH)
        for h in range(3):
            turned = []
            for i in range(2):
                first = proj[i * 192 + h * 64 : i * 192 + h * 64 + 32]
                second = proj[i * 192 + h * 64 + 32 : i * 192 + h * 64 + 64]
                turned.append(
                    jnp.concatenate(
                        [first * cos - second * sin, second * cos + first * sin], axis=0
                    )
                )
            vT = proj[384 + h * 64 : 384 + h * 64 + 64]
            s.qT[ch, h] = (turned[0] * 0.125).astype(BF)
            s.kvT[ch, 0, h] = turned[1].astype(BF)
            s.kvT[ch, 1, h] = vT.astype(BF)
            keep_keys(ch, h, turned[1], vT, tail)

    def clean_chunk(j):
        loads[2 + j].wait()
        project_chunk(2 + j, j)

        @pl.when(x == 0)
        def _():
            kvcopy.start(j)

    for j in range(2):
        clean_chunk(j)

    def noisy_chunk(j):
        loads[j].wait()
        project_chunk(j, j)

    for j in range(2):
        noisy_chunk(j)

    def scores(ch, h, kt, v, tail):
        query = jnp.concatenate([s.qT[ch, h], s.maskb[v], tail], axis=0)
        return nn(s.kaug[kt, h, :, 0:96], query)

    HEADS3 = [(ch, h) for ch in range(4) for h in range(3)]

    def mix(heads, tiles, fresh):
        tops = {}
        for ch, h in heads:
            top = None if fresh else s.stat[ch * 3 + h, 0:1, :]
            for kt, v in tiles[ch]:
                p = jnp.max(scores(ch, h, kt, v, s.plain[...]), axis=0, keepdims=True)
                top = p if top is None else jnp.maximum(top, p)
            tops[ch, h] = top
        items = [(ch, h, kt, v) for ch, h in heads for kt, v in tiles[ch]]
        tails = {}

        def product(ch, h, kt, v):
            if (ch, h) not in tails:
                tails[ch, h] = query_tail(tops[ch, h])
            return scores(ch, h, kt, v, tails[ch, h])

        sums, mixed = {}, {}
        ahead = product(*items[0])
        for n, (ch, h, kt, v) in enumerate(items):
            logits = ahead
            if n + 1 < len(items):
                ahead = product(*items[n + 1])
            e = jnp.exp(logits)
            total = jnp.sum(e, axis=0, keepdims=True)
            part = nn(s.kvT[kt, 1, h], e.astype(BF))
            sums[ch, h] = sums[ch, h] + total if (ch, h) in sums else total
            mixed[ch, h] = mixed[ch, h] + part if (ch, h) in mixed else part
            if n + 1 == len(items) or items[n + 1][:2] != (ch, h):
                at = ch * 3 + h
                total, part = sums[ch, h], mixed[ch, h]
                if not fresh:
                    scale = jnp.exp(s.stat[at, 0:1, :] - tops[ch, h])
                    total = total + s.stat[at, 1:2, :] * scale
                    part = part + s.oacc[ch, h] * scale
                s.stat[at, 0:1, :] = tops[ch, h]
                s.stat[at, 1:2, :] = total
                s.oacc[ch, h] = part

    mix(HEADS3, TILES, True)
    wcopy.arrived(0)
    wcopy.start(1)

    def close(ch):
        for h in range(3):
            at = ch * 3 + h
            total = s.stat[at, 1:2, :]
            out = s.oacc[ch, h] / total
            s.oacc[ch, h] = out
            s.qtail[at] = query_tail(s.stat[at, 0:1, :] + jnp.log(total))
            s.oT[ch, h * 64 : h * 64 + 64, :] = out.astype(BF)
        whole = jnp.concatenate([s.oacc[ch, h] for h in range(3)], axis=0)
        flat = jnp.transpose(whole)
        for k in range(4):
            pair = [flat[k * RW + 32 * i : k * RW + 32 * i + 32] for i in range(2)]
            s.on[ch, 32 * k : 32 * k + 32, :] = jnp.concatenate(pair, axis=1).astype(BF)
        for copy in ocopy:
            copy.start(ch)

    @pl.when(x == 1)
    def _():
        for j in range(2):
            kvcopy.arrived(j)
            tail = key_tail(j * CH)
            for h in range(3):
                keep_keys(
                    4 + j, h, s.kvT[4 + j, 0, h].astype(F32), s.kvT[4 + j, 1, h].astype(F32), tail
                )
            tiles = [((4 + j, 3),)] * 4
            if j == 0:
                mix(HEADS3, tiles, False)
        for ch in range(4):
            mix(HEADS3[3 * ch : 3 * ch + 3], tiles, False)
            close(ch)

    @pl.when(x == 0)
    def _():
        for ch in range(4):
            close(ch)

    wcopy.arrived(1)

    def out_rows(ch):
        total = s.x[ch, pl.ds(slot * RW, RW), :].astype(F32)

        def unpacked(v):
            v = v.astype(F32)
            return jnp.concatenate([v[:, :192], v[:, 192:]], axis=0).astype(BF)

        total = total + nn(unpacked(s.on[ch, pl.ds(slot * 32, 32), :]), s.wfull[slot])
        for r in (1, 2, 3):
            ocopy[r - 1].arrived(ch)
            total = total + nn(unpacked(s.orecv[ch, r - 1]), s.wfull[tpslot[r]])
        s.h1[ch] = total
        own(s.b, ch)[...] = (centred(total)[0] * gain2).astype(BF)
        ag1[0].start(ch)

    each(4, out_rows)
    for i in (7, 8, 9):
        loads[i].wait()

    def add_pair(rs, stage, ra, ch):
        rs[0].arrived(ch)
        rows = pl.ds(pslot * RW, RW)
        total = stage[ch, rows, :].astype(F32) + ra[ch, pl.ds((1 - y) * RW, RW), :].astype(F32)
        stage[ch, rows, :] = total.astype(BF)
        rs[1].start(ch)

    def add_last(rs, stage, ra, rb, ch):
        rs[1].arrived(ch)
        rows = pl.ds(slot * RW, RW)
        total = stage[ch, rows, :].astype(F32) + ra[ch, pl.ds(y * RW, RW), :].astype(F32)
        return total + rb[ch].astype(F32)

    def relay(ag, ch):
        ag[0].arrived(ch)
        ag[1].start(ch)

    def norm_back(grad, stream, gain, at):
        scaled, inverse = centred(stream)
        inner = grad * gain
        s.gsum[t, at : at + 1, :] += jnp.sum(grad * scaled, axis=0, keepdims=True)
        inner_mean = jnp.mean(inner, axis=-1, keepdims=True)
        mixed_mean = jnp.mean(inner * scaled, axis=-1, keepdims=True)
        return inverse * (inner - inner_mean - scaled * mixed_mean)

    def second_back(ch):
        grad = add_last(rs3, s.st3, s.ra3, s.rb3, ch)
        through = norm_back(grad, s.h1[ch], gain2, 1)
        cot = s.cot[pl.ds(ch * CH + slot * RW, RW), :].astype(F32)
        g1 = cot + through
        s.g1[ch] = g1
        own(s.gy, ch)[...] = g1.astype(BF)
        ag3[0].start(ch)

    def feed(ch):
        rows = pl.ds(ch * CH, CH)

        ag1[1].arrived(ch)
        low_b = s.b[rows, :]
        low_g = s.cot[rows, :]
        for n in range(3):
            cols = slice(n * CH, (n + 1) * CH)
            u = nn(low_b, s.wup[:, cols])
            gm = nt(low_g, s.wdown[cols, :])
            square = u * u
            hp = 0.5 + 0.5 * jnp.tanh(u * (GC + GC * GA * square))
            act = u * hp
            slope = hp + (act - act * hp) * (2.0 * GC + 6.0 * GC * GA * square)
            s.m[rows, cols] = act.astype(BF)
            s.gu[rows, cols] = (slope * gm).astype(BF)
            if n == 1:

                @pl.when(ch >= 1)
                def _():
                    add_pair(rs3, s.st3, s.ra3, ch - 1)

                @pl.when(ch < 3)
                def _():
                    relay(ag1, ch + 1)

        s.st3[ch] = nt(s.gu[rows, :], s.wup[...]).astype(BF)
        rs3[0].start(ch)

        s.st2[ch] = nn(s.m[rows, :], s.wdown[...]).astype(BF)
        rs2[0].start(ch)

    relay(ag1, 0)
    each(4, feed)
    add_pair(rs3, s.st3, s.ra3, 3)

    def transposed(dst, src):
        for ch in range(4):
            dst[ch] = jnp.transpose(src[pl.ds(ch * CH, CH), :])

    def rows_by(lhs, rhs):
        def value(zz):
            total = nn(lhs[0, pl.ds(192 * zz, 192), :], rhs[0:CH, :])
            for ch in range(1, 4):
                total = total + nn(lhs[ch, pl.ds(192 * zz, 192), :], rhs[ch * CH : ch * CH + CH, :])
            return total

        return value

    def back_tiles(items):
        def products(ch, h, kt, v):
            at = ch * 3 + h
            grad = jnp.concatenate([s.goT[ch, h], s.gtail[at]], axis=0)
            return scores(ch, h, kt, v, s.qtail[at]), nn(s.vn[kt, h, :, 0:80], grad)

        ahead = products(*items[0])
        for n, (ch, h, kt, v) in enumerate(items):
            logits, gp = ahead
            if n + 1 < len(items):
                ahead = products(*items[n + 1])
            weights = jnp.exp(logits)
            gs = (weights * gp).astype(BF)
            s.dkv[kt, 1, h] += nt(s.goT[ch, h], weights.astype(BF))
            s.dkv[kt, 0, h] += nt(s.qT[ch, h], gs)
            s.dq[ch, h] += nn(s.kvT[kt, 0, h], gs)

    def attention_back(ch):
        ag3[1].arrived(ch)
        goT = nt(s.wfull[slot], s.gy[pl.ds(ch * CH, CH), :])
        for h in range(3):
            low = goT[h * 64 : h * 64 + 64].astype(BF)
            s.goT[ch, h] = low
            inner = jnp.sum(low.astype(F32) * s.oacc[ch, h], axis=0, keepdims=True)
            s.gtail[ch * 3 + h] = minus(inner, 0).astype(BF)

        @pl.when(x == 1)
        def _():
            back_tiles([(ch, h, 4 + j, 3) for j in range(2) for h in range(3)])
            if ch == 3:
                for j in range(2):
                    s.dkvs[j] = s.dkv[4 + j].astype(BF)
                    dkcopy.start(j)


    def turn_back(u, cos, sin):
        first = u[:32]
        second = u[32:]
        return jnp.concatenate([first * cos + second * sin, second * cos - first * sin], axis=0)

    def grad_rows(ch):
        j = ch % 2
        cos = s.cs[j, 0]
        sin = s.cs[j, 1]
        for h in range(3):
            s.gT[ch, h] = turn_back(s.dq[ch, h] * 0.125, cos, sin).astype(BF)
            s.gT[ch, 3 + h] = turn_back(s.dkv[ch, 0, h], cos, sin).astype(BF)
            s.gT[ch, 6 + h] = s.dkv[ch, 1, h].astype(BF)
        s.st4[ch] = tn(s.gT[ch].reshape(576, CH), s.wT[...]).astype(BF)
        rs4[0].start(ch)

    def turn_query(ch):
        for h in range(3):
            s.gT[ch, h] = turn_back(s.dq[ch, h] * 0.125, s.cs[ch % 2, 0], s.cs[ch % 2, 1]).astype(BF)

    def hidden_rows(ch):
        total = s.h1[ch] + add_last(rs2, s.st2, s.ra2, s.rb2, ch)
        own(hid, ch)[...] = total.astype(BF)
        ag2[0].start(ch)

    def input_rows(ch):
        grad = add_last(rs4, s.st4, s.ra4, s.rb4, ch)
        stream = s.x[ch, pl.ds(slot * RW, RW), :].astype(F32)
        total = s.g1[ch] + norm_back(grad, stream, gain1, 0)
        own(ig, ch)[...] = total.astype(BF)
        ag4[0].start(ch)

    def out_piece(zz):
        total = nt(s.tT[0, pl.ds(192 * zz, 192), :], s.oT[0])
        for ch in range(1, 4):
            total = total + nt(s.tT[ch, pl.ds(192 * zz, 192), :], s.oT[ch])
        return total

    def part_piece(lo, hi):
        def value(zz):
            total = None
            for ch in range(4):
                grads = s.gT[ch, lo:hi].reshape((hi - lo) * 64, CH)
                part = nt(s.tT2[ch, pl.ds(192 * zz, 192), :], grads)
                total = part if total is None else total + part
            return total

        return value

    def keep(i):
        rows = pl.ds(i % 4 * CH, CH)
        src, dst = (hid, hid_h) if i < 4 else (ig, ig_h)
        return pltpu.make_async_copy(src.at[rows, :], dst.at[rows, :], lsem.at[10 + i])

    def save(ag, i):
        ag[1].arrived(i % 4)
        keep(i).start()

    second_back(0)
    second_back(1)
    transposed(s.tT, s.b)
    pieceU.compute(rows_by(s.tT, s.gu))
    transposed(s.tT, s.cot)
    send_near(rows_by(s.tT, s.m))
    second_back(2)
    relay(ag3, 0)
    relay(ag3, 1)
    second_back(3)
    for ch in range(4):
        add_pair(rs2, s.st2, s.ra2, ch)
    relay(ag3, 2)
    attention_back(0)
    attention_back(1)
    relay(ag3, 3)
    attention_back(2)
    attention_back(3)
    hidden_rows(0)
    hidden_rows(1)
    back_tiles([(ch, h, kt, v) for ch, h in HEADS3 for kt, v in TILES[ch]])
    for ch in range(2):
        grad_rows(ch)
    send_far()
    pieceU.z_near()
    for ch in range(2):
        add_pair(rs4, s.st4, s.ra4, ch)
    transposed(s.tT, s.gy)
    pieceO.compute(out_piece)
    transposed(s.tT2, s.a)
    for ch in range(2, 4):
        turn_query(ch)
    pieceQ.compute(part_piece(0, 3))
    hidden_rows(2)
    hidden_rows(3)

    @pl.when(x == 0)
    def _():
        for j in range(2):
            dkcopy.arrived(j)
            s.dkv[2 + j] += s.dkvr[j].astype(F32)

    for ch in range(2, 4):
        grad_rows(ch)
    pieceK.compute(part_piece(3, 9))
    for ch in range(2, 4):
        add_pair(rs4, s.st4, s.ra4, ch)
    for ch in range(2):
        input_rows(ch)
    pieceU.z_far()
    for ch in range(4):
        relay(ag2, ch)
    pieceO.z_near()
    pieceQ.z_near()
    for ch in range(2, 4):
        input_rows(ch)

    for copy in gtp:
        copy.start(0)
    for ch in range(2):
        relay(ag4, ch)
    send_last()
    pieceK.z_direct()
    pieceO.z_far()
    pieceQ.z_far()
    for copy in gtp:
        copy.arrived(0)
    s.gx[0] = s.gsum[0] + s.gsum[1] + s.gsum[2] + s.gsum[3]
    gxc.start(0)
    for i in range(6):
        save(ag2 if i < 4 else ag4, i)
    outU[...] = pieceU.finish()
    relay(ag4, 2)
    wlast.arrived(0)
    outW[...] = summed(x) + s.xW[...].astype(F32)
    gxc.arrived(0)
    gxc.sent(0)
    s.gx[0] = s.gx[0] + s.gx[1]
    for i in range(3):
        gzc.start(i)
    relay(ag4, 3)
    outO[...] = jnp.transpose(pieceO.finish())
    outQ[0] = pieceQ.finish()
    both = pieceK.finish_direct()
    outQ[1] = both[:, :192]
    outQ[2] = both[:, 192:]
    total = s.gx[0]
    for i in range(3):
        gzc.arrived(i)
        total = total + s.gz[i]
    for k in range(8):
        @pl.when(z * 2 + x == k)
        def _(k=k):
            outG[...] = total[0:2, 96 * k : 96 * k + 96]
    for i in range(6, 8):
        save(ag4, i)

    for fam in all_waits:
        if fam is gxc:
            continue
        for i in range(fam.count):
            fam.sent(i)

    @pl.when(x == 0)
    def _():
        for i in range(2):
            kvcopy.sent(i)

    @pl.when(x == 1)
    def _():
        for i in range(2):
            dkcopy.sent(i)

    for i in range(8):
        keep(i).wait()


def finish_kernel(*refs):
    sources, results = refs[:7], refs[7:14]
    rows, wide, smalls = refs[14], refs[15], refs[16:21]
    isem, osem = refs[21:]

    def part(ref, i):
        return ref.at[pl.ds(i * CH, CH), :]

    def move(src, dst, sem):
        return pltpu.make_async_copy(src, dst, sem)

    ins = [move(part(sources[1], i), rows.at[1, i], isem.at[4 + i]) for i in range(4)]
    ins += [move(part(sources[0], i), rows.at[0, i], isem.at[i]) for i in range(4)]
    ins += [move(sources[2 + k], smalls[k], isem.at[8 + k]) for k in range(5)]
    for copy in ins:
        copy.start()
    outs = []
    for i in range(4):
        ins[i].wait()
        wide[i] = rows[1, i].astype(F32)
        outs.append(move(wide.at[i], part(results[1], i), osem.at[4 + i]))
        outs[-1].start()
    for i in range(4):
        ins[4 + i].wait()
        outs.append(move(rows.at[0, i], part(results[0], i), osem.at[i]))
        outs[-1].start()
    for k in range(5):
        ins[8 + k].wait()
        outs.append(move(smalls[k], results[2 + k], osem.at[8 + k]))
        outs[-1].start()
    for copy in outs:
        copy.wait()


def finish(arrays):
    shapes = [jax.ShapeDtypeStruct(v.shape, v.dtype) for v in arrays]
    shapes[1] = jax.ShapeDtypeStruct(arrays[1].shape, F32)
    return pl.pallas_call(
        finish_kernel,
        out_shape=shapes,
        in_specs=[ANY] * 7,
        out_specs=[ANY] * 7,
        scratch_shapes=[pltpu.VMEM((2, 4, CH, 768), BF), pltpu.VMEM((4, CH, 768), F32)]
        + [pltpu.VMEM(v.shape, v.dtype) for v in arrays[2:]]
        + [pltpu.SemaphoreType.DMA((13,)), pltpu.SemaphoreType.DMA((13,))],
        name="finish",
    )(*arrays)


def rope_table(seq):
    half_dim = HEAD_DIM // 2
    freq = 10000.0 ** (-np.arange(half_dim) * 2.0 / HEAD_DIM)
    angle = freq[:, None] * np.arange(seq)[None, :]
    both = np.stack([np.cos(angle), np.sin(angle)])
    return np.moveaxis(both.reshape(2, half_dim, seq // CH, CH), 2, 0).astype(np.float32)


def fast(inputs, lengths, gains, w_qkv, w_out, w_up, w_down, cotangent):
    seg = inputs.shape[2]
    shape = jax.ShapeDtypeStruct
    found = pl.pallas_call(
        step_kernel,
        out_shape=(
            shape((1024, 768), BF),
            shape((1024, 768), BF),
            shape((3, 96, 192), F32),
            shape((192, 96), F32),
            shape((96, 768), F32),
            shape((96, 768), F32),
            shape((2, 96), F32),
        ),
        in_specs=[ANY, pl.BlockSpec(memory_space=pltpu.SMEM), VM, ANY, ANY, ANY, ANY, ANY, ANY],
        out_specs=[ANY] * 2 + [VM] * 5,
        scratch_shapes=[pltpu.VMEM(dims, kind) for dims, kind in SCRATCH.values()]
        + [
            pltpu.SemaphoreType.DMA((18,)),
            pltpu.SemaphoreType.DMA((140,)),
            pltpu.SemaphoreType.DMA((140,)),
        ],
        compiler_params=pltpu.CompilerParams(
            collective_id=0, has_side_effects=True, vmem_limit_bytes=64 * 1024 * 1024 - 65536
        ),
        name="step",
    )(
        inputs.reshape(4, CH, 768),
        lengths,
        gains[0],
        jnp.swapaxes(w_qkv[0], 1, 2).reshape(576, 768),
        w_out[0],
        w_up[0],
        w_down[0],
        cotangent.reshape(1024, 768),
        jnp.asarray(rope_table(seg * lax.axis_size("sp"))),
    )
    hid, ig, gq, go, gu, gd, gg = finish(found)
    return (
        hid.reshape(inputs.shape),
        ig.reshape(inputs.shape),
        gq[None],
        go[None],
        gu[None],
        jnp.swapaxes(gd, 0, 1)[None],
        gg[None],
    )


def pick(*args):
    inputs, w_out = args[0], args[4]
    plain = (1, 2, 512, 768)
    sizes = (lax.axis_size("tp"), lax.axis_size("dp"), lax.axis_size("sp"))
    if inputs.shape == plain and w_out.shape[1:] == (192, 768) and sizes == (4, 4, 2):
        return fast(*args)
    return shards(*args)


def solution(mesh):
    in_specs = (
        P("dp", None, "sp", None),
        P("dp"),
        P(),
        P(None, None, None, "tp"),
        P(None, "tp", None),
        P(None, None, "tp"),
        P(None, "tp", None),
        P("dp", None, "sp", None),
    )
    out_specs = (
        P("dp", None, "sp", None),
        P("dp", None, "sp", None),
        P(None, None, ("dp", "sp"), "tp"),
        P(None, "tp", ("dp", "sp")),
        P(None, ("dp", "sp"), "tp"),
        P(None, "tp", ("dp", "sp")),
        P(None, None, ("dp", "sp")),
    )
    return jax.shard_map(pick, mesh=mesh, in_specs=in_specs, out_specs=out_specs, check_vma=False)
```

```python
from functools import partial
from types import SimpleNamespace

import jax
import jax.numpy as jnp
import numpy as np
from jax import lax
from jax.experimental import pallas as pl
from jax.experimental.pallas import tpu as pltpu
from jax.sharding import PartitionSpec as P

HEAD_DIM = 64
BLOCK = 16


EPSILON = 1e-05


def normalize(value, gain):
    centre = value - jnp.mean(value, axis=-1, keepdims=True)
    inverse = lax.rsqrt(jnp.mean(centre * centre, axis=-1, keepdims=True) + EPSILON)
    scaled = centre * inverse
    return (scaled * gain, scaled, inverse)


def norm_back(grad, scaled, inverse, gain):
    inner = grad * gain
    gain_grad = jnp.sum(grad * scaled, axis=(0, 1, 2))
    centred = inner - jnp.mean(inner, axis=-1, keepdims=True)
    result = inverse * (centred - scaled * jnp.mean(inner * scaled, axis=-1, keepdims=True))
    return (result, gain_grad)


def rotate(value, cosine, sine):
    half_dim = value.shape[-1] // 2
    first = value[..., :half_dim]
    second = value[..., half_dim:]
    return jnp.concatenate(
        [first * cosine - second * sine, second * cosine + first * sine], axis=-1
    )


def tables(offset, count):
    half_dim = HEAD_DIM // 2
    freq = 10000.0 ** (-jnp.arange(half_dim).astype(jnp.float32) * 2.0 / HEAD_DIM)
    angle = (offset + jnp.arange(count)).astype(jnp.float32)[:, None] * freq[None, :]
    return (jnp.cos(angle)[:, None, :], jnp.sin(angle)[:, None, :])


def visible(lengths, offset, seg, seq):
    places = offset + jnp.arange(seg)
    query_block = jnp.concatenate([places, places]) // BLOCK
    query_clean = jnp.arange(2 * seg) >= seg
    key_place = jnp.concatenate([places, jnp.arange(seq)])
    key_block = key_place // BLOCK
    key_clean = jnp.arange(seg + seq) >= seg
    query_noisy = jnp.logical_not(query_clean)[:, None]
    same_noisy = (
        query_noisy
        & jnp.logical_not(key_clean)[None, :]
        & (key_block[None, :] == query_block[:, None])
    )
    earlier_clean = query_noisy & key_clean[None, :] & (key_block[None, :] < query_block[:, None])
    causal_clean = (
        query_clean[:, None] & key_clean[None, :] & (key_block[None, :] <= query_block[:, None])
    )
    inside = key_place[None, :] < lengths[:, None]
    return (same_noisy | earlier_clean | causal_clean)[None] & inside[:, None, :]


def reduce_branch(branch):
    return lax.psum(branch, "tp")


def norm_in(stream, gain):
    normed, scaled, inverse = normalize(stream, gain)
    return (normed.astype(jnp.bfloat16), scaled, inverse)


def project(low_normed, weights, cosine, sine, heads):
    projected = jnp.einsum(
        "rcsd,tde->trcse", low_normed, weights, preferred_element_type=jnp.float32
    )
    shape = projected.shape[1:4] + (heads, HEAD_DIM)
    query = rotate(projected[0].reshape(shape), cosine, sine).astype(jnp.bfloat16)
    keys = rotate(projected[1].reshape(shape), cosine, sine).astype(jnp.bfloat16)
    values = projected[2].reshape(shape).astype(jnp.bfloat16)
    return (query, keys, values)


def collect(keys, values):
    rows = keys.shape[0]
    seg = keys.shape[2]
    return (
        lax.all_gather(keys[:, 1].reshape(rows, seg, -1), "sp", axis=1, tiled=True),
        lax.all_gather(values[:, 1].reshape(rows, seg, -1), "sp", axis=1, tiled=True),
    )


def join(query, keys, values, clean):
    rows = query.shape[0]
    seg = query.shape[2]
    heads = query.shape[3]
    full_keys = jnp.concatenate([keys[:, 0], clean[0].reshape(rows, -1, heads, HEAD_DIM)], axis=1)
    full_values = jnp.concatenate(
        [values[:, 0], clean[1].reshape(rows, -1, heads, HEAD_DIM)], axis=1
    )
    return (query.reshape(rows, 2 * seg, heads, HEAD_DIM), full_keys, full_values)


def attend(query, keys, values, mask):
    scores = jnp.einsum("rqhd,rkhd->rhqk", query, keys, preferred_element_type=jnp.float32)
    logits = jnp.where(mask[:, None], scores * HEAD_DIM ** (-0.5), -1e30)
    top = jnp.max(logits, axis=-1, keepdims=True)
    total = jnp.sum(jnp.exp(logits - top), axis=-1, keepdims=True)
    logsum = top + jnp.log(total)
    weights = jnp.exp(logits - logsum).astype(jnp.bfloat16)
    mixed = jnp.einsum("rhqk,rkhd->rqhd", weights, values, preferred_element_type=jnp.float32)
    return (mixed, logsum)


def attend_back(query, keys, values, mask, logsum, grad_mixed):
    scores = jnp.einsum("rqhd,rkhd->rhqk", query, keys, preferred_element_type=jnp.float32)
    logits = jnp.where(mask[:, None], scores * HEAD_DIM ** (-0.5), -1e30)
    weights = jnp.exp(logits - logsum)
    low_weights = weights.astype(jnp.bfloat16)
    grad_weights = jnp.einsum(
        "rqhd,rkhd->rhqk", grad_mixed, values, preferred_element_type=jnp.float32
    )
    inner = jnp.sum(grad_weights * weights, axis=-1, keepdims=True)
    grad_scores = (weights * (grad_weights - inner) * HEAD_DIM ** (-0.5)).astype(jnp.bfloat16)
    grad_query = jnp.einsum(
        "rhqk,rkhd->rqhd", grad_scores, keys, preferred_element_type=jnp.float32
    )
    grad_keys = jnp.einsum(
        "rhqk,rqhd->rkhd", grad_scores, query, preferred_element_type=jnp.float32
    )
    grad_values = jnp.einsum(
        "rhqk,rqhd->rkhd", low_weights, grad_mixed, preferred_element_type=jnp.float32
    )
    return (grad_query, grad_keys, grad_values)


def shards(inputs, lengths, gains, w_qkv, w_out, w_up, w_down, cotangent):
    layers = w_qkv.shape[0]
    rows = inputs.shape[0]
    seg = inputs.shape[2]
    heads = w_out.shape[1] // HEAD_DIM
    offset = lax.axis_index("sp") * seg
    seq = seg * lax.axis_size("sp")
    cosine, sine = tables(offset, seg)
    mask = visible(lengths, offset, seg, seq)
    hidden = inputs.astype(jnp.float32)
    kept_clean = []
    layer = 0
    low_attn, scaled_attn, inverse_attn = norm_in(hidden, gains[layer, 0])
    query, keys, values = project(low_attn, w_qkv[layer], cosine, sine, heads)
    clean = collect(keys, values)
    kept_attn = [(low_attn, scaled_attn, inverse_attn)]
    kept_clean.append(clean)
    joined = join(query, keys, values, clean)
    attended = attend(joined[0], joined[1], joined[2], mask)
    low_mixed = attended[0].reshape(rows, 2, seg, -1).astype(jnp.bfloat16)
    branch = jnp.einsum(
        "rcse,ed->rcsd", low_mixed, w_out[layer], preferred_element_type=jnp.float32
    )
    hidden = hidden + reduce_branch(branch)
    low_mlp, scaled_mlp, inverse_mlp = norm_in(hidden, gains[layer, 1])
    kept_mlp = [(low_mlp, scaled_mlp, inverse_mlp)]
    upward = jnp.einsum("rcsd,df->rcsf", low_mlp, w_up[layer], preferred_element_type=jnp.float32)
    active = jax.nn.gelu(upward, approximate=True).astype(jnp.bfloat16)
    branch = jnp.einsum("rcsf,fd->rcsd", active, w_down[layer], preferred_element_type=jnp.float32)
    hidden = hidden + reduce_branch(branch)
    hidden_out = hidden.astype(jnp.bfloat16)
    grad = cotangent.astype(jnp.float32)
    qkv_list = [None] * layers
    out_list = [None] * layers
    up_list = [None] * layers
    down_list = [None] * layers
    gain_list = [None] * layers
    for layer in reversed(range(layers)):
        low_normed, scaled, inverse = kept_mlp[layer]
        upward = jnp.einsum(
            "rcsd,df->rcsf", low_normed, w_up[layer], preferred_element_type=jnp.float32
        )
        active, gelu_back = jax.vjp(partial(jax.nn.gelu, approximate=True), upward)
        low_active = active.astype(jnp.bfloat16)
        grad_branch = grad.astype(jnp.bfloat16)
        down_list[layer] = jnp.einsum(
            "rcsf,rcsd->fd", low_active, grad_branch, preferred_element_type=jnp.float32
        )
        grad_active = jnp.einsum(
            "rcsd,fd->rcsf", grad_branch, w_down[layer], preferred_element_type=jnp.float32
        )
        grad_upward = gelu_back(grad_active)[0].astype(jnp.bfloat16)
        up_list[layer] = jnp.einsum(
            "rcsd,rcsf->df", low_normed, grad_upward, preferred_element_type=jnp.float32
        )
        partial_grad = jnp.einsum(
            "rcsf,df->rcsd", grad_upward, w_up[layer], preferred_element_type=jnp.float32
        )
        grad_normed = reduce_branch(partial_grad)
        through, second_gain = norm_back(grad_normed, scaled, inverse, gains[layer, 1])
        grad = grad + through
        low_attn, scaled_attn, inverse_attn = kept_attn[layer]
        query, keys, values = project(low_attn, w_qkv[layer], cosine, sine, heads)
        clean = collect(keys, values)
        joined = join(query, keys, values, clean)
        attended = attend(joined[0], joined[1], joined[2], mask)
        low_mixed = attended[0].reshape(rows, 2, seg, -1).astype(jnp.bfloat16)
        grad_branch = grad.astype(jnp.bfloat16)
        out_list[layer] = jnp.einsum(
            "rcse,rcsd->ed", low_mixed, grad_branch, preferred_element_type=jnp.float32
        )
        grad_mixed = jnp.einsum(
            "rcsd,ed->rcse", grad_branch, w_out[layer], preferred_element_type=jnp.float32
        )
        grad_mixed = grad_mixed.astype(jnp.bfloat16).reshape(rows, 2 * seg, heads, HEAD_DIM)
        grad_query, grad_keys, grad_values = attend_back(
            joined[0], joined[1], joined[2], mask, attended[1], grad_mixed
        )
        clean_grads = (
            lax.psum_scatter(
                grad_keys[:, seg:].reshape(rows, seq, -1), "sp", scatter_dimension=1, tiled=True
            ),
            lax.psum_scatter(
                grad_values[:, seg:].reshape(rows, seq, -1), "sp", scatter_dimension=1, tiled=True
            ),
        )
        local_shape = (rows, seg, heads, HEAD_DIM)
        key_grad = jnp.stack([grad_keys[:, :seg], clean_grads[0].reshape(local_shape)], axis=1)
        value_grad = jnp.stack([grad_values[:, :seg], clean_grads[1].reshape(local_shape)], axis=1)
        query_grad = grad_query.reshape(rows, 2, seg, heads, HEAD_DIM)
        stacked = jnp.stack(
            [rotate(query_grad, cosine, -sine), rotate(key_grad, cosine, -sine), value_grad]
        )
        stacked = stacked.astype(jnp.bfloat16).reshape(3, rows, 2, seg, -1)
        qkv_list[layer] = jnp.einsum(
            "rcsd,trcse->tde", low_attn, stacked, preferred_element_type=jnp.float32
        )
        partial_grad = jnp.einsum(
            "trcse,tde->rcsd", stacked, w_qkv[layer], preferred_element_type=jnp.float32
        )
        grad_normed = reduce_branch(partial_grad)
        through, first_gain = norm_back(grad_normed, scaled_attn, inverse_attn, gains[layer, 0])
        grad = grad + through
        gain_list[layer] = jnp.stack([first_gain, second_gain])
    qkv_all = jnp.stack(qkv_list)
    out_all = jnp.stack(out_list)
    up_all = jnp.stack(up_list)
    down_all = jnp.stack(down_list)
    gain_all = jnp.stack(gain_list)
    partly = (
        lax.psum_scatter(qkv_all, "dp", scatter_dimension=2, tiled=True),
        lax.psum_scatter(out_all, "dp", scatter_dimension=2, tiled=True),
        lax.psum_scatter(up_all, "dp", scatter_dimension=1, tiled=True),
        lax.psum_scatter(down_all, "dp", scatter_dimension=2, tiled=True),
        lax.psum_scatter(gain_all, "dp", scatter_dimension=2, tiled=True),
    )
    summed = (
        lax.psum_scatter(partly[0], "sp", scatter_dimension=2, tiled=True),
        lax.psum_scatter(partly[1], "sp", scatter_dimension=2, tiled=True),
        lax.psum_scatter(partly[2], "sp", scatter_dimension=1, tiled=True),
        lax.psum_scatter(partly[3], "sp", scatter_dimension=2, tiled=True),
        lax.psum_scatter(partly[4], "sp", scatter_dimension=2, tiled=True),
    )
    return (hidden_out, grad, summed[0], summed[1], summed[2], summed[3], summed[4])


CH = 256
RW = 64
NEG = -1e30
GC = 0.7978845608028654
GA = 0.044715
BF = jnp.bfloat16
F32 = jnp.float32
MESH = pl.DeviceIdType.MESH
VM = pl.BlockSpec(memory_space=pltpu.VMEM)
ANY = pl.BlockSpec(memory_space=pl.ANY)


def nn(a, b):
    return lax.dot_general(a, b, (((1,), (0,)), ((), ())), preferred_element_type=F32)


def nt(a, b):
    return lax.dot_general(a, b, (((1,), (1,)), ((), ())), preferred_element_type=F32)


def tn(a, b):
    return lax.dot_general(a, b, (((0,), (0,)), ((), ())), preferred_element_type=F32)


def each(count, body, start=0):
    def step(i, carry):
        body(i)
        return carry

    lax.fori_loop(start, count, step, 0)


class Copies:
    def __init__(self, sems, base, make):
        self.sems, self.base, self.make = sems, base, make

    def at(self, i):
        src, dst, dev = self.make(i)
        return pltpu.make_async_remote_copy(
            src_ref=src,
            dst_ref=dst,
            send_sem=self.sems[0].at[self.base + i],
            recv_sem=self.sems[1].at[self.base + i],
            device_id=dev,
            device_id_type=MESH,
        )

    def start(self, i):
        self.at(i).start()

    def arrived(self, i):
        self.at(i).wait_recv()

    def sent(self, i):
        self.at(i).wait_send()


SCRATCH = dict(
    x=((4, CH, 768), BF),
    cot=((1024, 768), BF),
    wT=((576, 768), BF),
    wfull=((4, 192, 768), BF),
    wup=((768, 768), BF),
    wdown=((768, 768), BF),
    cs=((2, 2, 32, CH), F32),
    a=((1024, 768), BF),
    tT=((4, 768, CH), BF),
    tT2=((4, 768, CH), BF),
    qT=((4, 3, 64, CH), BF),
    kvT=((6, 2, 3, 64, CH), BF),
    kaug=((6, 3, CH, 128), BF),
    vn=((6, 3, CH, 128), BF),
    qtail=((12, 16, CH), BF),
    gtail=((12, 16, CH), BF),
    maskb=((4, 16, CH), BF),
    plain=((16, CH), BF),
    oacc=((4, 3, 64, CH), F32),
    stat=((12, 8, CH), F32),
    on=((4, 128, 384), BF),
    oT=((4, 192, CH), BF),
    orecv=((4, 3, 32, 384), BF),
    h1=((4, RW, 768), F32),
    b=((1024, 768), BF),
    m=((1024, 768), BF),
    gu=((1024, 768), BF),
    gy=((1024, 768), BF),
    g1=((4, RW, 768), F32),
    goT=((4, 3, 64, CH), BF),
    dkv=((6, 2, 3, 64, CH), F32),
    dkvs=((2, 2, 3, 64, CH), BF),
    dkvr=((2, 2, 3, 64, CH), BF),
    dq=((4, 3, 64, CH), F32),
    gT=((4, 9, 64, CH), BF),
    st2=((4, CH, 768), BF),
    st3=((4, CH, 768), BF),
    st4=((4, CH, 768), BF),
    ra2=((4, 128, 768), BF),
    ra3=((4, 128, 768), BF),
    ra4=((4, 128, 768), BF),
    rb2=((4, RW, 768), BF),
    rb3=((4, RW, 768), BF),
    rb4=((4, RW, 768), BF),
    pU=((4, 192, 768), BF),
    pW=((4, 192, 768), BF),
    pO=((4, 192, 192), BF),
    pQ=((4, 192, 192), BF),
    pK=((4, 192, 384), BF),
    xU=((4, 96, 768), BF),
    xW=((96, 768), BF),
    xWs=((96, 768), BF),
    xO=((4, 96, 192), BF),
    xQ=((4, 96, 192), BF),
    xK=((4, 96, 384), BF),
    zU=((3, 96, 768), BF),
    zW=((2, 192, 768), BF),
    zW2=((192, 768), BF),
    zO=((3, 96, 192), BF),
    zQ=((3, 96, 192), BF),
    zK=((3, 96, 384), BF),
    hid=((1024, 768), BF),
    ig=((1024, 768), BF),
    fQ=((3, 96, 192), F32),
    fO=((192, 96), F32),
    fU=((96, 768), F32),
    fW=((96, 768), F32),
    gsum=((4, 8, 768), F32),
    gx=((2, 8, 768), F32),
    gz=((3, 8, 768), F32),
)

TILES = (
    ((0, 0), (2, 1)),
    ((1, 0), (3, 1), (2, 3)),
    ((2, 2),),
    ((3, 2), (2, 3)),
)


def step_kernel(*refs):
    (x_h, len_r, gains, wqkv_h, wout_h, wup_h, wdown_h, cot_h, cs_h) = refs[:9]
    (hid_h, ig_h, outQ_h, outO_h, outU_h, outW_h, outG) = refs[9:16]
    s = SimpleNamespace(**dict(zip(SCRATCH, refs[16 : 16 + len(SCRATCH)])))
    lsem, ssem, rsem = refs[16 + len(SCRATCH) :]
    sems = (ssem, rsem)
    hid, ig = s.hid, s.ig
    outQ, outO, outU, outW = s.fQ, s.fO, s.fU, s.fW
    t = lax.axis_index("tp")
    z = lax.axis_index("dp")
    x = lax.axis_index("sp")
    c = lax.rem(t, 2)
    y = lax.div(t, 2)
    slot = 2 * c + y
    pslot = 2 * c + 1 - y
    partner = t + 1 - 2 * c
    ypeer = t + 2 - 4 * y
    diag = 3 - t
    tpdev = (None, partner, ypeer, diag)
    tpslot = (slot, 2 * (1 - c) + y, pslot, 2 * (1 - c) + 1 - y)

    barrier = pltpu.get_barrier_semaphore()
    for dev in (
        {"tp": partner},
        {"tp": ypeer},
        {"tp": diag},
        {"sp": 1 - x},
        {"dp": lax.rem(z + 1, 4)},
        {"dp": lax.rem(z + 2, 4)},
        {"dp": lax.rem(z + 3, 4)},
    ):
        pl.semaphore_signal(barrier, inc=1, device_id=dev, device_id_type=MESH)

    def own(ref, ch):
        return ref.at[pl.ds(ch * CH + slot * RW, RW), :]

    def half(ref, ch):
        return ref.at[pl.ds(ch * CH + c * 128, 128), :]

    def load(i, src, dst):
        return pltpu.make_async_copy(src, dst, lsem.at[i])

    loads = [load(i, x_h.at[i], s.x.at[i]) for i in range(4)]
    loads.append(load(4, wqkv_h, s.wT))
    loads.append(load(5, cs_h.at[pl.ds(2 * x, 2)], s.cs))
    loads.append(load(6, wout_h, s.wfull.at[slot]))
    loads.append(load(7, wup_h, s.wup))
    loads.append(load(8, wdown_h, s.wdown))
    loads.append(load(9, cot_h, s.cot))
    for i in (4, 2, 5, 3, 6, 0, 1, 7, 8, 9):
        loads[i].start()

    base = [0]

    def family(count, make):
        made = Copies(sems, base[0], make)
        made.count = count
        base[0] += count
        return made

    def spread(ref):
        return (
            family(4, lambda i: (own(ref, i), own(ref, i), {"tp": ypeer})),
            family(4, lambda i: (half(ref, i), half(ref, i), {"tp": partner})),
        )

    def gather(stage, ra, rb):
        return (
            family(
                4,
                lambda i: (
                    stage.at[i, pl.ds((1 - c) * 128, 128), :],
                    ra.at[i],
                    {"tp": partner},
                ),
            ),
            family(
                4, lambda i: (stage.at[i, pl.ds(pslot * RW, RW), :], rb.at[i], {"tp": ypeer})
            ),
        )

    def wmake(i):
        if i == 0:
            return (s.wfull.at[slot], s.wfull.at[slot], {"tp": ypeer})
        pair = pl.ds(2 * c, 2)
        return (s.wfull.at[pair], s.wfull.at[pair], {"tp": partner})

    wcopy = family(2, wmake)
    kvcopy = family(2, lambda i: (s.kvT.at[2 + i], s.kvT.at[4 + i], {"sp": 1 - x}))
    dkcopy = family(2, lambda i: (s.dkvs.at[i], s.dkvr.at[i], {"sp": 1 - x}))
    ocopy = [
        family(
            4,
            lambda i, r=r: (
                s.on.at[i, pl.ds(tpslot[r] * 32, 32), :],
                s.orecv.at[i, r - 1],
                {"tp": tpdev[r]},
            ),
        )
        for r in (1, 2, 3)
    ]
    ag1 = spread(s.b)
    ag2 = spread(hid)
    ag3 = spread(s.gy)
    ag4 = spread(ig)
    rs2 = gather(s.st2, s.ra2, s.rb2)
    rs3 = gather(s.st3, s.ra3, s.rb3)
    rs4 = gather(s.st4, s.ra4, s.rb4)
    all_waits = [wcopy, *ocopy, *ag1, *ag2, *ag3, *ag4, *rs2, *rs3, *rs4]

    znear = z + 1 - 2 * lax.rem(z, 2)
    zfar = lax.rem(z + 2, 4)
    order = (lax.rem(znear + 2, 4), znear, zfar, z)

    class Piece:
        def __init__(self, stage, xr, zr, direct=False):
            self.stage, self.xr, self.zr = stage, xr, zr
            rows = pl.ds(96 * x, 96)
            self.xc = family(
                4,
                lambda i: (
                    stage.at[i, pl.ds(96 * (1 - x), 96), :],
                    xr.at[i],
                    {"sp": 1 - x},
                ),
            )
            all_waits.append(self.xc)
            if direct:
                self.dc = family(
                    3,
                    lambda i: (
                        stage.at[lax.rem(z + 1 + i, 4), rows, :],
                        zr.at[i],
                        {"dp": lax.rem(z + 1 + i, 4)},
                    ),
                )
                all_waits.append(self.dc)
                return
            self.nc = family(
                2, lambda i: (stage.at[order[i], rows, :], zr.at[1 - i], {"dp": znear})
            )
            self.fc = family(1, lambda i: (stage.at[zfar, rows, :], zr.at[2], {"dp": zfar}))
            all_waits.extend([self.nc, self.fc])

        def compute(self, value, send=True):
            for zz in order:
                self.stage[zz] = value(zz).astype(BF)
                if send:
                    self.xc.start(zz)

        def send(self):
            for zz in order:
                self.xc.start(zz)

        def both(self, zz):
            self.xc.arrived(zz)
            return self.stage[zz, pl.ds(96 * x, 96), :].astype(F32) + self.xr[zz].astype(F32)

        def z_near(self):
            for i in range(2):
                self.stage[order[i], pl.ds(96 * x, 96), :] = self.both(order[i]).astype(BF)
                self.nc.start(i)

        def z_far(self):
            total = self.both(zfar)
            self.nc.arrived(0)
            total = total + self.zr[1].astype(F32)
            self.stage[zfar, pl.ds(96 * x, 96), :] = total.astype(BF)
            self.fc.start(0)

        def z_direct(self):
            for i in range(3):
                zz = lax.rem(z + 1 + i, 4)
                self.stage[zz, pl.ds(96 * x, 96), :] = self.both(zz).astype(BF)
                self.dc.start(i)

        def finish_direct(self):
            total = self.both(z)
            for i in range(3):
                self.dc.arrived(i)
                total = total + self.zr[i].astype(F32)
            return total

        def finish(self):
            total = self.both(z)
            self.nc.arrived(1)
            self.fc.arrived(0)
            return total + self.zr[0].astype(F32) + self.zr[2].astype(F32)

    pieceU = Piece(s.pU, s.xU, s.zU)
    pieceK = Piece(s.pK, s.xK, s.zK, True)

    def near_make(i):
        k = 1 - lax.div(i, 2)
        rows = pl.ds(96 * lax.rem(i, 2), 96)
        return (
            s.pW.at[lax.rem(znear + 2 * k, 4), rows, :],
            s.zW.at[k, rows, :],
            {"dp": znear},
        )

    def far_make(i):
        rows = pl.ds(96 * i, 96)
        return (s.pW.at[zfar, rows, :], s.zW2.at[rows, :], {"dp": zfar})

    wnear = family(4, near_make)
    wfar = family(2, far_make)
    wlast = family(1, lambda i: (s.xWs, s.xW, {"sp": 1 - x}))
    all_waits.extend([wnear, wfar, wlast])

    def send_near(value):
        for i, zz in enumerate(order):
            s.pW[zz] = value(zz).astype(BF)
            if i < 2:
                wnear.start(2 * i)
                wnear.start(2 * i + 1)

    def send_far():
        for i in range(2):
            wnear.arrived(i)
            rows = pl.ds(96 * i, 96)
            total = s.pW[zfar, rows, :].astype(F32) + s.zW[1, rows, :].astype(F32)
            s.pW[zfar, rows, :] = total.astype(BF)
            wfar.start(i)

    def summed(side):
        rows = pl.ds(96 * side, 96)
        total = s.pW[z, rows, :].astype(F32) + s.zW[0, rows, :].astype(F32)
        return total + s.zW2[rows, :].astype(F32)

    def send_last():
        for i in range(2):
            wnear.arrived(2 + i)
            wfar.arrived(i)
        s.xWs[...] = summed(1 - x).astype(BF)
        wlast.start(0)

    pieceO = Piece(s.pO, s.xO, s.zO)
    pieceQ = Piece(s.pQ, s.xQ, s.zQ)

    gtp = [
        family(1, lambda i, r=r: (s.gsum.at[t], s.gsum.at[t], {"tp": tpdev[r]}))
        for r in (1, 2, 3)
    ]
    gxc = family(1, lambda i: (s.gx.at[0], s.gx.at[1], {"sp": 1 - x}))
    gzc = family(
        3, lambda i: (s.gx.at[0], s.gz.at[i], {"dp": lax.rem(z + 1 + i, 4)})
    )
    all_waits.extend([*gtp, gxc, gzc])

    row = lax.broadcasted_iota(jnp.int32, (64, CH), 0)
    col = lax.broadcasted_iota(jnp.int32, (64, CH), 1)
    blk = lax.shift_right_logical(col, 4)
    few = row[:16]
    blk16 = blk[:16]
    for v, shown in enumerate((few == blk16, few < blk16, few <= blk16, few < 16)):
        s.maskb[v] = jnp.where(shown, 0.0, NEG).astype(BF)
    s.plain[...] = jnp.where(few == 0, 1.0, 0.0).astype(BF)
    length = len_r[0]
    hot = jnp.where((row == blk) | ((row > 16) & (row < 20)), 1.0, 0.0).astype(F32)
    unit = jnp.where(row < 3, 1.0, 0.0).astype(F32)

    def minus(value, first):
        high = value.astype(BF).astype(F32)
        middle = (value - high).astype(BF).astype(F32)
        low = value - high - middle
        out = jnp.where(few == first, -high, 0.0)
        out = jnp.where(few == first + 1, -middle, out)
        return jnp.where(few == first + 2, -low, out)

    def query_tail(value):
        return (minus(value, 1) + jnp.where(few == 0, 1.0, 0.0)).astype(BF)

    def key_tail(start):
        outside = (row == 16) & (col + start >= length)
        return jnp.where(outside, NEG, hot)

    def keep_keys(kt, h, kT, vT, tail):
        s.kaug[kt, h] = jnp.transpose(jnp.concatenate([kT, tail], axis=0)).astype(BF)
        s.vn[kt, h] = jnp.transpose(jnp.concatenate([vT, unit], axis=0)).astype(BF)

    for ref in (s.dkv, s.dq):
        ref[...] = jnp.zeros_like(ref)
    s.gsum[...] = jnp.zeros_like(s.gsum)

    loads[4].wait()
    pl.semaphore_wait(barrier, 7)
    loads[6].wait()
    wcopy.start(0)
    loads[5].wait()

    gain1 = gains[0:1, :]
    gain2 = gains[1:2, :]

    def centred(v):
        centre = v - jnp.mean(v, axis=-1, keepdims=True)
        inverse = lax.rsqrt(jnp.mean(centre * centre, axis=-1, keepdims=True) + EPSILON)
        return centre * inverse, inverse

    def project_chunk(ch, j):
        def rows(r):
            v = s.x[ch, pl.ds(r * RW, RW), :].astype(F32)
            s.a[pl.ds(ch * CH + r * RW, RW), :] = (centred(v)[0] * gain1).astype(BF)

        for r in range(4):
            rows(r)
        proj = nt(s.wT[...], s.a[pl.ds(ch * CH, CH), :])
        cos = s.cs[j, 0]
        sin = s.cs[j, 1]
        tail = key_tail(x * (2 * CH) + j * CH)
        for h in range(3):
            turned = []
            for i in range(2):
                first = proj[i * 192 + h * 64 : i * 192 + h * 64 + 32]
                second = proj[i * 192 + h * 64 + 32 : i * 192 + h * 64 + 64]
                turned.append(
                    jnp.concatenate(
                        [first * cos - second * sin, second * cos + first * sin], axis=0
                    )
                )
            vT = proj[384 + h * 64 : 384 + h * 64 + 64]
            s.qT[ch, h] = (turned[0] * 0.125).astype(BF)
            s.kvT[ch, 0, h] = turned[1].astype(BF)
            s.kvT[ch, 1, h] = vT.astype(BF)
            keep_keys(ch, h, turned[1], vT, tail)

    def clean_chunk(j):
        loads[2 + j].wait()
        project_chunk(2 + j, j)

        @pl.when(x == 0)
        def _():
            kvcopy.start(j)

    for j in range(2):
        clean_chunk(j)

    def noisy_chunk(j):
        loads[j].wait()
        project_chunk(j, j)

    for j in range(2):
        noisy_chunk(j)

    def scores(ch, h, kt, v, tail):
        query = jnp.concatenate([s.qT[ch, h], s.maskb[v], tail], axis=0)
        return nn(s.kaug[kt, h, :, 0:96], query)

    HEADS3 = [(ch, h) for ch in range(4) for h in range(3)]

    def mix(heads, tiles, fresh):
        tops = {}
        for ch, h in heads:
            top = None if fresh else s.stat[ch * 3 + h, 0:1, :]
            for kt, v in tiles[ch]:
                p = jnp.max(scores(ch, h, kt, v, s.plain[...]), axis=0, keepdims=True)
                top = p if top is None else jnp.maximum(top, p)
            tops[ch, h] = top
        items = [(ch, h, kt, v) for ch, h in heads for kt, v in tiles[ch]]
        tails = {}

        def product(ch, h, kt, v):
            if (ch, h) not in tails:
                tails[ch, h] = query_tail(tops[ch, h])
            return scores(ch, h, kt, v, tails[ch, h])

        sums, mixed = {}, {}
        ahead = product(*items[0])
        for n, (ch, h, kt, v) in enumerate(items):
            logits = ahead
            if n + 1 < len(items):
                ahead = product(*items[n + 1])
            e = jnp.exp(logits)
            total = jnp.sum(e, axis=0, keepdims=True)
            part = nn(s.kvT[kt, 1, h], e.astype(BF))
            sums[ch, h] = sums[ch, h] + total if (ch, h) in sums else total
            mixed[ch, h] = mixed[ch, h] + part if (ch, h) in mixed else part
            if n + 1 == len(items) or items[n + 1][:2] != (ch, h):
                at = ch * 3 + h
                total, part = sums[ch, h], mixed[ch, h]
                if not fresh:
                    scale = jnp.exp(s.stat[at, 0:1, :] - tops[ch, h])
                    total = total + s.stat[at, 1:2, :] * scale
                    part = part + s.oacc[ch, h] * scale
                s.stat[at, 0:1, :] = tops[ch, h]
                s.stat[at, 1:2, :] = total
                s.oacc[ch, h] = part

    mix(HEADS3, TILES, True)
    wcopy.arrived(0)
    wcopy.start(1)

    def close(ch):
        for h in range(3):
            at = ch * 3 + h
            total = s.stat[at, 1:2, :]
            out = s.oacc[ch, h] / total
            s.oacc[ch, h] = out
            s.qtail[at] = query_tail(s.stat[at, 0:1, :] + jnp.log(total))
            s.oT[ch, h * 64 : h * 64 + 64, :] = out.astype(BF)
        whole = jnp.concatenate([s.oacc[ch, h] for h in range(3)], axis=0)
        flat = jnp.transpose(whole)
        for k in range(4):
            pair = [flat[k * RW + 32 * i : k * RW + 32 * i + 32] for i in range(2)]
            s.on[ch, 32 * k : 32 * k + 32, :] = jnp.concatenate(pair, axis=1).astype(BF)
        for copy in ocopy:
            copy.start(ch)

    @pl.when(x == 1)
    def _():
        for j in range(2):
            kvcopy.arrived(j)
            tail = key_tail(j * CH)
            for h in range(3):
                keep_keys(
                    4 + j, h, s.kvT[4 + j, 0, h].astype(F32), s.kvT[4 + j, 1, h].astype(F32), tail
                )
            tiles = [((4 + j, 3),)] * 4
            if j == 0:
                mix(HEADS3, tiles, False)
        for ch in range(4):
            mix(HEADS3[3 * ch : 3 * ch + 3], tiles, False)
            close(ch)

    @pl.when(x == 0)
    def _():
        for ch in range(4):
            close(ch)

    wcopy.arrived(1)

    def out_rows(ch):
        total = s.x[ch, pl.ds(slot * RW, RW), :].astype(F32)

        def unpacked(v):
            v = v.astype(F32)
            return jnp.concatenate([v[:, :192], v[:, 192:]], axis=0).astype(BF)

        total = total + nn(unpacked(s.on[ch, pl.ds(slot * 32, 32), :]), s.wfull[slot])
        for r in (1, 2, 3):
            ocopy[r - 1].arrived(ch)
            total = total + nn(unpacked(s.orecv[ch, r - 1]), s.wfull[tpslot[r]])
        s.h1[ch] = total
        own(s.b, ch)[...] = (centred(total)[0] * gain2).astype(BF)
        ag1[0].start(ch)

    each(4, out_rows)
    for i in (7, 8, 9):
        loads[i].wait()

    def add_pair(rs, stage, ra, ch):
        rs[0].arrived(ch)
        rows = pl.ds(pslot * RW, RW)
        total = stage[ch, rows, :].astype(F32) + ra[ch, pl.ds((1 - y) * RW, RW), :].astype(F32)
        stage[ch, rows, :] = total.astype(BF)
        rs[1].start(ch)

    def add_last(rs, stage, ra, rb, ch):
        rs[1].arrived(ch)
        rows = pl.ds(slot * RW, RW)
        total = stage[ch, rows, :].astype(F32) + ra[ch, pl.ds(y * RW, RW), :].astype(F32)
        return total + rb[ch].astype(F32)

    def relay(ag, ch):
        ag[0].arrived(ch)
        ag[1].start(ch)

    def norm_back(grad, stream, gain, at):
        scaled, inverse = centred(stream)
        inner = grad * gain
        s.gsum[t, at : at + 1, :] += jnp.sum(grad * scaled, axis=0, keepdims=True)
        inner_mean = jnp.mean(inner, axis=-1, keepdims=True)
        mixed_mean = jnp.mean(inner * scaled, axis=-1, keepdims=True)
        return inverse * (inner - inner_mean - scaled * mixed_mean)

    def second_back(ch):
        grad = add_last(rs3, s.st3, s.ra3, s.rb3, ch)
        through = norm_back(grad, s.h1[ch], gain2, 1)
        cot = s.cot[pl.ds(ch * CH + slot * RW, RW), :].astype(F32)
        g1 = cot + through
        s.g1[ch] = g1
        own(s.gy, ch)[...] = g1.astype(BF)
        ag3[0].start(ch)

    def feed(ch):
        rows = pl.ds(ch * CH, CH)

        ag1[1].arrived(ch)
        low_b = s.b[rows, :]
        low_g = s.cot[rows, :]
        for n in range(3):
            cols = slice(n * CH, (n + 1) * CH)
            u = nn(low_b, s.wup[:, cols])
            gm = nt(low_g, s.wdown[cols, :])
            square = u * u
            hp = 0.5 + 0.5 * jnp.tanh(u * (GC + GC * GA * square))
            act = u * hp
            slope = hp + (act - act * hp) * (2.0 * GC + 6.0 * GC * GA * square)
            s.m[rows, cols] = act.astype(BF)
            s.gu[rows, cols] = (slope * gm).astype(BF)
            if n == 1:

                @pl.when(ch >= 1)
                def _():
                    add_pair(rs3, s.st3, s.ra3, ch - 1)

                @pl.when(ch < 3)
                def _():
                    relay(ag1, ch + 1)

        s.st3[ch] = nt(s.gu[rows, :], s.wup[...]).astype(BF)
        rs3[0].start(ch)

        s.st2[ch] = nn(s.m[rows, :], s.wdown[...]).astype(BF)
        rs2[0].start(ch)

    relay(ag1, 0)
    each(4, feed)
    add_pair(rs3, s.st3, s.ra3, 3)

    def transposed(dst, src):
        for ch in range(4):
            dst[ch] = jnp.transpose(src[pl.ds(ch * CH, CH), :])

    def rows_by(lhs, rhs):
        def value(zz):
            total = nn(lhs[0, pl.ds(192 * zz, 192), :], rhs[0:CH, :])
            for ch in range(1, 4):
                total = total + nn(lhs[ch, pl.ds(192 * zz, 192), :], rhs[ch * CH : ch * CH + CH, :])
            return total

        return value

    def back_tiles(items):
        def products(ch, h, kt, v):
            at = ch * 3 + h
            grad = jnp.concatenate([s.goT[ch, h], s.gtail[at]], axis=0)
            return scores(ch, h, kt, v, s.qtail[at]), nn(s.vn[kt, h, :, 0:80], grad)

        ahead = products(*items[0])
        for n, (ch, h, kt, v) in enumerate(items):
            logits, gp = ahead
            if n + 1 < len(items):
                ahead = products(*items[n + 1])
            weights = jnp.exp(logits)
            gs = (weights * gp).astype(BF)
            s.dkv[kt, 1, h] += nt(s.goT[ch, h], weights.astype(BF))
            s.dkv[kt, 0, h] += nt(s.qT[ch, h], gs)
            s.dq[ch, h] += nn(s.kvT[kt, 0, h], gs)

    def attention_back(ch):
        ag3[1].arrived(ch)
        goT = nt(s.wfull[slot], s.gy[pl.ds(ch * CH, CH), :])
        for h in range(3):
            low = goT[h * 64 : h * 64 + 64].astype(BF)
            s.goT[ch, h] = low
            inner = jnp.sum(low.astype(F32) * s.oacc[ch, h], axis=0, keepdims=True)
            s.gtail[ch * 3 + h] = minus(inner, 0).astype(BF)

        @pl.when(x == 1)
        def _():
            back_tiles([(ch, h, 4 + j, 3) for j in range(2) for h in range(3)])
            if ch == 3:
                for j in range(2):
                    s.dkvs[j] = s.dkv[4 + j].astype(BF)
                    dkcopy.start(j)


    def turn_back(u, cos, sin):
        first = u[:32]
        second = u[32:]
        return jnp.concatenate([first * cos + second * sin, second * cos - first * sin], axis=0)

    def grad_rows(ch):
        j = ch % 2
        cos = s.cs[j, 0]
        sin = s.cs[j, 1]
        for h in range(3):
            s.gT[ch, h] = turn_back(s.dq[ch, h] * 0.125, cos, sin).astype(BF)
            s.gT[ch, 3 + h] = turn_back(s.dkv[ch, 0, h], cos, sin).astype(BF)
            s.gT[ch, 6 + h] = s.dkv[ch, 1, h].astype(BF)
        s.st4[ch] = tn(s.gT[ch].reshape(576, CH), s.wT[...]).astype(BF)
        rs4[0].start(ch)

    def turn_query(ch):
        for h in range(3):
            s.gT[ch, h] = turn_back(s.dq[ch, h] * 0.125, s.cs[ch % 2, 0], s.cs[ch % 2, 1]).astype(BF)

    def hidden_rows(ch):
        total = s.h1[ch] + add_last(rs2, s.st2, s.ra2, s.rb2, ch)
        own(hid, ch)[...] = total.astype(BF)
        ag2[0].start(ch)

    def input_rows(ch):
        grad = add_last(rs4, s.st4, s.ra4, s.rb4, ch)
        stream = s.x[ch, pl.ds(slot * RW, RW), :].astype(F32)
        total = s.g1[ch] + norm_back(grad, stream, gain1, 0)
        own(ig, ch)[...] = total.astype(BF)
        ag4[0].start(ch)

    def out_piece(zz):
        total = nt(s.tT[0, pl.ds(192 * zz, 192), :], s.oT[0])
        for ch in range(1, 4):
            total = total + nt(s.tT[ch, pl.ds(192 * zz, 192), :], s.oT[ch])
        return total

    def part_piece(lo, hi):
        def value(zz):
            total = None
            for ch in range(4):
                grads = s.gT[ch, lo:hi].reshape((hi - lo) * 64, CH)
                part = nt(s.tT2[ch, pl.ds(192 * zz, 192), :], grads)
                total = part if total is None else total + part
            return total

        return value

    def keep(i):
        rows = pl.ds(i % 4 * CH, CH)
        src, dst = (hid, hid_h) if i < 4 else (ig, ig_h)
        return pltpu.make_async_copy(src.at[rows, :], dst.at[rows, :], lsem.at[10 + i])

    grads_out = [
        load(18 + k, src, dst)
        for k, (src, dst) in enumerate(
            ((outU, outU_h), (outW, outW_h), (outO, outO_h), (outQ, outQ_h))
        )
    ]

    def save(ag, i):
        ag[1].arrived(i % 4)
        keep(i).start()

    second_back(0)
    second_back(1)
    transposed(s.tT, s.b)
    pieceU.compute(rows_by(s.tT, s.gu))
    transposed(s.tT, s.cot)
    send_near(rows_by(s.tT, s.m))
    second_back(2)
    relay(ag3, 0)
    relay(ag3, 1)
    second_back(3)
    for ch in range(4):
        add_pair(rs2, s.st2, s.ra2, ch)
    relay(ag3, 2)
    attention_back(0)
    attention_back(1)
    relay(ag3, 3)
    attention_back(2)
    attention_back(3)
    hidden_rows(0)
    hidden_rows(1)
    back_tiles([(ch, h, kt, v) for ch, h in HEADS3 for kt, v in TILES[ch]])
    for ch in range(2):
        grad_rows(ch)
    send_far()
    pieceU.z_near()
    for ch in range(2):
        add_pair(rs4, s.st4, s.ra4, ch)
    transposed(s.tT, s.gy)
    pieceO.compute(out_piece)
    transposed(s.tT2, s.a)
    for ch in range(2, 4):
        turn_query(ch)
    pieceQ.compute(part_piece(0, 3))
    hidden_rows(2)
    hidden_rows(3)

    @pl.when(x == 0)
    def _():
        for j in range(2):
            dkcopy.arrived(j)
            s.dkv[2 + j] += s.dkvr[j].astype(F32)

    for ch in range(2, 4):
        grad_rows(ch)
    pieceK.compute(part_piece(3, 9))
    for ch in range(2, 4):
        add_pair(rs4, s.st4, s.ra4, ch)
    for ch in range(2):
        input_rows(ch)
    pieceU.z_far()
    pieceO.z_near()
    pieceQ.z_near()
    for ch in range(4):
        relay(ag2, ch)
    for ch in range(2, 4):
        input_rows(ch)

    for copy in gtp:
        copy.start(0)
    for ch in range(2):
        relay(ag4, ch)
    send_last()
    pieceO.z_far()
    pieceQ.z_far()
    pieceK.z_direct()
    for copy in gtp:
        copy.arrived(0)
    s.gx[0] = s.gsum[0] + s.gsum[1] + s.gsum[2] + s.gsum[3]
    gxc.start(0)
    for i in range(6):
        save(ag2 if i < 4 else ag4, i)
    outU[...] = pieceU.finish()
    grads_out[0].start()
    relay(ag4, 2)
    wlast.arrived(0)
    outW[...] = summed(x) + s.xW[...].astype(F32)
    grads_out[1].start()
    gxc.arrived(0)
    gxc.sent(0)
    s.gx[0] = s.gx[0] + s.gx[1]
    for i in range(3):
        gzc.start(i)
    relay(ag4, 3)
    outO[...] = jnp.transpose(pieceO.finish())
    grads_out[2].start()
    outQ[0] = pieceQ.finish()
    both = pieceK.finish_direct()
    outQ[1] = both[:, :192]
    outQ[2] = both[:, 192:]
    grads_out[3].start()
    total = s.gx[0]
    for i in range(3):
        gzc.arrived(i)
        total = total + s.gz[i]
    for k in range(8):
        @pl.when(z * 2 + x == k)
        def _(k=k):
            outG[...] = total[0:2, 96 * k : 96 * k + 96]
    for i in range(6, 8):
        save(ag4, i)

    for fam in all_waits:
        if fam is gxc:
            continue
        for i in range(fam.count):
            fam.sent(i)

    @pl.when(x == 0)
    def _():
        for i in range(2):
            kvcopy.sent(i)

    @pl.when(x == 1)
    def _():
        for i in range(2):
            dkcopy.sent(i)

    for i in range(8):
        keep(i).wait()
    for copy in grads_out:
        copy.wait()


def finish_kernel(*refs):
    sources, results = refs[:7], refs[7:14]
    rows, wide, smalls = refs[14], refs[15], refs[16:21]
    isem, osem = refs[21:]

    def part(ref, i):
        return ref.at[pl.ds(i * CH, CH), :]

    def move(src, dst, sem):
        return pltpu.make_async_copy(src, dst, sem)

    ins = [move(part(sources[1], i), rows.at[1, i], isem.at[4 + i]) for i in range(4)]
    ins += [move(part(sources[0], i), rows.at[0, i], isem.at[i]) for i in range(4)]
    ins += [move(sources[2 + k], smalls[k], isem.at[8 + k]) for k in range(5)]
    for copy in ins:
        copy.start()
    outs = []
    for i in range(4):
        ins[i].wait()
        wide[i] = rows[1, i].astype(F32)
        outs.append(move(wide.at[i], part(results[1], i), osem.at[4 + i]))
        outs[-1].start()
    for i in range(4):
        ins[4 + i].wait()
        outs.append(move(rows.at[0, i], part(results[0], i), osem.at[i]))
        outs[-1].start()
    for k in range(5):
        ins[8 + k].wait()
        outs.append(move(smalls[k], results[2 + k], osem.at[8 + k]))
        outs[-1].start()
    for copy in outs:
        copy.wait()


def finish(arrays):
    shapes = [jax.ShapeDtypeStruct(v.shape, v.dtype) for v in arrays]
    shapes[1] = jax.ShapeDtypeStruct(arrays[1].shape, F32)
    return pl.pallas_call(
        finish_kernel,
        out_shape=shapes,
        in_specs=[ANY] * 7,
        out_specs=[ANY] * 7,
        scratch_shapes=[pltpu.VMEM((2, 4, CH, 768), BF), pltpu.VMEM((4, CH, 768), F32)]
        + [pltpu.VMEM(v.shape, v.dtype) for v in arrays[2:]]
        + [pltpu.SemaphoreType.DMA((13,)), pltpu.SemaphoreType.DMA((13,))],
        name="finish",
    )(*arrays)


def rope_table(seq):
    half_dim = HEAD_DIM // 2
    freq = 10000.0 ** (-np.arange(half_dim) * 2.0 / HEAD_DIM)
    angle = freq[:, None] * np.arange(seq)[None, :]
    both = np.stack([np.cos(angle), np.sin(angle)])
    return np.moveaxis(both.reshape(2, half_dim, seq // CH, CH), 2, 0).astype(np.float32)


def fast(inputs, lengths, gains, w_qkv, w_out, w_up, w_down, cotangent):
    seg = inputs.shape[2]
    shape = jax.ShapeDtypeStruct
    found = pl.pallas_call(
        step_kernel,
        out_shape=(
            shape((1024, 768), BF),
            shape((1024, 768), BF),
            shape((3, 96, 192), F32),
            shape((192, 96), F32),
            shape((96, 768), F32),
            shape((96, 768), F32),
            shape((2, 96), F32),
        ),
        in_specs=[ANY, pl.BlockSpec(memory_space=pltpu.SMEM), VM, ANY, ANY, ANY, ANY, ANY, ANY],
        out_specs=[ANY] * 6 + [VM],
        scratch_shapes=[pltpu.VMEM(dims, kind) for dims, kind in SCRATCH.values()]
        + [
            pltpu.SemaphoreType.DMA((22,)),
            pltpu.SemaphoreType.DMA((140,)),
            pltpu.SemaphoreType.DMA((140,)),
        ],
        compiler_params=pltpu.CompilerParams(
            collective_id=0, has_side_effects=True, vmem_limit_bytes=64 * 1024 * 1024 - 65536
        ),
        name="step",
    )(
        inputs.reshape(4, CH, 768),
        lengths,
        gains[0],
        jnp.swapaxes(w_qkv[0], 1, 2).reshape(576, 768),
        w_out[0],
        w_up[0],
        w_down[0],
        cotangent.reshape(1024, 768),
        jnp.asarray(rope_table(seg * lax.axis_size("sp"))),
    )
    hid, ig, gq, go, gu, gd, gg = finish(found)
    return (
        hid.reshape(inputs.shape),
        ig.reshape(inputs.shape),
        gq[None],
        go[None],
        gu[None],
        jnp.swapaxes(gd, 0, 1)[None],
        gg[None],
    )


def pick(*args):
    inputs, w_out = args[0], args[4]
    plain = (1, 2, 512, 768)
    sizes = (lax.axis_size("tp"), lax.axis_size("dp"), lax.axis_size("sp"))
    if inputs.shape == plain and w_out.shape[1:] == (192, 768) and sizes == (4, 4, 2):
        return fast(*args)
    return shards(*args)


def solution(mesh):
    in_specs = (
        P("dp", None, "sp", None),
        P("dp"),
        P(),
        P(None, None, None, "tp"),
        P(None, "tp", None),
        P(None, None, "tp"),
        P(None, "tp", None),
        P("dp", None, "sp", None),
    )
    out_specs = (
        P("dp", None, "sp", None),
        P("dp", None, "sp", None),
        P(None, None, ("dp", "sp"), "tp"),
        P(None, "tp", ("dp", "sp")),
        P(None, ("dp", "sp"), "tp"),
        P(None, "tp", ("dp", "sp")),
        P(None, None, ("dp", "sp")),
    )
    return jax.shard_map(pick, mesh=mesh, in_specs=in_specs, out_specs=out_specs, check_vma=False)
```
